32 devices in a mesh: dp: 2 (over y), expert: 16 (over z, x, core).
Axes of the slice: x: 2, y: 2, z: 4, core: 2. Of those that a mesh axis runs over, the one named last changes fastest.
Arguments:
- tokens: bfloat16 [2, 2, 1024, 2048], P(None, 'dp', 'expert'), may hold values from -6 to 6
- grad_out: bfloat16 [2, 2, 1024, 2048], P(None, 'dp', 'expert'), may hold values from -6 to 6
- segments: int32 [2, 2, 1024], P(None, 'dp'), may hold values from 0 to 3, never falling along the last dimension, each value on 1 to 512 neighbouring positions
- routes: int32 [2, 2, 1024, 6], P(None, 'dp', 'expert'), may hold values from 0 to 15, all different within a row; in each aligned block of 64 rows (0 to 63, 64 to 127, ..., all dimensions but the last counted through in order) at most 32 rows name the same one
- gates: float32 [2, 2, 1024, 6], P(None, 'dp', 'expert'), may hold values from 0.05 to 0.45
- attn_gain: bfloat16 [2048], P('dp'), may hold values from 0.5 to 1.5
- w_query: bfloat16 [2048, 3072], P('dp'), may hold values from -0.125 to 0.125
- w_kv_down: bfloat16 [2048, 576], P('dp'), may hold values from -0.125 to 0.125
- kv_gain: bfloat16 [512], P('dp'), may hold values from 0.5 to 1.5
- w_kv_up: bfloat16 [512, 4096], P('dp'), may hold values from -0.25 to 0.25
- w_out: bfloat16 [2048, 2048], P('dp'), may hold values from -0.375 to 0.375
- ffn_gain: bfloat16 [2048], P('dp'), may hold values from 0.5 to 1.5
- w_shared_in: bfloat16 [2048, 5632], P('dp'), may hold values from -0.125 to 0.125
- w_shared_out: bfloat16 [2816, 2048], P('dp'), may hold values from -0.109375 to 0.109375
- w_expert_in: bfloat16 [16, 2048, 2816], P('expert', 'dp'), may hold values from -0.125 to 0.125
- w_expert_out: bfloat16 [16, 1408, 2048], P('expert', 'dp'), may hold values from -0.15625 to 0.15625
Outputs:
- mixed: bfloat16 [2, 2, 1024, 2048], P(None, 'dp', 'expert')
- input_grad: float32 [2, 2, 1024, 2048], P(None, 'dp', 'expert')
- attn_gain_grad: float32 [2048], P('dp')
- w_query_grad: float32 [2048, 3072], P('dp')
- w_kv_down_grad: float32 [2048, 576], P('dp')
- kv_gain_grad: float32 [512], P('dp')
- w_kv_up_grad: float32 [512, 4096], P('dp')
- w_out_grad: float32 [2048, 2048], P('dp')
- ffn_gain_grad: float32 [2048], P('dp')
- w_shared_in_grad: float32 [2048, 5632], P('dp')
- w_shared_out_grad: float32 [2816, 2048], P('dp')
- w_expert_in_grad: float32 [16, 2048, 2816], P('expert', 'dp')
- w_expert_out_grad: float32 [16, 1408, 2048], P('expert', 'dp')
The draws below stay inside these ranges and needn't reach their ends.
Inputs may be any that keep to these rules, and one draw needn't show every extreme that they name: `routes`: within the tokens of one device in one micro-batch (aligned blocks of 64 rows in the order micro-batch, sequence, position) no expert is named more than 32 times, a bound that some block reaches. A token names 6 different experts. `segments`: document numbers never fall along a sequence; a document may cross the positions of several devices.
All inputs are finite; a program needn't handle non-finite values.
Results may differ from the reference program's by a relative error of at most 0.018.
Values may be sent and summed in bfloat16 or wider, within the bound.
No kernel may reach another device: no remote copies, remote signals or barrier semaphores. Data moves between devices by JAX's collectives and lax.ppermute only.
A program may use at most 576 MiB of HBM per device.

```python
import math
import jax
import jax.numpy as jnp
import numpy as np
from jax import lax

D = 2048
HEADS = 16
NOPE = 128
ROPE = 64
VDIM = 128
LATENT = 512
FFE = 1408
SHARED_FF = 2816
TOP = 6
MICRO = 2
SEQ = 1024
TOK_MB = 64
SEQS = 2
EXPERTS = 16
CAP = 32


def level_of(rng, shape, shards, smallest, high):
    def one(axis_at, parts):
        draws = jax.random.uniform(jax.random.fold_in(jax.random.fold_in(rng, 6), axis_at), (parts,), jnp.float32, smallest / len(shards), high / len(shards))
        return jnp.repeat(jnp.exp(draws), shape[axis_at] // parts).reshape((-1,) + (1,) * (len(shape) - axis_at - 1))

    factor_of = one(*shards[0])
    for cut in shards[1:]:
        factor_of = factor_of * one(*cut)
    return factor_of


def split_up(number_of, total, most, skew):
    portions = [(1 << 20) // math.isqrt(grade ** skew) + 1 for grade in range(2, number_of + 1)]
    surplus, holding = total - most - (number_of - 1), [1] * (number_of - 1)
    while surplus > 0:
        candidates = [i for i in range(number_of - 1) if holding[i] < most]
        mass, left = sum([portions[i] for i in candidates]), surplus
        for i in candidates:
            addition = min(most - holding[i], max(1, left * portions[i] // mass), surplus)
            holding[i] = holding[i] + addition
            surplus = surplus - addition
    return np.array([most] + holding)


def ragged(rng, amount, total, reach, lean):
    if amount == 2:
        one = jax.random.randint(rng, (), max(1, total - reach), min(reach, total - 1) + 1)
        return jnp.stack([one, total - one])
    sizes = jnp.asarray(split_up(amount, total, reach, lean), jnp.int32)
    couples = (amount - 1) // 2
    giver, receiver = sizes[1:1 + 2 * couples:2], sizes[2:2 + 2 * couples:2]
    slack = jnp.minimum(giver - 1, reach - receiver)
    shifted = jax.random.randint(jax.random.fold_in(rng, 1), (couples,), 0, 1 << 20) % (slack + 1)
    sizes = sizes.at[1:1 + 2 * couples:2].set(giver - shifted).at[2:2 + 2 * couples:2].set(receiver + shifted)
    return sizes[jax.random.permutation(jax.random.fold_in(rng, 2), amount)]


def shared_out(rng, own, number, rows, amount, top, most, lean):
    ranking = jax.random.permutation(rng, amount)
    heavy_load, ordinary = portions_of(amount, rows * top, most, lean, True), portions_of(amount, rows * top, most, lean, False)
    places = jnp.arange(amount)

    def named(sizes, rotation):
        used = int((sizes > 0).sum())
        fixed = max(1, used // 4)
        moved = fixed + (places - fixed + rotation * (used - fixed)) % max(1, amount - fixed)
        return jnp.zeros((amount,), jnp.int32).at[ranking[jnp.where(places < fixed, places, moved)]].set(jnp.asarray(sizes, jnp.int32))

    sizes = jnp.where(number % 4 == 0, named(heavy_load, number // 4), named(ordinary, number - number // 4 - 1))
    mixed = jax.random.permutation(jax.random.fold_in(own, 3), amount)
    donor, sink = mixed[0:amount // 2 * 2:2], mixed[1:amount // 2 * 2:2]
    room = jnp.minimum(sizes[donor] - 1, most - sizes[sink]) // 2
    room = jnp.where((donor == ranking[0]) | (sink == ranking[0]) | (sizes[sink] == 0), 0, jnp.maximum(room, 0))
    moved = jax.random.randint(jax.random.fold_in(own, 4), (amount // 2,), 0, 1 << 20) % (room + 1)
    sizes = sizes.at[donor].add(-moved).at[sink].add(moved)
    labels = jnp.searchsorted(jnp.cumsum(sizes), jnp.arange(rows * top), side="right").astype(jnp.int32)
    table = labels.reshape(top, rows).T
    table = table[jax.random.permutation(jax.random.fold_in(own, 1), rows)]
    rotation = jax.random.randint(jax.random.fold_in(own, 2), (rows, 1), 0, top)
    return jnp.take_along_axis(table, (jnp.arange(top)[None, :] + rotation) % top, axis=1)


def portions_of(amount, total, reach, slope, full):
    portions = [(1 << 20) // math.isqrt(rank ** slope) + 1 for rank in range(1, amount + 1)]
    largest = reach if full else min(reach, max(-(-total // amount), total * portions[0] // sum(portions)))
    least = 1 if total - largest >= amount - 1 else 0
    given, surplus = [largest] + [least] * (amount - 1), total - largest - least * (amount - 1)
    while surplus > 0:
        free = [i for i in range(1, amount) if given[i] < largest] or [i for i in range(1, amount) if given[i] < reach]
        mass, budget = sum([portions[i] for i in free]), surplus
        for i in free:
            extra = min(reach - given[i], max(1, budget * portions[i] // mass), surplus)
            given[i] = given[i] + extra
            surplus = surplus - extra
    return np.array(given)


def bell_draw(rng, extent, scale, bound, pieces=(), kind=jnp.bfloat16):
    entries = scale * jax.random.normal(rng, extent, jnp.float32)
    if pieces:
        entries = entries * level_of(rng, extent, pieces, -0.22, 0.18)
    return jnp.clip(entries, -bound, bound).astype(kind)


def setup_inputs(seed: int = 0) -> dict:
    seeds = jax.random.split(jax.random.key(seed), 17)
    tokens = bell_draw(seeds[0], (MICRO, SEQS, SEQ, D), 1.0, 6.0, ((1, 2), (2, 16)))
    grad_out = bell_draw(seeds[1], (MICRO, SEQS, SEQ, D), 1.0, 6.0, ((1, 2), (2, 16)))
    segments = jax.vmap(lambda own: jnp.searchsorted(jnp.cumsum(ragged(own, max(4, SEQ // 256), SEQ, SEQ // 2, 1)), jnp.arange(SEQ), side="right"))(jax.random.split(seeds[2], MICRO * SEQS)).reshape((MICRO, SEQS, SEQ)).astype(jnp.int32)
    routes_keys = jax.random.split(jax.random.fold_in(seeds[3], 1), MICRO * SEQS * SEQ // TOK_MB)
    routes_turns = jax.random.permutation(jax.random.fold_in(seeds[3], 3), MICRO * SEQS * SEQ // TOK_MB)
    routes = jax.vmap(lambda own, number: shared_out(jax.random.fold_in(seeds[3], 2), own, number, TOK_MB, EXPERTS, TOP, CAP, 2))(routes_keys, routes_turns).reshape((MICRO, SEQS, SEQ, TOP))
    gates = jnp.clip(0.05 + 0.39999999 * jax.random.uniform(seeds[4], (MICRO, SEQS, SEQ, TOP), jnp.float32) ** level_of(seeds[4], (MICRO, SEQS, SEQ, TOP), ((1, 2), (2, 16)), -0.2, 0.2), 0.05, 0.45)
    attn_gain = jnp.clip(1.0 + 0.1 * jax.random.normal(seeds[5], (D,), jnp.float32), 0.5, 1.5).astype(jnp.bfloat16)
    w_query = bell_draw(seeds[6], (D, HEADS * (NOPE + ROPE)), D ** -0.5, 0.125, ((0, 2),))
    w_kv_down = bell_draw(seeds[7], (D, LATENT + ROPE), D ** -0.5, 0.125, ((0, 2),))
    kv_gain = jnp.clip(1.0 + 0.1 * jax.random.normal(seeds[8], (LATENT,), jnp.float32), 0.5, 1.5).astype(jnp.bfloat16)
    w_kv_up = bell_draw(seeds[9], (LATENT, HEADS * (NOPE + VDIM)), LATENT ** -0.5, 0.25, ((0, 2),))
    w_out = bell_draw(seeds[10], (HEADS * VDIM, D), (HEADS * VDIM // 8) ** -0.5, 0.375, ((0, 2),))
    ffn_gain = jnp.clip(1.0 + 0.1 * jax.random.normal(seeds[11], (D,), jnp.float32), 0.5, 1.5).astype(jnp.bfloat16)
    w_shared_in = bell_draw(seeds[12], (D, 2 * SHARED_FF), D ** -0.5, 0.125, ((0, 2),))
    w_shared_out = bell_draw(seeds[13], (SHARED_FF, D), SHARED_FF ** -0.5, 0.109375, ((0, 2),))
    w_expert_in = bell_draw(seeds[14], (EXPERTS, D, 2 * FFE), D ** -0.5, 0.125, ((0, 16), (1, 2)))
    w_expert_out = bell_draw(seeds[15], (EXPERTS, FFE, D), FFE ** -0.5, 0.15625, ((0, 16), (1, 2)))
    return {"tokens": tokens, "grad_out": grad_out, "segments": segments, "routes": routes, "gates": gates, "attn_gain": attn_gain, "w_query": w_query, "w_kv_down": w_kv_down, "kv_gain": kv_gain, "w_kv_up": w_kv_up, "w_out": w_out, "ffn_gain": ffn_gain, "w_shared_in": w_shared_in, "w_shared_out": w_shared_out, "w_expert_in": w_expert_in, "w_expert_out": w_expert_out}


@jax.custom_vjp
def low(v):
    return lax.optimization_barrier(v.astype(jnp.bfloat16)).astype(jnp.float32)

@jax.custom_vjp
def low_back(v):
    return v

def low_keep(v):
    return (low(v), None)

def low_pass(kept, grad):
    return (grad,)

def back_keep(v):
    return (v, None)

def back_low(kept, grad):
    return (low(grad),)
low.defvjp(low_keep, low_pass)
low_back.defvjp(back_keep, back_low)
theta_base = 50000.0
eps_norm = 1e-06
highest = lax.Precision.HIGHEST

def rope_tables(length, width):
    half = width // 2
    freq = theta_base ** (-2.0 * jnp.arange(half, dtype=jnp.float32) / width)
    angle = jnp.arange(length, dtype=jnp.float32)[:, None] * freq[None, :]
    cosine = jnp.concatenate([jnp.cos(angle), jnp.cos(angle)], -1)
    sine = jnp.concatenate([jnp.sin(angle), jnp.sin(angle)], -1)
    return (cosine, sine)

def rotate(value, cosine, sine):
    half = value.shape[-1] // 2
    turned = jnp.concatenate([-value[..., half:], value[..., :half]], -1)
    return value * cosine + turned * sine

def normed(value, gain):
    return value * lax.rsqrt(lax.optimization_barrier(jnp.mean(value * value, -1, keepdims=True)) + eps_norm) * gain

def matmul(left, right):
    return jnp.dot(left, right, precision=highest)

def swiglu(packed):
    half = packed.shape[-1] // 2
    return jax.nn.silu(packed[..., :half]) * packed[..., half:]

def layer_seq(params, hidden_in, seg_ids, table, cosine, sine):
    attn_gain, w_query, w_kv_down, kv_gain, w_kv_up, w_out, ffn_gain, w_shared_in, w_shared_out, w_expert_in, w_expert_out = params
    length = hidden_in.shape[0]
    blocks = length // TOK_MB
    normed_in = low(normed(hidden_in, attn_gain))
    query_full = low_back(matmul(normed_in, w_query)).reshape(length, HEADS, NOPE + ROPE)
    query = low(jnp.concatenate([query_full[..., :NOPE], rotate(query_full[..., NOPE:], cosine[:, None, :], sine[:, None, :])], -1))
    kv_full = low_back(matmul(normed_in, w_kv_down))
    latent = low(normed(kv_full[:, :LATENT], kv_gain))
    key_rope = low(rotate(kv_full[:, LATENT:], cosine, sine))
    kv_up = low(matmul(latent, w_kv_up))
    scale = (NOPE + ROPE) ** (-0.5)
    places = jnp.arange(length, dtype=jnp.int32)
    rope_heads = jnp.broadcast_to(key_rope[:, None, :], (length, HEADS, ROPE))

    def block_attend(kv_copy, query_block, seg_block, place_block):
        kv_heads = low_back(kv_copy).reshape(length, HEADS, NOPE + VDIM)
        keys = jnp.concatenate([kv_heads[..., :NOPE], rope_heads], -1)
        values = kv_heads[..., NOPE:]
        raw = jnp.einsum('thd,shd->hts', query_block, keys, precision=highest)
        allowed = (seg_block[:, None] == seg_ids[None, :]) & (places[None, :] <= place_block[:, None])
        score = jnp.where(allowed[None], low_back(raw) * scale, -1e+30)
        probs = low(jax.nn.softmax(score, -1))
        return jnp.einsum('hts,shd->thd', probs, values, precision=highest).reshape(TOK_MB, HEADS * VDIM)
    kv_copies = jnp.broadcast_to(kv_up[None], (blocks,) + kv_up.shape)
    attended = jax.vmap(block_attend)(kv_copies, query.reshape(blocks, TOK_MB, HEADS, NOPE + ROPE), seg_ids.reshape(blocks, TOK_MB), places.reshape(blocks, TOK_MB))
    attended = low(low_back(attended.reshape(length, HEADS * VDIM)))
    first_sum = hidden_in + low_back(matmul(attended, w_out))
    ffn_in = low(normed(first_sum, ffn_gain))
    shared_pre = low_back(matmul(ffn_in, w_shared_in))
    shared_act = low(swiglu(shared_pre))
    shared = low_back(matmul(shared_act, w_shared_out))

    def expert_step(total, inputs):
        weight_in, weight_down, column = inputs
        expert_in = low_back(ffn_in)
        expert_pre = low_back(matmul(expert_in, weight_in))
        expert_act = low(swiglu(expert_pre))
        expert_out = low(low_back(matmul(expert_act, weight_down)))
        return (total + column[:, None] * expert_out, None)
    routed, _ = lax.scan(expert_step, jnp.zeros_like(hidden_in), (w_expert_in, w_expert_out, table.T))
    return first_sum + shared + routed

def reference(tokens, grad_out, segments, routes, gates, attn_gain, w_query, w_kv_down, kv_gain, w_kv_up, w_out, ffn_gain, w_shared_in, w_shared_out, w_expert_in, w_expert_out):
    params = tuple((item.astype(jnp.float32) for item in (attn_gain, w_query, w_kv_down, kv_gain, w_kv_up, w_out, ffn_gain, w_shared_in, w_shared_out, w_expert_in, w_expert_out)))
    count = MICRO * SEQS
    inputs = tokens.astype(jnp.float32).reshape(count, SEQ, D)
    cotangent = grad_out.astype(jnp.float32).reshape(count, SEQ, D)
    seg_all = segments.reshape(count, SEQ)
    chosen = (routes[..., None] == jnp.arange(EXPERTS, dtype=jnp.int32)).astype(gates.dtype)
    table = lax.optimization_barrier(jnp.sum(chosen * gates[..., None], axis=-2)).reshape(count, SEQ, EXPERTS)
    cosine, sine = rope_tables(SEQ, ROPE)
    layer_saved = jax.checkpoint(layer_seq)

    def forward(weights, hidden):

        def one(item):
            return layer_saved(weights, item[0], item[1], item[2], cosine, sine)
        return lax.map(one, (hidden, seg_all, table))
    result, pull = jax.vjp(forward, params, inputs)
    grads, dinputs = pull(cotangent)
    return (result.astype(jnp.bfloat16).reshape(tokens.shape), dinputs.reshape(tokens.shape), grads[0], grads[1], grads[2], grads[3], grads[4], grads[5], grads[6], grads[7], grads[8], grads[9], grads[10])
```

```python
import functools

import jax
import jax.numpy as jnp
from jax import lax
from jax.experimental import pallas as pl
from jax.experimental.layout import Layout, with_layout_constraint
from jax.experimental.pallas import tpu as pltpu
from jax.sharding import PartitionSpec as P

HEADS = 16
NOPE = 128
ROPE = 64
VDIM = 128
LATENT = 512
DOC_MAX = 512

theta_base = 50000.0
eps_norm = 1e-06
bf16 = jnp.bfloat16
f32 = jnp.float32


def rope_tables(length, width):
    half = width // 2
    freq = theta_base ** (-2.0 * jnp.arange(half, dtype=f32) / width)
    angle = jnp.arange(length, dtype=f32)[:, None] * freq[None, :]
    cosine = jnp.concatenate([jnp.cos(angle), jnp.cos(angle)], -1)
    sine = jnp.concatenate([jnp.sin(angle), jnp.sin(angle)], -1)
    return (cosine, sine)


def rotate_back(value, cosine, sine):
    half = value.shape[-1] // 2
    scaled = value * sine
    turned = jnp.concatenate([scaled[..., half:], -scaled[..., :half]], -1)
    return value * cosine + turned


def normed(value, gain):
    return (
        value
        * lax.rsqrt(jnp.mean(value * value, -1, keepdims=True) + eps_norm)
        * gain.astype(f32)
    )


def normed_back(value, gain, grad):
    inv = lax.rsqrt(jnp.mean(value * value, -1, keepdims=True) + eps_norm)
    hat = value * inv
    scaled = grad * gain.astype(f32)
    inner = jnp.mean(scaled * hat, -1, keepdims=True)
    return inv * (scaled - hat * inner), jnp.sum(grad * hat, 0)


def swiglu_parts(packed):
    half = packed.shape[-1] // 2
    return packed[..., :half], packed[..., half:]


def swiglu(packed):
    gate, up = swiglu_parts(packed)
    return gate * jax.nn.sigmoid(gate) * up


def swiglu_back(packed, grad):
    gate, up = swiglu_parts(packed)
    sig = jax.nn.sigmoid(gate)
    d_gate = grad * up * sig * (1.0 + gate * (1.0 - sig))
    d_up = grad * gate * sig
    return jnp.concatenate([d_gate, d_up], -1)


def dot(left, right):
    return jnp.dot(left, right, preferred_element_type=f32)


def dot_tn(left, right):
    return lax.dot_general(left, right, (((0,), (0,)), ((), ())), preferred_element_type=f32)


def dot_nt(left, right):
    return lax.dot_general(left, right, (((1,), (1,)), ((), ())), preferred_element_type=f32)


def row_major(x):
    return with_layout_constraint(x, Layout(major_to_minor=tuple(range(x.ndim))))


def after(value, *first):
    return lax.optimization_barrier((value,) + first)[0]


def block_of_keys(refs, start, stop, low):
    qn_ref, rope_ref, kv_ref, seg_col, seg_row = refs
    rows = qn_ref.shape[2]

    def take(ref, first, last):
        return ref[first // rows : last // rows, 0].reshape(last - first, ref.shape[3])

    query = jnp.concatenate([take(qn_ref, start, stop), take(rope_ref, start, stop)[:, :ROPE]], 1)
    kv = take(kv_ref, low, stop)
    key = jnp.concatenate([kv[:, :NOPE], take(rope_ref, low, stop)[:, ROPE:]], 1)
    value = kv[:, NOPE:]
    score = dot_nt(query, key) * ((NOPE + ROPE) ** (-0.5))
    size = (stop - start, stop - low)
    q_at = lax.broadcasted_iota(jnp.int32, size, 0) + (start - low)
    k_at = lax.broadcasted_iota(jnp.int32, size, 1)
    allowed = (seg_col[0, start:stop] == seg_row[0, :, low:stop]) & (k_at <= q_at)
    return query, key, value, jnp.where(allowed, score, -1e30)


def query_blocks(seq, rows, size=256):
    for start in range(0, seq, size):
        low = max(0, start - DOC_MAX + 1) // rows * rows
        yield start, start + size, low


def attend_kernel(qn_ref, rope_ref, kv_ref, seg_col, seg_row, out_ref, lse_ref):
    owners, _, rows, _ = qn_ref.shape
    refs = (qn_ref, rope_ref, kv_ref, seg_col, seg_row)
    for start, stop, low in query_blocks(owners * rows, rows):
        _, _, value, score = block_of_keys(refs, start, stop, low)
        top = jnp.max(score, -1, keepdims=True)
        expo = jnp.exp(score - top)
        total = jnp.sum(expo, -1, keepdims=True)
        out = dot((expo / total).astype(bf16), value).astype(bf16)
        at = slice(start // rows, stop // rows)
        out_ref[at, 0] = out.reshape((stop - start) // rows, rows, VDIM)
        lse_ref[0, start:stop] = top + jnp.log(total)


def attend_back_kernel(
    qn_ref, rope_ref, kv_ref, seg_col, seg_row, lse_ref, dout_ref, cos_ref, sin_ref, back_ref, acc
):
    owners, _, rows, _ = qn_ref.shape
    seq = owners * rows
    refs = (qn_ref, rope_ref, kv_ref, seg_col, seg_row)
    acc[...] = jnp.zeros_like(acc)
    for start, stop, low in query_blocks(seq, rows):
        at = slice(start // rows, stop // rows)
        query, key, value, score = block_of_keys(refs, start, stop, low)
        prob = jnp.exp(score - lse_ref[0, start:stop])
        dout = dout_ref[at, 0].reshape(stop - start, VDIM)
        dprob = dot_nt(dout, value)
        delta = jnp.sum(prob * dprob, -1, keepdims=True)
        dscore = (prob * (dprob - delta) * ((NOPE + ROPE) ** (-0.5))).astype(bf16)
        dquery = dot(dscore, key)
        acc[low:stop, : NOPE + ROPE] += dot_tn(dscore, query)
        acc[low:stop, 256:] += dot_tn(prob.astype(bf16), dout)
        rope = rotate_back(dquery[:, NOPE:], cos_ref[start:stop], sin_ref[start:stop])
        whole = jnp.concatenate([dquery[:, :NOPE], rope, rope, dquery, rope], 1)
        back_ref[at, 0] = whole.astype(bf16).reshape((stop - start) // rows, rows, 512)
    dkey = acc[...]
    tail = jnp.concatenate([dkey[:, NOPE : NOPE + ROPE], dkey[:, :NOPE], dkey[:, 256:]], 1)
    back_ref[:, 0, :, NOPE + ROPE :] = tail.astype(bf16).reshape(owners, rows, 320)


def attend(q_nope, roped, kvup, segs):
    owners, micro, rows, _ = q_nope.shape
    seq = owners * rows
    spec = lambda c: pl.BlockSpec((owners, 1, rows, c), lambda m: (0, m, 0, 0))
    return pl.pallas_call(
        attend_kernel,
        out_shape=(
            jax.ShapeDtypeStruct((owners, micro, rows, VDIM), bf16),
            jax.ShapeDtypeStruct((micro, seq, 1), f32),
        ),
        grid=(micro,),
        in_specs=[
            spec(NOPE),
            spec(2 * ROPE),
            spec(2 * NOPE),
            pl.BlockSpec((1, seq, 1), lambda m: (m, 0, 0)),
            pl.BlockSpec((1, 1, seq), lambda m: (m, 0, 0)),
        ],
        out_specs=(spec(VDIM), pl.BlockSpec((1, seq, 1), lambda m: (m, 0, 0))),
        cost_estimate=pl.CostEstimate(
            flops=2 * micro * seq * 640 * 320,
            transcendentals=micro * seq * 640,
            bytes_accessed=micro * seq * 1400,
        ),
    )(q_nope, roped, kvup, segs[:, :, None], segs[:, None, :])


def attend_back(q_nope, roped, kvup, segs, lse, dout, cosine, sine):
    owners, micro, rows, _ = q_nope.shape
    seq = owners * rows
    spec = lambda c: pl.BlockSpec((owners, 1, rows, c), lambda m: (0, m, 0, 0))
    flat = pl.BlockSpec((seq, ROPE), lambda m: (0, 0))
    return pl.pallas_call(
        attend_back_kernel,
        out_shape=jax.ShapeDtypeStruct((owners, micro, rows, 512), bf16),
        grid=(micro,),
        in_specs=[
            spec(NOPE),
            spec(2 * ROPE),
            spec(2 * NOPE),
            pl.BlockSpec((1, seq, 1), lambda m: (m, 0, 0)),
            pl.BlockSpec((1, 1, seq), lambda m: (m, 0, 0)),
            pl.BlockSpec((1, seq, 1), lambda m: (m, 0, 0)),
            spec(VDIM),
            flat,
            flat,
        ],
        out_specs=spec(512),
        scratch_shapes=[pltpu.VMEM((seq, 384), f32)],
        cost_estimate=pl.CostEstimate(
            flops=2 * micro * seq * 640 * 832,
            transcendentals=micro * seq * 640,
            bytes_accessed=micro * seq * 2600,
        ),
    )(q_nope, roped, kvup, segs[:, :, None], segs[:, None, :], lse, dout, cosine, sine)


def put_back_kernel(place_ref, rows_ref, units_ref, weight_ref, out_ref, *, product):
    blocks, size, capacity = place_ref.shape
    shared = product(units_ref[...], weight_ref[...])
    for b in range(blocks):
        placed = dot(place_ref[b], rows_ref[b * capacity : (b + 1) * capacity])
        at = slice(b * size, (b + 1) * size)
        out_ref[at] = (placed + shared[at]).astype(bf16)


def put_back(place, rows, units, weight, product):
    blocks, size, capacity = place.shape
    total, count = units.shape
    width = rows.shape[1]
    many = 4
    return pl.pallas_call(
        functools.partial(put_back_kernel, product=product),
        out_shape=jax.ShapeDtypeStruct((total, width), bf16),
        grid=(blocks // many,),
        in_specs=[
            pl.BlockSpec((many, size, capacity), lambda i: (i, 0, 0)),
            pl.BlockSpec((many * capacity, width), lambda i: (i, 0)),
            pl.BlockSpec((many * size, count), lambda i: (i, 0)),
            pl.BlockSpec(weight.shape, lambda i: (0, 0)),
        ],
        out_specs=pl.BlockSpec((many * size, width), lambda i: (i, 0)),
        cost_estimate=pl.CostEstimate(
            flops=2 * total * width * (capacity + count),
            transcendentals=0,
            bytes_accessed=2 * (total * width + rows.size + units.size + weight.size),
        ),
    )(place, rows, units, weight)


def columns_kernel(x_ref, out_ref, *, runs, piece):
    groups = x_ref.shape[0]
    length = groups * piece
    parts = []
    for c in range(runs):
        parts += [x_ref[e, :, c * piece : (c + 1) * piece].astype(f32) for e in range(groups)]
        if length % 128 == 0:
            out_ref[:, c * length : (c + 1) * length] = jnp.concatenate(parts, 1)
            parts = []
    if parts:
        out_ref[...] = jnp.concatenate(parts, 1)


def run_columns(stacked, runs):
    groups, rows, count = stacked.shape
    size = min(128, rows)
    return pl.pallas_call(
        functools.partial(columns_kernel, runs=runs, piece=count // runs),
        out_shape=jax.ShapeDtypeStruct((rows, groups * count), f32),
        grid=(rows // size,),
        in_specs=[pl.BlockSpec((groups, size, count), lambda i: (0, i, 0))],
        out_specs=pl.BlockSpec((size, groups * count), lambda i: (i, 0)),
        cost_estimate=pl.CostEstimate(
            flops=0, transcendentals=0, bytes_accessed=6 * stacked.size
        ),
    )(stacked)


def attn_columns_kernel(x_ref, out_ref, query_ref, *, a, b):
    for e in range(0, x_ref.shape[0], 2):
        one, two = x_ref[e].astype(f32), x_ref[e + 1].astype(f32)
        out_ref[:, e * a : (e + 2) * a] = jnp.concatenate([one[:, :a], two[:, :a]], 1)
        query_ref[:, e * b : (e + 2) * b] = jnp.concatenate(
            [one[:, a : a + b], two[:, a : a + b]], 1
        )


def attn_columns(stacked, a, b):
    groups, rows, count = stacked.shape
    size = min(128, rows)
    return pl.pallas_call(
        functools.partial(attn_columns_kernel, a=a, b=b),
        out_shape=(
            jax.ShapeDtypeStruct((rows, groups * a), f32),
            jax.ShapeDtypeStruct((rows, groups * b), f32),
        ),
        grid=(rows // size,),
        in_specs=[pl.BlockSpec((groups, size, count), lambda i: (0, i, 0))],
        out_specs=(
            pl.BlockSpec((size, groups * a), lambda i: (i, 0)),
            pl.BlockSpec((size, groups * b), lambda i: (i, 0)),
        ),
        cost_estimate=pl.CostEstimate(
            flops=0, transcendentals=0, bytes_accessed=6 * stacked.size
        ),
    )(stacked)


def per_device(
    tokens,
    grad_out,
    segments,
    routes,
    gates,
    attn_gain,
    w_query,
    w_kv_down,
    kv_gain,
    w_kv_up,
    w_out,
    ffn_gain,
    w_shared_in,
    w_shared_out,
    w_expert_in,
    w_expert_out,
):
    micro, _, rows, width = tokens.shape
    groups = lax.axis_size("expert")
    parts = lax.axis_size("dp")
    me = lax.axis_index("expert")
    part = lax.axis_index("dp")
    own = micro * rows
    total = groups * own
    seq = rows * groups
    top = routes.shape[3]
    capacity = max(2, rows * top * 4 // (3 * groups))
    qk = NOPE + ROPE
    assert HEADS == groups

    def shift(x, step):
        return lax.ppermute(x, "dp", [((i + step) % parts, i) for i in range(parts)])

    def send(x, step):
        return lax.ppermute(x, "dp", [(i, (i + step) % parts) for i in range(parts)])

    def others(x):
        return [shift(x, r) for r in range(1, parts)]

    def turn(x, axis, amount):
        size = x.shape[axis]
        return lax.dynamic_slice_in_dim(
            jnp.concatenate([x, x], axis), amount * (size // parts), size, axis
        )

    def own_first(x, axis):
        return turn(x, axis, part)

    def natural(x, axis):
        return turn(x, axis, (parts - part) % parts)

    def lay_out(x, rest):
        size = x.shape[0]
        whole = jnp.zeros((parts * size,) + x.shape[1:], x.dtype)
        for r, piece in enumerate([x] + rest):
            at = ((part + r) % parts) * size
            whole = lax.dynamic_update_slice_in_dim(whole, piece, at, 0)
        return whole

    def block_of(full, index):
        size = full.shape[0] // parts
        return lax.dynamic_slice_in_dim(full, (index % parts) * size, size, 0)

    def exchanged(own_block, block_for):
        result = own_block.astype(f32)
        for r in range(1, parts):
            result = result + send(block_for(r), r).astype(f32)
        return result

    pairs = [(i, i ^ 1) for i in range(groups)]
    odd = me % 2

    def pieces(x, *first):
        size = x.shape[0]
        found = [(x, part * size)]
        if parts == 2:
            half = size // 2
            asked = lax.dynamic_slice_in_dim(x, odd * half, half, 0)
            if first:
                asked = after(asked, *first)
            got = shift(asked, 1)
            swapped = lax.ppermute(got, "expert", pairs)
            base = (1 - part) * size
            found += [(got, base + odd * half), (swapped, base + (1 - odd) * half)]
        else:
            asked = after(x, *first) if first else x
            found += [(y, ((part + r) % parts) * size) for r, y in enumerate(others(asked), 1)]
        return found

    def dot_pieces(x, blocks):
        return sum(
            dot(lax.dynamic_slice_in_dim(x, at, w.shape[0], 1), w) for w, at in blocks
        )

    def dot_pieces_t(x, blocks):
        whole = jnp.zeros((x.shape[0], sum(w.shape[0] for w, _ in blocks)), f32)
        for w, at in blocks:
            whole = lax.dynamic_update_slice_in_dim(whole, dot_nt(x, w), at, 1)
        return whole

    def spread(x):
        return lax.all_gather(x, "expert", axis=0, tiled=True)

    def stack(x):
        return lax.all_gather(x, "expert", axis=0, tiled=False)

    def swap(x):
        return lax.all_to_all(x, "expert", split_axis=0, concat_axis=0, tiled=True)

    def collect(x):
        return lax.psum_scatter(x, "expert", scatter_dimension=0, tiled=True)

    gain_sizes = (width // parts, LATENT // parts, width // parts)
    cuts = (gain_sizes[0], gain_sizes[0] + gain_sizes[1])
    own_gains = jnp.concatenate([attn_gain, kv_gain, ffn_gain])
    gain_rows = jnp.split(lay_out(own_gains[None], [y[None] for y in others(own_gains)]), cuts, 1)
    gain_attn, gain_kv, gain_ffn = (rows_of.reshape(-1) for rows_of in gain_rows)

    first_own = jnp.concatenate(
        [lax.dynamic_slice_in_dim(w_query, me * qk, qk, 1), w_kv_down], 1
    )
    first_all = jnp.concatenate([first_own] + others(first_own), 0)
    wkvup_own = lax.dynamic_slice_in_dim(w_kv_up, me * 2 * NOPE, 2 * NOPE, 1)
    wkvup_me = lay_out(wkvup_own, others(wkvup_own))
    wout = pieces(w_out)

    def turned(w):
        return jnp.concatenate([-w[:, ROPE // 2 :], w[:, : ROPE // 2]], 1)

    w_down = first_all[:, qk:]
    rope_q, rope_k = first_all[:, NOPE:qk], first_all[:, qk + LATENT :]
    w_first = jnp.concatenate(
        [
            first_all[:, :NOPE],
            first_all[:, qk : qk + LATENT],
            rope_q,
            rope_k,
            turned(rope_q),
            turned(rope_k),
        ],
        1,
    )

    x_own = tokens[:, 0].reshape(own, width)
    dy_own = grad_out[:, 0].reshape(own, width)
    act_own = normed(x_own.astype(f32), gain_attn).astype(bf16)
    act = spread(own_first(act_own, 1))
    dy_all = spread(after(dy_own, act))

    expert_ids = jnp.arange(groups, dtype=jnp.int32)
    routes_own = routes[:, 0].reshape(own, top)
    gates_own = gates[:, 0].reshape(own, top)
    table = jnp.sum(
        jnp.where(routes_own[None] == expert_ids[:, None, None], gates_own[None], 0.0), -1
    )
    gate_rows = swap(table).reshape(groups * micro, rows)
    hit = gate_rows > 0.0
    slot = jnp.cumsum(hit.astype(jnp.int32), 1) - 1
    pick = (slot[:, None, :] == jnp.arange(capacity, dtype=jnp.int32)[None, :, None]) & hit[
        :, None, :
    ]
    gate_slots = jnp.sum(jnp.where(pick, gate_rows[:, None, :], 0.0), -1).reshape(-1, 1)
    pick = pick.astype(bf16)
    place = pick.swapaxes(1, 2)

    def dispatch(x):
        picked = jnp.einsum(
            "bst,btd->bsd",
            pick,
            x.reshape(groups * micro, rows, width),
            preferred_element_type=f32,
        )
        return picked.reshape(groups * micro * capacity, width)

    ff = w_shared_in.shape[1] // 2
    run = ff // (parts * groups)
    wout_in = wout[1][0]
    wsi_own = jnp.concatenate(
        [
            lax.dynamic_slice_in_dim(w_shared_in, c * (ff // parts) + me * run, run, 1)
            for c in range(2 * parts)
        ],
        1,
    )
    wso_own = lax.dynamic_slice_in_dim(w_shared_out, me * run, run, 0)
    wsi_me = jnp.concatenate([wsi_own] + others(after(wsi_own, wout_in)), 0)
    wso_me = lay_out(wso_own, others(after(wso_own, wout_in)))
    wei_others = others(after(w_expert_in[0], wout_in))
    weo_others = others(after(w_expert_out[0], wout_in))
    wq = pieces(w_query, wei_others[0], weo_others[0])
    wkvup = pieces(w_kv_up, wei_others[0], weo_others[0])

    cosine, sine = rope_tables(seq, ROPE)

    def table_of(values):
        both = jnp.concatenate([values, values], 1).reshape(groups, 1, rows, 2 * ROPE)
        return jnp.broadcast_to(both, (groups, micro, rows, 2 * ROPE)).reshape(total, 2 * ROPE)

    first = dot(after(act, gate_rows), w_first)
    q_nope = first[:, :NOPE].astype(bf16)
    latent_raw = first[:, NOPE : NOPE + LATENT]
    latent = normed(latent_raw, gain_kv).astype(bf16)
    at = NOPE + LATENT
    roped = (
        first[:, at : at + 2 * ROPE] * table_of(cosine) + first[:, at + 2 * ROPE :] * table_of(sine)
    ).astype(bf16)
    kvup = dot(latent, wkvup_me).astype(bf16)

    def owners(x):
        return x.reshape(groups, micro, rows, x.shape[-1])

    segs = segments[:, 0]
    head = (owners(q_nope), owners(roped), owners(kvup), segs)
    attn, lse = attend(*head)
    attn_own = swap(attn.reshape(groups, own, VDIM))
    attn_own = attn_own.swapaxes(0, 1).reshape(own, groups * VDIM)
    x1 = x_own.astype(f32) + dot_pieces(attn_own, wout)
    hid_own = normed(x1, gain_ffn).astype(bf16)
    hid_all = spread(own_first(hid_own, 1))
    attn_all = spread(after(attn_own, hid_all))

    spre = dot(hid_all, wsi_me)
    sact = swiglu(spre).astype(bf16)
    dsact = dot_nt(dy_all, wso_me)
    dspre = swiglu_back(spre, dsact).astype(bf16)
    g_si = dot_tn(hid_all, dspre)
    size = width // parts
    g_si = exchanged(g_si[:size], lambda r: g_si[r * size : (r + 1) * size].astype(bf16))
    g_so = dot_tn(sact, dy_all)
    g_so = exchanged(block_of(g_so, part), lambda r: block_of(g_so, part + r).astype(bf16))
    g_si = stack(row_major(g_si.astype(bf16)))
    g_so = stack(row_major(g_so.astype(bf16)))

    arrived = dispatch(hid_all).astype(bf16)
    dyexp = (gate_slots * dispatch(dy_all)).astype(bf16)
    wei = jnp.concatenate([w_expert_in[0]] + wei_others, 0)
    weo = lay_out(w_expert_out[0], weo_others)
    epre = dot(arrived, wei)
    eact = swiglu(epre).astype(bf16)
    deact = dot_nt(dyexp, weo)
    depre = swiglu_back(epre, deact).astype(bf16)
    dhid_rows = dot_nt(depre, wei).astype(bf16)
    dhid_part = put_back(place, dhid_rows, dspre, wsi_me, dot_nt)
    dhid_sum = collect(after(dhid_part, g_si, g_so))

    arrived, depre, eact, dyexp = lax.optimization_barrier(
        (arrived, depre, eact, dyexp, dhid_part)
    )[:4]
    gated = (gate_slots * dot(eact, weo)).astype(bf16)
    out_part = put_back(place, gated, sact, wso_me, dot)

    def expert_in_grad(r):
        return dot_tn(arrived[:, r * size : (r + 1) * size], depre)

    def expert_out_grad(r):
        short = eact.shape[1] // parts
        some = lax.dynamic_slice_in_dim(eact, ((part + r) % parts) * short, short, 1)
        return dot_tn(some, dyexp)

    sent_in = [expert_in_grad(r).astype(bf16) for r in range(1, parts)]
    sent_out = [expert_out_grad(r).astype(bf16) for r in range(1, parts)]
    dhid_sum = after(dhid_sum, out_part, *sent_in, *sent_out)
    got_in = [send(x, r).astype(f32) for r, x in enumerate(sent_in, 1)]
    got_out = [send(x, r).astype(f32) for r, x in enumerate(sent_out, 1)]
    out_sum = collect(after(out_part, dhid_sum))
    dhid = natural(dhid_sum, 1).astype(f32)

    dy = dy_own.astype(f32)
    dx1_norm, g_ffn_gain = normed_back(x1, gain_ffn, dhid)
    dx1 = dy + dx1_norm
    dx1_low = dx1.astype(bf16)
    dattn_own = dot_pieces_t(dx1_low, wout).astype(bf16)
    dattn = swap(dattn_own.reshape(own, groups, VDIM).swapaxes(0, 1))
    dao = after(dx1_low, dattn).reshape(own, groups, width // groups).swapaxes(0, 1)
    dao = swap(dao)
    dattn = dattn.reshape(groups, micro, rows, VDIM)
    back = attend_back(*head, lse, dattn, cosine, sine)
    moved = swap(back.reshape(groups, own, 512))

    def back_of(x, first_column, last_column):
        piece = x[..., first_column:last_column]
        return piece.swapaxes(0, 1).reshape(own, groups * (last_column - first_column))

    flat = back.reshape(total, 512)
    g_query = dot_tn(act, flat[:, :qk])
    g_kvup = dot_tn(latent, flat[:, 256:])
    g_out = dot_tn(attn_all, dao.reshape(total, width // groups))

    def fold(x):
        many = size // x.shape[0]
        return jnp.concatenate(jnp.split(x, many, 1), 0)

    def unfold(x, height):
        return jnp.concatenate(jnp.split(x, x.shape[1] // height, 1), 2)

    def attn_grads(r):
        return jnp.concatenate(
            [
                block_of(g_out, part + r),
                g_query[r * size : (r + 1) * size],
                fold(block_of(g_kvup, part + r)),
            ],
            1,
        )

    g_attn = exchanged(attn_grads(0), lambda r: attn_grads(r).astype(bf16))
    g_attn = stack(row_major(g_attn.astype(bf16)))

    dq_own = back_of(moved, 0, qk)
    dkvup_own = back_of(moved, 256, 512)
    dkrope_own = jnp.sum(moved[..., qk:256].astype(f32), 0)
    dlatent = dot_pieces_t(dkvup_own, wkvup)
    latent_own = lax.dynamic_slice_in_dim(latent_raw, me * own, own, 0)
    cos_own = jnp.tile(lax.dynamic_slice_in_dim(cosine, me * rows, rows, 0), (micro, 1))
    sin_own = jnp.tile(lax.dynamic_slice_in_dim(sine, me * rows, rows, 0), (micro, 1))
    dlatent_raw, g_kv_gain = normed_back(latent_own, gain_kv, dlatent)
    dkvfull = jnp.concatenate([dlatent_raw, rotate_back(dkrope_own, cos_own, sin_own)], -1)
    dkvfull = dkvfull.astype(bf16)
    dkv_all = spread(dkvfull)
    dact = dot_pieces_t(dq_own, wq) + natural(dot_nt(dkvfull, w_down), 1)
    dx_norm, g_attn_gain = normed_back(x_own.astype(f32), gain_attn, dact)
    input_grad = dx1 + dx_norm

    step = width // (parts * groups)
    act_rows = jnp.concatenate(
        [
            lax.dynamic_slice_in_dim(act, c * size + me * step, step, 1)
            for c in range(parts)
        ],
        1,
    )
    g_down = dot_tn(act_rows, dkv_all)

    def last_grads(r):
        gains = [block_of(g, part + r) for g in (g_attn_gain, g_kv_gain, g_ffn_gain)]
        gains = jnp.concatenate(gains).reshape(-1, LATENT + ROPE)
        return jnp.concatenate([g_down[r * step : (r + 1) * step], gains], 0)

    last = exchanged(last_grads(0), lambda r: last_grads(r).astype(bf16))
    last = stack(last.astype(bf16))
    g_down = last[:, :step].astype(f32).reshape(size, LATENT + ROPE)
    gains = jnp.sum(last[:, step:].astype(f32), 0).reshape(-1)
    gains = jnp.split(gains, cuts)

    mixed = (x1 + out_sum.astype(f32)).astype(bf16)
    g_ein = sum(got_in, expert_in_grad(0))
    g_eout = sum(got_out, expert_out_grad(0))
    out_grad, query_grad = attn_columns(g_attn, width // groups, qk)
    kvup_grad = unfold(g_attn[..., width // groups + qk :], LATENT // parts)
    kvup_grad = kvup_grad.swapaxes(0, 1).reshape(LATENT // parts, -1).astype(f32)
    return (
        mixed.reshape(micro, 1, rows, width),
        input_grad.reshape(micro, 1, rows, width),
        gains[0],
        query_grad,
        g_down,
        gains[1],
        kvup_grad,
        out_grad,
        gains[2],
        run_columns(g_si, 2 * parts),
        g_so.astype(f32).reshape(ff // parts, width),
        g_ein[None],
        g_eout[None],
    )


def solution(mesh):
    tok = P(None, "dp", "expert", None)
    row = P("dp", None)
    exp = P("expert", "dp", None)
    in_specs = (
        tok, tok, P(None, "dp", None), tok, tok,
        P("dp"), row, row, P("dp"), row, row, P("dp"), row, row, exp, exp,
    )
    out_specs = (
        tok, tok, P("dp"), row, row, P("dp"), row, row, P("dp"), row, row, exp, exp,
    )

    return jax.shard_map(
        per_device, mesh=mesh, in_specs=in_specs, out_specs=out_specs, check_vma=False
    )
```

```python
import functools

import jax
import jax.numpy as jnp
from jax import lax
from jax.experimental import pallas as pl
from jax.experimental.layout import Layout, with_layout_constraint
from jax.experimental.pallas import tpu as pltpu
from jax.sharding import PartitionSpec as P

HEADS = 16
NOPE = 128
ROPE = 64
VDIM = 128
LATENT = 512
DOC_MAX = 512

theta_base = 50000.0
eps_norm = 1e-06
bf16 = jnp.bfloat16
f32 = jnp.float32


def rope_tables(length, width):
    half = width // 2
    freq = theta_base ** (-2.0 * jnp.arange(half, dtype=f32) / width)
    angle = jnp.arange(length, dtype=f32)[:, None] * freq[None, :]
    cosine = jnp.concatenate([jnp.cos(angle), jnp.cos(angle)], -1)
    sine = jnp.concatenate([jnp.sin(angle), jnp.sin(angle)], -1)
    return (cosine, sine)


def rotate_back(value, cosine, sine):
    half = value.shape[-1] // 2
    scaled = value * sine
    turned = jnp.concatenate([scaled[..., half:], -scaled[..., :half]], -1)
    return value * cosine + turned


def normed(value, gain):
    return (
        value
        * lax.rsqrt(jnp.mean(value * value, -1, keepdims=True) + eps_norm)
        * gain.astype(f32)
    )


def normed_back(value, gain, grad):
    inv = lax.rsqrt(jnp.mean(value * value, -1, keepdims=True) + eps_norm)
    hat = value * inv
    scaled = grad * gain.astype(f32)
    inner = jnp.mean(scaled * hat, -1, keepdims=True)
    return inv * (scaled - hat * inner), jnp.sum(grad * hat, 0)


def swiglu_parts(packed):
    half = packed.shape[-1] // 2
    return packed[..., :half], packed[..., half:]


def swiglu(packed):
    gate, up = swiglu_parts(packed)
    return gate * jax.nn.sigmoid(gate) * up


def swiglu_back(packed, grad):
    gate, up = swiglu_parts(packed)
    sig = jax.nn.sigmoid(gate)
    d_gate = grad * up * sig * (1.0 + gate * (1.0 - sig))
    d_up = grad * gate * sig
    return jnp.concatenate([d_gate, d_up], -1)


def dot(left, right):
    return jnp.dot(left, right, preferred_element_type=f32)


def dot_tn(left, right):
    return lax.dot_general(left, right, (((0,), (0,)), ((), ())), preferred_element_type=f32)


def dot_nt(left, right):
    return lax.dot_general(left, right, (((1,), (1,)), ((), ())), preferred_element_type=f32)


def row_major(x):
    return with_layout_constraint(x, Layout(major_to_minor=tuple(range(x.ndim))))


def after(value, *first):
    return lax.optimization_barrier((value,) + first)[0]


def block_of_keys(refs, start, stop, low):
    qn_ref, rope_ref, kv_ref, seg_col, seg_row = refs
    rows = qn_ref.shape[2]

    def take(ref, first, last):
        return ref[first // rows : last // rows, 0].reshape(last - first, ref.shape[3])

    query = jnp.concatenate([take(qn_ref, start, stop), take(rope_ref, start, stop)[:, :ROPE]], 1)
    kv = take(kv_ref, low, stop)
    key = jnp.concatenate([kv[:, :NOPE], take(rope_ref, low, stop)[:, ROPE:]], 1)
    value = kv[:, NOPE:]
    score = dot_nt(query, key) * ((NOPE + ROPE) ** (-0.5))
    size = (stop - start, stop - low)
    q_at = lax.broadcasted_iota(jnp.int32, size, 0) + (start - low)
    k_at = lax.broadcasted_iota(jnp.int32, size, 1)
    allowed = (seg_col[0, start:stop] == seg_row[0, :, low:stop]) & (k_at <= q_at)
    return query, key, value, jnp.where(allowed, score, -1e30)


def query_blocks(seq, rows, size=256):
    for start in range(0, seq, size):
        low = max(0, start - DOC_MAX + 1) // rows * rows
        yield start, start + size, low


def attend_kernel(qn_ref, rope_ref, kv_ref, seg_col, seg_row, out_ref, lse_ref):
    owners, _, rows, _ = qn_ref.shape
    refs = (qn_ref, rope_ref, kv_ref, seg_col, seg_row)
    for start, stop, low in query_blocks(owners * rows, rows):
        _, _, value, score = block_of_keys(refs, start, stop, low)
        top = jnp.max(score, -1, keepdims=True)
        expo = jnp.exp(score - top)
        total = jnp.sum(expo, -1, keepdims=True)
        out = dot((expo / total).astype(bf16), value).astype(bf16)
        at = slice(start // rows, stop // rows)
        out_ref[at, 0] = out.reshape((stop - start) // rows, rows, VDIM)
        lse_ref[0, start:stop] = top + jnp.log(total)


def attend_back_kernel(
    qn_ref, rope_ref, kv_ref, seg_col, seg_row, lse_ref, dout_ref, cos_ref, sin_ref, back_ref, acc
):
    owners, _, rows, _ = qn_ref.shape
    seq = owners * rows
    refs = (qn_ref, rope_ref, kv_ref, seg_col, seg_row)
    acc[...] = jnp.zeros_like(acc)
    for start, stop, low in query_blocks(seq, rows):
        at = slice(start // rows, stop // rows)
        query, key, value, score = block_of_keys(refs, start, stop, low)
        prob = jnp.exp(score - lse_ref[0, start:stop])
        dout = dout_ref[at, 0].reshape(stop - start, VDIM)
        dprob = dot_nt(dout, value)
        delta = jnp.sum(prob * dprob, -1, keepdims=True)
        dscore = (prob * (dprob - delta) * ((NOPE + ROPE) ** (-0.5))).astype(bf16)
        dquery = dot(dscore, key)
        acc[low:stop, : NOPE + ROPE] += dot_tn(dscore, query)
        acc[low:stop, 256:] += dot_tn(prob.astype(bf16), dout)
        rope = rotate_back(dquery[:, NOPE:], cos_ref[start:stop], sin_ref[start:stop])
        whole = jnp.concatenate([dquery[:, :NOPE], rope, rope, dquery, rope], 1)
        back_ref[at, 0] = whole.astype(bf16).reshape((stop - start) // rows, rows, 512)
    dkey = acc[...]
    tail = jnp.concatenate([dkey[:, NOPE : NOPE + ROPE], dkey[:, :NOPE], dkey[:, 256:]], 1)
    back_ref[:, 0, :, NOPE + ROPE :] = tail.astype(bf16).reshape(owners, rows, 320)


def attend(q_nope, roped, kvup, segs):
    owners, micro, rows, _ = q_nope.shape
    seq = owners * rows
    spec = lambda c: pl.BlockSpec((owners, 1, rows, c), lambda m: (0, m, 0, 0))
    return pl.pallas_call(
        attend_kernel,
        out_shape=(
            jax.ShapeDtypeStruct((owners, micro, rows, VDIM), bf16),
            jax.ShapeDtypeStruct((micro, seq, 1), f32),
        ),
        grid=(micro,),
        in_specs=[
            spec(NOPE),
            spec(2 * ROPE),
            spec(2 * NOPE),
            pl.BlockSpec((1, seq, 1), lambda m: (m, 0, 0)),
            pl.BlockSpec((1, 1, seq), lambda m: (m, 0, 0)),
        ],
        out_specs=(spec(VDIM), pl.BlockSpec((1, seq, 1), lambda m: (m, 0, 0))),
        cost_estimate=pl.CostEstimate(
            flops=2 * micro * seq * 640 * 320,
            transcendentals=micro * seq * 640,
            bytes_accessed=micro * seq * 1400,
        ),
    )(q_nope, roped, kvup, segs[:, :, None], segs[:, None, :])


def attend_back(q_nope, roped, kvup, segs, lse, dout, cosine, sine):
    owners, micro, rows, _ = q_nope.shape
    seq = owners * rows
    spec = lambda c: pl.BlockSpec((owners, 1, rows, c), lambda m: (0, m, 0, 0))
    flat = pl.BlockSpec((seq, ROPE), lambda m: (0, 0))
    return pl.pallas_call(
        attend_back_kernel,
        out_shape=jax.ShapeDtypeStruct((owners, micro, rows, 512), bf16),
        grid=(micro,),
        in_specs=[
            spec(NOPE),
            spec(2 * ROPE),
            spec(2 * NOPE),
            pl.BlockSpec((1, seq, 1), lambda m: (m, 0, 0)),
            pl.BlockSpec((1, 1, seq), lambda m: (m, 0, 0)),
            pl.BlockSpec((1, seq, 1), lambda m: (m, 0, 0)),
            spec(VDIM),
            flat,
            flat,
        ],
        out_specs=spec(512),
        scratch_shapes=[pltpu.VMEM((seq, 384), f32)],
        cost_estimate=pl.CostEstimate(
            flops=2 * micro * seq * 640 * 832,
            transcendentals=micro * seq * 640,
            bytes_accessed=micro * seq * 2600,
        ),
    )(q_nope, roped, kvup, segs[:, :, None], segs[:, None, :], lse, dout, cosine, sine)


def put_back_kernel(place_ref, rows_ref, units_ref, weight_ref, out_ref, *, product):
    blocks, size, capacity = place_ref.shape
    shared = product(units_ref[...], weight_ref[...])
    for b in range(blocks):
        placed = dot(place_ref[b], rows_ref[b * capacity : (b + 1) * capacity])
        at = slice(b * size, (b + 1) * size)
        out_ref[at] = (placed + shared[at]).astype(bf16)


def put_back(place, rows, units, weight, product):
    blocks, size, capacity = place.shape
    total, count = units.shape
    width = rows.shape[1]
    many = 4
    return pl.pallas_call(
        functools.partial(put_back_kernel, product=product),
        out_shape=jax.ShapeDtypeStruct((total, width), bf16),
        grid=(blocks // many,),
        in_specs=[
            pl.BlockSpec((many, size, capacity), lambda i: (i, 0, 0)),
            pl.BlockSpec((many * capacity, width), lambda i: (i, 0)),
            pl.BlockSpec((many * size, count), lambda i: (i, 0)),
            pl.BlockSpec(weight.shape, lambda i: (0, 0)),
        ],
        out_specs=pl.BlockSpec((many * size, width), lambda i: (i, 0)),
        cost_estimate=pl.CostEstimate(
            flops=2 * total * width * (capacity + count),
            transcendentals=0,
            bytes_accessed=2 * (total * width + rows.size + units.size + weight.size),
        ),
    )(place, rows, units, weight)


def shared_in_kernel(x_ref, out_ref, *, runs, piece):
    groups = x_ref.shape[0]
    turned = [x_ref[e].astype(f32).T for e in range(groups)]
    length = groups * piece
    parts = []
    for c in range(runs):
        parts += [t[:, c * piece : (c + 1) * piece] for t in turned]
        if length % 128 == 0:
            out_ref[:, c * length : (c + 1) * length] = jnp.concatenate(parts, 1)
            parts = []
    if parts:
        out_ref[...] = jnp.concatenate(parts, 1)


def shared_out_kernel(x_ref, out_ref, *, piece):
    rows = x_ref[0].astype(f32)
    count = rows.shape[0] // piece
    out_ref[0] = jnp.concatenate([rows[c * piece : (c + 1) * piece] for c in range(count)], 1)


def shared_rows(stacked, runs, piece):
    groups, count, size = stacked.shape
    first = runs * piece
    rest = count - first
    step = 128
    in_grad = pl.pallas_call(
        functools.partial(shared_in_kernel, runs=runs, piece=piece),
        out_shape=jax.ShapeDtypeStruct((size, groups * first), f32),
        grid=(size // step,),
        in_specs=[pl.BlockSpec((groups, first, step), lambda i: (0, 0, i))],
        out_specs=pl.BlockSpec((step, groups * first), lambda i: (i, 0)),
        cost_estimate=pl.CostEstimate(
            flops=0, transcendentals=0, bytes_accessed=6 * groups * first * size
        ),
    )(stacked)
    out_grad = pl.pallas_call(
        functools.partial(shared_out_kernel, piece=piece),
        out_shape=jax.ShapeDtypeStruct((groups, piece, rest // piece * size), f32),
        grid=(groups,),
        in_specs=[pl.BlockSpec((1, rest, size), lambda e: (e, first // rest, 0))],
        out_specs=pl.BlockSpec((1, piece, rest // piece * size), lambda e: (e, 0, 0)),
        cost_estimate=pl.CostEstimate(
            flops=0, transcendentals=0, bytes_accessed=6 * groups * rest * size
        ),
    )(stacked)
    return in_grad, out_grad.reshape(groups * piece, -1)


def kvup_columns_kernel(x_ref, out_ref, *, skip, height):
    groups, rows, _ = x_ref.shape
    for e in range(groups):
        runs = [
            x_ref[e, c * height : (c + 1) * height, skip:].astype(f32)
            for c in range(rows // height)
        ]
        whole = jnp.concatenate(runs, 1)
        count = whole.shape[1]
        out_ref[:, e * count : (e + 1) * count] = whole


def kvup_columns(stacked, start, height):
    groups, rows, count = stacked.shape
    tile = start // 128
    width = (count - start) * (rows // height)
    return pl.pallas_call(
        functools.partial(kvup_columns_kernel, skip=start - 128 * tile, height=height),
        out_shape=jax.ShapeDtypeStruct((height, groups * width), f32),
        grid=(1,),
        in_specs=[pl.BlockSpec((groups, rows, count - 128 * tile), lambda i: (0, 0, tile))],
        out_specs=pl.BlockSpec((height, groups * width), lambda i: (0, 0)),
        cost_estimate=pl.CostEstimate(
            flops=0, transcendentals=0, bytes_accessed=8 * groups * height * width
        ),
    )(stacked)


def attn_columns_kernel(x_ref, out_ref, query_ref, *, a, b):
    for e in range(0, x_ref.shape[0], 2):
        one, two = x_ref[e].astype(f32), x_ref[e + 1].astype(f32)
        out_ref[:, e * a : (e + 2) * a] = jnp.concatenate([one[:, :a], two[:, :a]], 1)
        query_ref[:, e * b : (e + 2) * b] = jnp.concatenate(
            [one[:, a : a + b], two[:, a : a + b]], 1
        )


def attn_columns(stacked, a, b):
    groups, rows, count = stacked.shape
    size = min(128, rows)
    return pl.pallas_call(
        functools.partial(attn_columns_kernel, a=a, b=b),
        out_shape=(
            jax.ShapeDtypeStruct((rows, groups * a), f32),
            jax.ShapeDtypeStruct((rows, groups * b), f32),
        ),
        grid=(rows // size,),
        in_specs=[pl.BlockSpec((groups, size, count), lambda i: (0, i, 0))],
        out_specs=(
            pl.BlockSpec((size, groups * a), lambda i: (i, 0)),
            pl.BlockSpec((size, groups * b), lambda i: (i, 0)),
        ),
        cost_estimate=pl.CostEstimate(
            flops=0, transcendentals=0, bytes_accessed=6 * stacked.size
        ),
    )(stacked)


def per_device(
    tokens,
    grad_out,
    segments,
    routes,
    gates,
    attn_gain,
    w_query,
    w_kv_down,
    kv_gain,
    w_kv_up,
    w_out,
    ffn_gain,
    w_shared_in,
    w_shared_out,
    w_expert_in,
    w_expert_out,
):
    micro, _, rows, width = tokens.shape
    groups = lax.axis_size("expert")
    parts = lax.axis_size("dp")
    me = lax.axis_index("expert")
    part = lax.axis_index("dp")
    own = micro * rows
    total = groups * own
    seq = rows * groups
    top = routes.shape[3]
    capacity = max(2, rows * top * 4 // (3 * groups))
    qk = NOPE + ROPE
    assert HEADS == groups

    def shift(x, step):
        return lax.ppermute(x, "dp", [((i + step) % parts, i) for i in range(parts)])

    def send(x, step):
        return lax.ppermute(x, "dp", [(i, (i + step) % parts) for i in range(parts)])

    def others(x):
        return [shift(x, r) for r in range(1, parts)]

    def turn(x, axis, amount):
        size = x.shape[axis]
        return lax.dynamic_slice_in_dim(
            jnp.concatenate([x, x], axis), amount * (size // parts), size, axis
        )

    def own_first(x, axis):
        return turn(x, axis, part)

    def natural(x, axis):
        return turn(x, axis, (parts - part) % parts)

    def lay_out(x, rest):
        size = x.shape[0]
        whole = jnp.zeros((parts * size,) + x.shape[1:], x.dtype)
        for r, piece in enumerate([x] + rest):
            at = ((part + r) % parts) * size
            whole = lax.dynamic_update_slice_in_dim(whole, piece, at, 0)
        return whole

    def block_of(full, index):
        size = full.shape[0] // parts
        return lax.dynamic_slice_in_dim(full, (index % parts) * size, size, 0)

    def exchanged(own_block, block_for):
        result = own_block.astype(f32)
        for r in range(1, parts):
            result = result + send(block_for(r), r).astype(f32)
        return result

    pairs = [(i, i ^ 1) for i in range(groups)]
    odd = me % 2

    def pieces(x, *first):
        size = x.shape[0]
        found = [(x, part * size)]
        if parts == 2:
            half = size // 2
            asked = lax.dynamic_slice_in_dim(x, odd * half, half, 0)
            if first:
                asked = after(asked, *first)
            got = shift(asked, 1)
            swapped = lax.ppermute(got, "expert", pairs)
            base = (1 - part) * size
            found += [(got, base + odd * half), (swapped, base + (1 - odd) * half)]
        else:
            asked = after(x, *first) if first else x
            found += [(y, ((part + r) % parts) * size) for r, y in enumerate(others(asked), 1)]
        return found

    def dot_pieces(x, blocks):
        return sum(
            dot(lax.dynamic_slice_in_dim(x, at, w.shape[0], 1), w) for w, at in blocks
        )

    def dot_pieces_t(x, blocks):
        whole = jnp.zeros((x.shape[0], sum(w.shape[0] for w, _ in blocks)), f32)
        for w, at in blocks:
            whole = lax.dynamic_update_slice_in_dim(whole, dot_nt(x, w), at, 1)
        return whole

    def spread(x):
        return lax.all_gather(x, "expert", axis=0, tiled=True)

    def stack(x):
        return lax.all_gather(x, "expert", axis=0, tiled=False)

    def swap(x):
        return lax.all_to_all(x, "expert", split_axis=0, concat_axis=0, tiled=True)

    def broadcast(x):
        return swap(jnp.broadcast_to(x[None], (groups,) + x.shape))

    def collect(x):
        return lax.psum_scatter(x, "expert", scatter_dimension=0, tiled=True)

    gain_sizes = (width // parts, LATENT // parts, width // parts)
    cuts = (gain_sizes[0], gain_sizes[0] + gain_sizes[1])
    own_gains = jnp.concatenate([attn_gain, kv_gain, ffn_gain])
    gain_rows = jnp.split(lay_out(own_gains[None], [y[None] for y in others(own_gains)]), cuts, 1)
    gain_attn, gain_kv, gain_ffn = (rows_of.reshape(-1) for rows_of in gain_rows)

    first_own = jnp.concatenate(
        [lax.dynamic_slice_in_dim(w_query, me * qk, qk, 1), w_kv_down], 1
    )
    first_all = jnp.concatenate([first_own] + others(first_own), 0)
    wkvup_own = lax.dynamic_slice_in_dim(w_kv_up, me * 2 * NOPE, 2 * NOPE, 1)
    wkvup_me = lay_out(wkvup_own, others(wkvup_own))
    wout = pieces(w_out)

    def turned(w):
        return jnp.concatenate([-w[:, ROPE // 2 :], w[:, : ROPE // 2]], 1)

    w_down = first_all[:, qk:]
    rope_q, rope_k = first_all[:, NOPE:qk], first_all[:, qk + LATENT :]
    w_first = jnp.concatenate(
        [
            first_all[:, :NOPE],
            first_all[:, qk : qk + LATENT],
            rope_q,
            rope_k,
            turned(rope_q),
            turned(rope_k),
        ],
        1,
    )

    x_own = tokens[:, 0].reshape(own, width)
    dy_own = grad_out[:, 0].reshape(own, width)
    act_own = normed(x_own.astype(f32), gain_attn).astype(bf16)
    act = spread(own_first(act_own, 1))
    dy_all = spread(after(dy_own, act))

    expert_ids = jnp.arange(groups, dtype=jnp.int32)
    routes_own = routes[:, 0].reshape(own, top)
    gates_own = gates[:, 0].reshape(own, top)
    table = jnp.sum(
        jnp.where(routes_own[None] == expert_ids[:, None, None], gates_own[None], 0.0), -1
    )
    gate_rows = swap(table).reshape(groups * micro, rows)
    hit = gate_rows > 0.0
    slot = jnp.cumsum(hit.astype(jnp.int32), 1) - 1
    pick = (slot[:, None, :] == jnp.arange(capacity, dtype=jnp.int32)[None, :, None]) & hit[
        :, None, :
    ]
    gate_slots = jnp.sum(jnp.where(pick, gate_rows[:, None, :], 0.0), -1).reshape(-1, 1)
    pick = pick.astype(bf16)
    place = pick.swapaxes(1, 2)

    def dispatch(x):
        picked = jnp.einsum(
            "bst,btd->bsd",
            pick,
            x.reshape(groups * micro, rows, width),
            preferred_element_type=f32,
        )
        return picked.reshape(groups * micro * capacity, width)

    ff = w_shared_in.shape[1] // 2
    run = ff // (parts * groups)
    wsi_own = jnp.concatenate(
        [
            lax.dynamic_slice_in_dim(w_shared_in, c * (ff // parts) + me * run, run, 1)
            for c in range(2 * parts)
        ],
        1,
    )
    wso_own = lax.dynamic_slice_in_dim(w_shared_out, me * run, run, 0)
    wsi_me = jnp.concatenate([wsi_own] + others(wsi_own), 0)
    wso_me = lay_out(wso_own, others(wso_own))
    wei_others = others(w_expert_in[0])
    weo_others = others(w_expert_out[0])
    wq = pieces(w_query, wei_others[0], weo_others[0])
    wkvup = pieces(w_kv_up, wei_others[0], weo_others[0])

    cosine, sine = rope_tables(seq, ROPE)

    def table_of(values):
        both = jnp.concatenate([values, values], 1).reshape(groups, 1, rows, 2 * ROPE)
        return jnp.broadcast_to(both, (groups, micro, rows, 2 * ROPE)).reshape(total, 2 * ROPE)

    first = dot(after(act, gate_rows), w_first)
    q_nope = first[:, :NOPE].astype(bf16)
    latent_raw = first[:, NOPE : NOPE + LATENT]
    latent = normed(latent_raw, gain_kv).astype(bf16)
    at = NOPE + LATENT
    roped = (
        first[:, at : at + 2 * ROPE] * table_of(cosine) + first[:, at + 2 * ROPE :] * table_of(sine)
    ).astype(bf16)
    kvup = dot(latent, wkvup_me).astype(bf16)

    def owners(x):
        return x.reshape(groups, micro, rows, x.shape[-1])

    segs = segments[:, 0]
    head = (owners(q_nope), owners(roped), owners(kvup), segs)
    attn, lse = attend(*head)
    attn_own = swap(attn.reshape(groups, own, VDIM))
    attn_own = attn_own.swapaxes(0, 1).reshape(own, groups * VDIM)
    x1 = x_own.astype(f32) + dot_pieces(attn_own, wout)
    hid_own = normed(x1, gain_ffn).astype(bf16)
    hid_all = spread(own_first(hid_own, 1))
    attn_all = spread(after(attn_own, hid_all))

    spre = dot(hid_all, wsi_me)
    sact = swiglu(spre).astype(bf16)
    dsact = dot_nt(dy_all, wso_me)
    dspre = swiglu_back(spre, dsact).astype(bf16)
    size = width // parts
    g_si = dot_tn(dspre, hid_all)
    g_so = dot_tn(sact, dy_all)

    def shared_grads(r):
        rows_of = block_of(g_so, part + r)
        return jnp.concatenate(
            [g_si[:, r * size : (r + 1) * size]] + jnp.split(rows_of, parts, 1), 0
        )

    g_shared = exchanged(shared_grads(0), lambda r: shared_grads(r).astype(bf16)).astype(bf16)

    arrived = dispatch(hid_all).astype(bf16)
    dyexp = (gate_slots * dispatch(dy_all)).astype(bf16)
    wei = jnp.concatenate([w_expert_in[0]] + wei_others, 0)
    weo = lay_out(w_expert_out[0], weo_others)
    epre = dot(arrived, wei)
    eact = swiglu(epre).astype(bf16)
    deact = dot_nt(dyexp, weo)
    depre = swiglu_back(epre, deact).astype(bf16)
    dhid_rows = dot_nt(depre, wei).astype(bf16)
    dhid_part = put_back(place, dhid_rows, dspre, wsi_me, dot_nt)
    dhid_sum = collect(dhid_part)
    g_shared = stack(after(g_shared, dhid_sum))

    arrived, depre, eact, dyexp = lax.optimization_barrier(
        (arrived, depre, eact, dyexp, dhid_part)
    )[:4]
    gated = (gate_slots * dot(eact, weo)).astype(bf16)
    out_part = put_back(place, gated, sact, wso_me, dot)

    def expert_in_grad(r):
        return dot_tn(arrived[:, r * size : (r + 1) * size], depre)

    def expert_out_grad(r):
        short = eact.shape[1] // parts
        some = lax.dynamic_slice_in_dim(eact, ((part + r) % parts) * short, short, 1)
        return dot_tn(some, dyexp)

    sent_in = [expert_in_grad(r).astype(bf16) for r in range(1, parts)]
    sent_out = [expert_out_grad(r).astype(bf16) for r in range(1, parts)]
    dhid_sum = after(dhid_sum, out_part, *sent_in, *sent_out)
    got_in = [send(x, r).astype(f32) for r, x in enumerate(sent_in, 1)]
    got_out = [send(x, r).astype(f32) for r, x in enumerate(sent_out, 1)]
    dhid = natural(dhid_sum, 1).astype(f32)

    dy = dy_own.astype(f32)
    dx1_norm, g_ffn_gain = normed_back(x1, gain_ffn, dhid)
    dx1 = dy + dx1_norm
    dx1_low = dx1.astype(bf16)
    dattn_own = dot_pieces_t(dx1_low, wout).astype(bf16)
    dattn = swap(dattn_own.reshape(own, groups, VDIM).swapaxes(0, 1))
    dao = after(dx1_low, dattn).reshape(own, groups, width // groups).swapaxes(0, 1)
    dao = swap(dao)
    dattn = dattn.reshape(groups, micro, rows, VDIM)
    back = attend_back(*head, lse, dattn, cosine, sine)
    moved = swap(back.reshape(groups, own, 512))

    def back_of(x, first_column, last_column):
        piece = x[..., first_column:last_column]
        return piece.swapaxes(0, 1).reshape(own, groups * (last_column - first_column))

    flat = back.reshape(total, 512)
    g_query = dot_tn(act, flat[:, :qk])
    g_kvup = dot_tn(latent, flat[:, 256:])
    g_out = dot_tn(attn_all, dao.reshape(total, width // groups))

    def fold(x):
        many = size // x.shape[0]
        return jnp.concatenate(jnp.split(x, many, 1), 0)

    def attn_grads(r):
        return jnp.concatenate(
            [
                block_of(g_out, part + r),
                g_query[r * size : (r + 1) * size],
                fold(block_of(g_kvup, part + r)),
            ],
            1,
        )

    g_attn = exchanged(attn_grads(0), lambda r: attn_grads(r).astype(bf16))
    g_attn = g_attn.astype(bf16)
    out_sum = collect(after(out_part, g_attn))
    g_attn = stack(row_major(g_attn))

    dq_own = back_of(moved, 0, qk)
    dkvup_own = back_of(moved, 256, 512)
    dkrope_own = jnp.sum(moved[..., qk:256].astype(f32), 0)
    dlatent = dot_pieces_t(dkvup_own, wkvup)
    latent_own = lax.dynamic_slice_in_dim(latent_raw, me * own, own, 0)
    cos_own = jnp.tile(lax.dynamic_slice_in_dim(cosine, me * rows, rows, 0), (micro, 1))
    sin_own = jnp.tile(lax.dynamic_slice_in_dim(sine, me * rows, rows, 0), (micro, 1))
    dlatent_raw, g_kv_gain = normed_back(latent_own, gain_kv, dlatent)
    dkvfull = jnp.concatenate([dlatent_raw, rotate_back(dkrope_own, cos_own, sin_own)], -1)
    dkvfull = dkvfull.astype(bf16)
    dkv_all = broadcast(dkvfull).reshape(total, LATENT + ROPE)
    dact = dot_pieces_t(dq_own, wq) + natural(dot_nt(dkvfull, w_down), 1)
    dx_norm, g_attn_gain = normed_back(x_own.astype(f32), gain_attn, dact)
    input_grad = dx1 + dx_norm

    step = width // (parts * groups)
    act_rows = jnp.concatenate(
        [
            lax.dynamic_slice_in_dim(act, c * size + me * step, step, 1)
            for c in range(parts)
        ],
        1,
    )
    g_down = dot_tn(act_rows, dkv_all)

    def last_grads(r):
        gains = [block_of(g, part + r) for g in (g_attn_gain, g_kv_gain, g_ffn_gain)]
        gains = jnp.concatenate(gains).reshape(-1, LATENT + ROPE)
        return jnp.concatenate([g_down[r * step : (r + 1) * step], gains], 0)

    last = exchanged(last_grads(0), lambda r: last_grads(r).astype(bf16))
    last = broadcast(last.astype(bf16))
    g_down = last[:, :step].astype(f32).reshape(size, LATENT + ROPE)
    gains = jnp.sum(last[:, step:].astype(f32), 0).reshape(-1)
    gains = jnp.split(gains, cuts)

    mixed = (x1 + out_sum.astype(f32)).astype(bf16)
    g_ein = sum(got_in, expert_in_grad(0))
    g_eout = sum(got_out, expert_out_grad(0))
    out_grad, query_grad = attn_columns(g_attn, width // groups, qk)
    kvup_grad = kvup_columns(g_attn, width // groups + qk, LATENT // parts)
    shared_in_grad, shared_out_grad = shared_rows(g_shared, 2 * parts, run)
    return (
        mixed.reshape(micro, 1, rows, width),
        input_grad.reshape(micro, 1, rows, width),
        gains[0],
        query_grad,
        g_down,
        gains[1],
        kvup_grad,
        out_grad,
        gains[2],
        shared_in_grad,
        shared_out_grad,
        g_ein[None],
        g_eout[None],
    )


def solution(mesh):
    tok = P(None, "dp", "expert", None)
    row = P("dp", None)
    exp = P("expert", "dp", None)
    in_specs = (
        tok, tok, P(None, "dp", None), tok, tok,
        P("dp"), row, row, P("dp"), row, row, P("dp"), row, row, exp, exp,
    )
    out_specs = (
        tok, tok, P("dp"), row, row, P("dp"), row, row, P("dp"), row, row, exp, exp,
    )

    return jax.shard_map(
        per_device, mesh=mesh, in_specs=in_specs, out_specs=out_specs, check_vma=False
    )
```

```python
import functools

import jax
import jax.numpy as jnp
from jax import lax
from jax.experimental import pallas as pl
from jax.experimental.layout import Layout, with_layout_constraint
from jax.experimental.pallas import tpu as pltpu
from jax.sharding import PartitionSpec as P

HEADS = 16
NOPE = 128
ROPE = 64
VDIM = 128
LATENT = 512
DOC_MAX = 512

theta_base = 50000.0
eps_norm = 1e-06
bf16 = jnp.bfloat16
f32 = jnp.float32


def rope_tables(length, width):
    half = width // 2
    freq = theta_base ** (-2.0 * jnp.arange(half, dtype=f32) / width)
    angle = jnp.arange(length, dtype=f32)[:, None] * freq[None, :]
    cosine = jnp.concatenate([jnp.cos(angle), jnp.cos(angle)], -1)
    sine = jnp.concatenate([jnp.sin(angle), jnp.sin(angle)], -1)
    return (cosine, sine)


def rotate_back(value, cosine, sine):
    half = value.shape[-1] // 2
    scaled = value * sine
    turned = jnp.concatenate([scaled[..., half:], -scaled[..., :half]], -1)
    return value * cosine + turned


def normed(value, gain):
    return (
        value
        * lax.rsqrt(jnp.mean(value * value, -1, keepdims=True) + eps_norm)
        * gain.astype(f32)
    )


def normed_back(value, gain, grad):
    inv = lax.rsqrt(jnp.mean(value * value, -1, keepdims=True) + eps_norm)
    hat = value * inv
    scaled = grad * gain.astype(f32)
    inner = jnp.mean(scaled * hat, -1, keepdims=True)
    return inv * (scaled - hat * inner), jnp.sum(grad * hat, 0)


def swiglu_parts(packed):
    half = packed.shape[-1] // 2
    return packed[..., :half], packed[..., half:]


def swiglu(packed):
    gate, up = swiglu_parts(packed)
    return gate * jax.nn.sigmoid(gate) * up


def swiglu_back(packed, grad):
    gate, up = swiglu_parts(packed)
    sig = jax.nn.sigmoid(gate)
    d_gate = grad * up * sig * (1.0 + gate * (1.0 - sig))
    d_up = grad * gate * sig
    return jnp.concatenate([d_gate, d_up], -1)


def dot(left, right):
    return jnp.dot(left, right, preferred_element_type=f32)


def dot_tn(left, right):
    return lax.dot_general(left, right, (((0,), (0,)), ((), ())), preferred_element_type=f32)


def dot_nt(left, right):
    return lax.dot_general(left, right, (((1,), (1,)), ((), ())), preferred_element_type=f32)


def row_major(x):
    return with_layout_constraint(x, Layout(major_to_minor=tuple(range(x.ndim))))


def after(value, *first):
    return lax.optimization_barrier((value,) + first)[0]


def block_of_keys(refs, start, stop, low):
    qn_ref, rope_ref, kv_ref, seg_col, seg_row = refs
    rows = qn_ref.shape[2]

    def take(ref, first, last):
        return ref[first // rows : last // rows, 0].reshape(last - first, ref.shape[3])

    query = jnp.concatenate([take(qn_ref, start, stop), take(rope_ref, start, stop)[:, :ROPE]], 1)
    kv = take(kv_ref, low, stop)
    key = jnp.concatenate([kv[:, :NOPE], take(rope_ref, low, stop)[:, ROPE:]], 1)
    value = kv[:, NOPE:]
    score = dot_nt(query, key) * ((NOPE + ROPE) ** (-0.5))
    size = (stop - start, stop - low)
    q_at = lax.broadcasted_iota(jnp.int32, size, 0) + (start - low)
    k_at = lax.broadcasted_iota(jnp.int32, size, 1)
    allowed = (seg_col[0, start:stop] == seg_row[0, :, low:stop]) & (k_at <= q_at)
    return query, key, value, jnp.where(allowed, score, -1e30)


def query_blocks(seq, rows, size=256):
    for start in range(0, seq, size):
        low = max(0, start - DOC_MAX + 1) // rows * rows
        yield start, start + size, low


def attend_kernel(qn_ref, rope_ref, kv_ref, seg_col, seg_row, out_ref, lse_ref):
    owners, _, rows, _ = qn_ref.shape
    refs = (qn_ref, rope_ref, kv_ref, seg_col, seg_row)
    for start, stop, low in query_blocks(owners * rows, rows):
        _, _, value, score = block_of_keys(refs, start, stop, low)
        top = jnp.max(score, -1, keepdims=True)
        expo = jnp.exp(score - top)
        total = jnp.sum(expo, -1, keepdims=True)
        out = dot((expo / total).astype(bf16), value).astype(bf16)
        at = slice(start // rows, stop // rows)
        out_ref[at, 0] = out.reshape((stop - start) // rows, rows, VDIM)
        lse_ref[0, start:stop] = top + jnp.log(total)


def attend_back_kernel(
    qn_ref, rope_ref, kv_ref, seg_col, seg_row, lse_ref, dout_ref, cos_ref, sin_ref, back_ref, acc
):
    owners, _, rows, _ = qn_ref.shape
    seq = owners * rows
    refs = (qn_ref, rope_ref, kv_ref, seg_col, seg_row)
    acc[...] = jnp.zeros_like(acc)
    for start, stop, low in query_blocks(seq, rows):
        at = slice(start // rows, stop // rows)
        query, key, value, score = block_of_keys(refs, start, stop, low)
        prob = jnp.exp(score - lse_ref[0, start:stop])
        dout = dout_ref[at, 0].reshape(stop - start, VDIM)
        dprob = dot_nt(dout, value)
        delta = jnp.sum(prob * dprob, -1, keepdims=True)
        dscore = (prob * (dprob - delta) * ((NOPE + ROPE) ** (-0.5))).astype(bf16)
        dquery = dot(dscore, key)
        acc[low:stop, : NOPE + ROPE] += dot_tn(dscore, query)
        acc[low:stop, 256:] += dot_tn(prob.astype(bf16), dout)
        rope = rotate_back(dquery[:, NOPE:], cos_ref[start:stop], sin_ref[start:stop])
        whole = jnp.concatenate([dquery[:, :NOPE], rope, rope, dquery, rope], 1)
        back_ref[at, 0] = whole.astype(bf16).reshape((stop - start) // rows, rows, 512)
    dkey = acc[...]
    tail = jnp.concatenate([dkey[:, NOPE : NOPE + ROPE], dkey[:, :NOPE], dkey[:, 256:]], 1)
    back_ref[:, 0, :, NOPE + ROPE :] = tail.astype(bf16).reshape(owners, rows, 320)


def attend(q_nope, roped, kvup, segs):
    owners, micro, rows, _ = q_nope.shape
    seq = owners * rows
    spec = lambda c: pl.BlockSpec((owners, 1, rows, c), lambda m: (0, m, 0, 0))
    return pl.pallas_call(
        attend_kernel,
        out_shape=(
            jax.ShapeDtypeStruct((owners, micro, rows, VDIM), bf16),
            jax.ShapeDtypeStruct((micro, seq, 1), f32),
        ),
        grid=(micro,),
        in_specs=[
            spec(NOPE),
            spec(2 * ROPE),
            spec(2 * NOPE),
            pl.BlockSpec((1, seq, 1), lambda m: (m, 0, 0)),
            pl.BlockSpec((1, 1, seq), lambda m: (m, 0, 0)),
        ],
        out_specs=(spec(VDIM), pl.BlockSpec((1, seq, 1), lambda m: (m, 0, 0))),
        cost_estimate=pl.CostEstimate(
            flops=2 * micro * seq * 640 * 320,
            transcendentals=micro * seq * 640,
            bytes_accessed=micro * seq * 1400,
        ),
    )(q_nope, roped, kvup, segs[:, :, None], segs[:, None, :])


def attend_back(q_nope, roped, kvup, segs, lse, dout, cosine, sine):
    owners, micro, rows, _ = q_nope.shape
    seq = owners * rows
    spec = lambda c: pl.BlockSpec((owners, 1, rows, c), lambda m: (0, m, 0, 0))
    flat = pl.BlockSpec((seq, ROPE), lambda m: (0, 0))
    return pl.pallas_call(
        attend_back_kernel,
        out_shape=jax.ShapeDtypeStruct((owners, micro, rows, 512), bf16),
        grid=(micro,),
        in_specs=[
            spec(NOPE),
            spec(2 * ROPE),
            spec(2 * NOPE),
            pl.BlockSpec((1, seq, 1), lambda m: (m, 0, 0)),
            pl.BlockSpec((1, 1, seq), lambda m: (m, 0, 0)),
            pl.BlockSpec((1, seq, 1), lambda m: (m, 0, 0)),
            spec(VDIM),
            flat,
            flat,
        ],
        out_specs=spec(512),
        scratch_shapes=[pltpu.VMEM((seq, 384), f32)],
        cost_estimate=pl.CostEstimate(
            flops=2 * micro * seq * 640 * 832,
            transcendentals=micro * seq * 640,
            bytes_accessed=micro * seq * 2600,
        ),
    )(q_nope, roped, kvup, segs[:, :, None], segs[:, None, :], lse, dout, cosine, sine)


def put_back_kernel(place_ref, rows_ref, units_ref, weight_ref, out_ref, *, product):
    blocks, size, capacity = place_ref.shape
    shared = product(units_ref[...], weight_ref[...])
    for b in range(blocks):
        placed = dot(place_ref[b], rows_ref[b * capacity : (b + 1) * capacity])
        at = slice(b * size, (b + 1) * size)
        out_ref[at] = (placed + shared[at]).astype(bf16)


def put_back(place, rows, units, weight, product):
    blocks, size, capacity = place.shape
    total, count = units.shape
    width = rows.shape[1]
    many = 4
    return pl.pallas_call(
        functools.partial(put_back_kernel, product=product),
        out_shape=jax.ShapeDtypeStruct((total, width), bf16),
        grid=(blocks // many,),
        in_specs=[
            pl.BlockSpec((many, size, capacity), lambda i: (i, 0, 0)),
            pl.BlockSpec((many * capacity, width), lambda i: (i, 0)),
            pl.BlockSpec((many * size, count), lambda i: (i, 0)),
            pl.BlockSpec(weight.shape, lambda i: (0, 0)),
        ],
        out_specs=pl.BlockSpec((many * size, width), lambda i: (i, 0)),
        cost_estimate=pl.CostEstimate(
            flops=2 * total * width * (capacity + count),
            transcendentals=0,
            bytes_accessed=2 * (total * width + rows.size + units.size + weight.size),
        ),
    )(place, rows, units, weight)


def shared_in_kernel(x_ref, out_ref, *, runs, piece):
    groups = x_ref.shape[0]
    turned = [x_ref[e].astype(f32).T for e in range(groups)]
    length = groups * piece
    parts = []
    for c in range(runs):
        parts += [t[:, c * piece : (c + 1) * piece] for t in turned]
        if length % 128 == 0:
            out_ref[:, c * length : (c + 1) * length] = jnp.concatenate(parts, 1)
            parts = []
    if parts:
        out_ref[...] = jnp.concatenate(parts, 1)


def shared_out_kernel(x_ref, out_ref, *, piece):
    rows = x_ref[0].astype(f32)
    count = rows.shape[0] // piece
    out_ref[0] = jnp.concatenate([rows[c * piece : (c + 1) * piece] for c in range(count)], 1)


def shared_rows(stacked, runs, piece):
    groups, count, size = stacked.shape
    first = runs * piece
    rest = count - first
    step = 128
    in_grad = pl.pallas_call(
        functools.partial(shared_in_kernel, runs=runs, piece=piece),
        out_shape=jax.ShapeDtypeStruct((size, groups * first), f32),
        grid=(size // step,),
        in_specs=[pl.BlockSpec((groups, first, step), lambda i: (0, 0, i))],
        out_specs=pl.BlockSpec((step, groups * first), lambda i: (i, 0)),
        cost_estimate=pl.CostEstimate(
            flops=0, transcendentals=0, bytes_accessed=6 * groups * first * size
        ),
    )(stacked)
    out_grad = pl.pallas_call(
        functools.partial(shared_out_kernel, piece=piece),
        out_shape=jax.ShapeDtypeStruct((groups, piece, rest // piece * size), f32),
        grid=(groups,),
        in_specs=[pl.BlockSpec((1, rest, size), lambda e: (e, first // rest, 0))],
        out_specs=pl.BlockSpec((1, piece, rest // piece * size), lambda e: (e, 0, 0)),
        cost_estimate=pl.CostEstimate(
            flops=0, transcendentals=0, bytes_accessed=6 * groups * rest * size
        ),
    )(stacked)
    return in_grad, out_grad.reshape(groups * piece, -1)


def kvup_columns_kernel(x_ref, out_ref, *, skip, height):
    groups, rows, _ = x_ref.shape
    for e in range(groups):
        runs = [
            x_ref[e, c * height : (c + 1) * height, skip:].astype(f32)
            for c in range(rows // height)
        ]
        whole = jnp.concatenate(runs, 1)
        count = whole.shape[1]
        out_ref[:, e * count : (e + 1) * count] = whole


def kvup_columns(stacked, rows, start, height):
    groups, _, count = stacked.shape
    tile = start // 128
    width = (count - start) * (rows // height)
    return pl.pallas_call(
        functools.partial(kvup_columns_kernel, skip=start - 128 * tile, height=height),
        out_shape=jax.ShapeDtypeStruct((height, groups * width), f32),
        grid=(1,),
        in_specs=[pl.BlockSpec((groups, rows, count - 128 * tile), lambda i: (0, 0, tile))],
        out_specs=pl.BlockSpec((height, groups * width), lambda i: (0, 0)),
        cost_estimate=pl.CostEstimate(
            flops=0, transcendentals=0, bytes_accessed=8 * groups * height * width
        ),
    )(stacked)


def attn_columns_kernel(x_ref, out_ref, query_ref, *, a, b):
    for e in range(0, x_ref.shape[0], 2):
        one, two = x_ref[e].astype(f32), x_ref[e + 1].astype(f32)
        out_ref[:, e * a : (e + 2) * a] = jnp.concatenate([one[:, :a], two[:, :a]], 1)
        query_ref[:, e * b : (e + 2) * b] = jnp.concatenate(
            [one[:, a : a + b], two[:, a : a + b]], 1
        )


def attn_columns(stacked, rows, a, b):
    groups, _, count = stacked.shape
    size = min(128, rows)
    return pl.pallas_call(
        functools.partial(attn_columns_kernel, a=a, b=b),
        out_shape=(
            jax.ShapeDtypeStruct((rows, groups * a), f32),
            jax.ShapeDtypeStruct((rows, groups * b), f32),
        ),
        grid=(rows // size,),
        in_specs=[pl.BlockSpec((groups, size, count), lambda i: (0, i, 0))],
        out_specs=(
            pl.BlockSpec((size, groups * a), lambda i: (i, 0)),
            pl.BlockSpec((size, groups * b), lambda i: (i, 0)),
        ),
        cost_estimate=pl.CostEstimate(
            flops=0, transcendentals=0, bytes_accessed=6 * stacked.size
        ),
    )(stacked)


def per_device(
    tokens,
    grad_out,
    segments,
    routes,
    gates,
    attn_gain,
    w_query,
    w_kv_down,
    kv_gain,
    w_kv_up,
    w_out,
    ffn_gain,
    w_shared_in,
    w_shared_out,
    w_expert_in,
    w_expert_out,
):
    micro, _, rows, width = tokens.shape
    groups = lax.axis_size("expert")
    parts = lax.axis_size("dp")
    me = lax.axis_index("expert")
    part = lax.axis_index("dp")
    own = micro * rows
    total = groups * own
    seq = rows * groups
    top = routes.shape[3]
    capacity = max(2, rows * top * 4 // (3 * groups))
    qk = NOPE + ROPE
    assert HEADS == groups

    def shift(x, step):
        return lax.ppermute(x, "dp", [((i + step) % parts, i) for i in range(parts)])

    def send(x, step):
        return lax.ppermute(x, "dp", [(i, (i + step) % parts) for i in range(parts)])

    def others(x):
        return [shift(x, r) for r in range(1, parts)]

    def turn(x, axis, amount):
        size = x.shape[axis]
        return lax.dynamic_slice_in_dim(
            jnp.concatenate([x, x], axis), amount * (size // parts), size, axis
        )

    def own_first(x, axis):
        return turn(x, axis, part)

    def natural(x, axis):
        return turn(x, axis, (parts - part) % parts)

    def lay_out(x, rest):
        size = x.shape[0]
        whole = jnp.zeros((parts * size,) + x.shape[1:], x.dtype)
        for r, piece in enumerate([x] + rest):
            at = ((part + r) % parts) * size
            whole = lax.dynamic_update_slice_in_dim(whole, piece, at, 0)
        return whole

    def block_of(full, index):
        size = full.shape[0] // parts
        return lax.dynamic_slice_in_dim(full, (index % parts) * size, size, 0)

    def exchanged(own_block, block_for):
        result = own_block.astype(f32)
        for r in range(1, parts):
            result = result + send(block_for(r), r).astype(f32)
        return result

    pairs = [(i, i ^ 1) for i in range(groups)]
    odd = me % 2

    def pieces(x, *first):
        size = x.shape[0]
        found = [(x, part * size)]
        if parts == 2:
            half = size // 2
            asked = lax.dynamic_slice_in_dim(x, odd * half, half, 0)
            if first:
                asked = after(asked, *first)
            got = shift(asked, 1)
            swapped = lax.ppermute(got, "expert", pairs)
            base = (1 - part) * size
            found += [(got, base + odd * half), (swapped, base + (1 - odd) * half)]
        else:
            asked = after(x, *first) if first else x
            found += [(y, ((part + r) % parts) * size) for r, y in enumerate(others(asked), 1)]
        return found

    def dot_pieces(x, blocks):
        return sum(
            dot(lax.dynamic_slice_in_dim(x, at, w.shape[0], 1), w) for w, at in blocks
        )

    def dot_pieces_t(x, blocks):
        whole = jnp.zeros((x.shape[0], sum(w.shape[0] for w, _ in blocks)), f32)
        for w, at in blocks:
            whole = lax.dynamic_update_slice_in_dim(whole, dot_nt(x, w), at, 1)
        return whole

    def spread(x):
        return lax.all_gather(x, "expert", axis=0, tiled=True)

    def stack(x):
        return lax.all_gather(x, "expert", axis=0, tiled=False)

    def swap(x):
        return lax.all_to_all(x, "expert", split_axis=0, concat_axis=0, tiled=True)

    def collect(x):
        return lax.psum_scatter(x, "expert", scatter_dimension=0, tiled=True)

    gain_sizes = (width // parts, LATENT // parts, width // parts)
    cuts = (gain_sizes[0], gain_sizes[0] + gain_sizes[1])
    own_gains = jnp.concatenate([attn_gain, kv_gain, ffn_gain])
    gain_rows = jnp.split(lay_out(own_gains[None], [y[None] for y in others(own_gains)]), cuts, 1)
    gain_attn, gain_kv, gain_ffn = (rows_of.reshape(-1) for rows_of in gain_rows)

    first_own = jnp.concatenate(
        [lax.dynamic_slice_in_dim(w_query, me * qk, qk, 1), w_kv_down], 1
    )
    first_all = jnp.concatenate([first_own] + others(first_own), 0)
    wkvup_own = lax.dynamic_slice_in_dim(w_kv_up, me * 2 * NOPE, 2 * NOPE, 1)
    wkvup_me = lay_out(wkvup_own, others(wkvup_own))
    wout = pieces(w_out)

    def turned(w):
        return jnp.concatenate([-w[:, ROPE // 2 :], w[:, : ROPE // 2]], 1)

    w_down = first_all[:, qk:]
    rope_q, rope_k = first_all[:, NOPE:qk], first_all[:, qk + LATENT :]
    w_first = jnp.concatenate(
        [
            first_all[:, :NOPE],
            first_all[:, qk : qk + LATENT],
            rope_q,
            rope_k,
            turned(rope_q),
            turned(rope_k),
        ],
        1,
    )

    x_own = tokens[:, 0].reshape(own, width)
    dy_own = grad_out[:, 0].reshape(own, width)
    act_own = normed(x_own.astype(f32), gain_attn).astype(bf16)
    act = spread(own_first(act_own, 1))
    dy_all = spread(after(dy_own, act))

    expert_ids = jnp.arange(groups, dtype=jnp.int32)
    routes_own = routes[:, 0].reshape(own, top)
    gates_own = gates[:, 0].reshape(own, top)
    table = jnp.sum(
        jnp.where(routes_own[None] == expert_ids[:, None, None], gates_own[None], 0.0), -1
    )
    gate_rows = swap(table).reshape(groups * micro, rows)
    hit = gate_rows > 0.0
    slot = jnp.cumsum(hit.astype(jnp.int32), 1) - 1
    pick = (slot[:, None, :] == jnp.arange(capacity, dtype=jnp.int32)[None, :, None]) & hit[
        :, None, :
    ]
    gate_slots = jnp.sum(jnp.where(pick, gate_rows[:, None, :], 0.0), -1).reshape(-1, 1)
    pick = pick.astype(bf16)
    place = pick.swapaxes(1, 2)

    def dispatch(x):
        picked = jnp.einsum(
            "bst,btd->bsd",
            pick,
            x.reshape(groups * micro, rows, width),
            preferred_element_type=f32,
        )
        return picked.reshape(groups * micro * capacity, width)

    ff = w_shared_in.shape[1] // 2
    run = ff // (parts * groups)
    wsi_own = jnp.concatenate(
        [
            lax.dynamic_slice_in_dim(w_shared_in, c * (ff // parts) + me * run, run, 1)
            for c in range(2 * parts)
        ],
        1,
    )
    wso_own = lax.dynamic_slice_in_dim(w_shared_out, me * run, run, 0)
    wsi_me = jnp.concatenate([wsi_own] + others(wsi_own), 0)
    wso_me = lay_out(wso_own, others(wso_own))
    wei_others = others(w_expert_in[0])
    weo_others = others(w_expert_out[0])
    wq = pieces(w_query, wei_others[0], weo_others[0])
    wkvup = pieces(w_kv_up, wei_others[0], weo_others[0])

    cosine, sine = rope_tables(seq, ROPE)

    def table_of(values):
        both = jnp.concatenate([values, values], 1).reshape(groups, 1, rows, 2 * ROPE)
        return jnp.broadcast_to(both, (groups, micro, rows, 2 * ROPE)).reshape(total, 2 * ROPE)

    first = dot(after(act, gate_rows), w_first)
    q_nope = first[:, :NOPE].astype(bf16)
    latent_raw = first[:, NOPE : NOPE + LATENT]
    latent = normed(latent_raw, gain_kv).astype(bf16)
    at = NOPE + LATENT
    roped = (
        first[:, at : at + 2 * ROPE] * table_of(cosine) + first[:, at + 2 * ROPE :] * table_of(sine)
    ).astype(bf16)
    kvup = dot(latent, wkvup_me).astype(bf16)

    def owners(x):
        return x.reshape(groups, micro, rows, x.shape[-1])

    segs = segments[:, 0]
    head = (owners(q_nope), owners(roped), owners(kvup), segs)
    attn, lse = attend(*head)
    attn_own = swap(attn.reshape(groups, own, VDIM))
    attn_own = attn_own.swapaxes(0, 1).reshape(own, groups * VDIM)
    x1 = x_own.astype(f32) + dot_pieces(attn_own, wout)
    hid_own = normed(x1, gain_ffn).astype(bf16)
    hid_all = spread(own_first(hid_own, 1))
    attn_all = spread(after(attn_own, hid_all))

    spre = dot(hid_all, wsi_me)
    sact = swiglu(spre).astype(bf16)
    dsact = dot_nt(dy_all, wso_me)
    dspre = swiglu_back(spre, dsact).astype(bf16)
    size = width // parts
    g_si = dot_tn(dspre, hid_all)
    g_so = dot_tn(sact, dy_all)

    def shared_grads(r):
        rows_of = block_of(g_so, part + r)
        return jnp.concatenate(
            [g_si[:, r * size : (r + 1) * size]] + jnp.split(rows_of, parts, 1), 0
        )

    g_shared = exchanged(shared_grads(0), lambda r: shared_grads(r).astype(bf16)).astype(bf16)

    arrived = dispatch(hid_all).astype(bf16)
    dyexp = (gate_slots * dispatch(dy_all)).astype(bf16)
    wei = jnp.concatenate([w_expert_in[0]] + wei_others, 0)
    weo = lay_out(w_expert_out[0], weo_others)
    epre = dot(arrived, wei)
    eact = swiglu(epre).astype(bf16)
    deact = dot_nt(dyexp, weo)
    depre = swiglu_back(epre, deact).astype(bf16)
    dhid_rows = dot_nt(depre, wei).astype(bf16)
    dhid_part = put_back(place, dhid_rows, dspre, wsi_me, dot_nt)
    dhid_sum = collect(dhid_part)
    g_shared = stack(after(g_shared, dhid_sum))

    arrived, depre, eact, dyexp = lax.optimization_barrier(
        (arrived, depre, eact, dyexp, dhid_part)
    )[:4]
    gated = (gate_slots * dot(eact, weo)).astype(bf16)
    out_part = put_back(place, gated, sact, wso_me, dot)

    def expert_in_grad(r):
        return dot_tn(arrived[:, r * size : (r + 1) * size], depre)

    def expert_out_grad(r):
        short = eact.shape[1] // parts
        some = lax.dynamic_slice_in_dim(eact, ((part + r) % parts) * short, short, 1)
        return dot_tn(some, dyexp)

    sent_in = [expert_in_grad(r).astype(bf16) for r in range(1, parts)]
    sent_out = [expert_out_grad(r).astype(bf16) for r in range(1, parts)]
    dhid_sum = after(dhid_sum, out_part, *sent_in, *sent_out)
    got_in = [send(x, r).astype(f32) for r, x in enumerate(sent_in, 1)]
    got_out = [send(x, r).astype(f32) for r, x in enumerate(sent_out, 1)]
    out_sum = collect(after(out_part, dhid_sum))
    dhid = natural(dhid_sum, 1).astype(f32)

    dy = dy_own.astype(f32)
    dx1_norm, g_ffn_gain = normed_back(x1, gain_ffn, dhid)
    dx1 = dy + dx1_norm
    dx1_low = dx1.astype(bf16)
    dattn_own = dot_pieces_t(dx1_low, wout).astype(bf16)
    dattn = swap(dattn_own.reshape(own, groups, VDIM).swapaxes(0, 1))
    dao = after(dx1_low, dattn).reshape(own, groups, width // groups).swapaxes(0, 1)
    dao = swap(dao)
    dattn = dattn.reshape(groups, micro, rows, VDIM)
    back = attend_back(*head, lse, dattn, cosine, sine)
    moved = swap(back.reshape(groups, own, 512))

    def back_of(x, first_column, last_column):
        piece = x[..., first_column:last_column]
        return piece.swapaxes(0, 1).reshape(own, groups * (last_column - first_column))

    flat = back.reshape(total, 512)
    g_query = dot_tn(act, flat[:, :qk])
    g_kvup = dot_tn(latent, flat[:, 256:])
    g_out = dot_tn(attn_all, dao.reshape(total, width // groups))

    def fold(x):
        many = size // x.shape[0]
        return jnp.concatenate(jnp.split(x, many, 1), 0)

    def attn_grads(r):
        return jnp.concatenate(
            [
                block_of(g_out, part + r),
                g_query[r * size : (r + 1) * size],
                fold(block_of(g_kvup, part + r)),
            ],
            1,
        )

    g_attn = exchanged(attn_grads(0), lambda r: attn_grads(r).astype(bf16))

    dq_own = back_of(moved, 0, qk)
    dkvup_own = back_of(moved, 256, 512)
    dkrope_own = jnp.sum(moved[..., qk:256].astype(f32), 0)
    dlatent = dot_pieces_t(dkvup_own, wkvup)
    latent_own = lax.dynamic_slice_in_dim(latent_raw, me * own, own, 0)
    cos_own = jnp.tile(lax.dynamic_slice_in_dim(cosine, me * rows, rows, 0), (micro, 1))
    sin_own = jnp.tile(lax.dynamic_slice_in_dim(sine, me * rows, rows, 0), (micro, 1))
    dlatent_raw, g_kv_gain = normed_back(latent_own, gain_kv, dlatent)
    dkvfull = jnp.concatenate([dlatent_raw, rotate_back(dkrope_own, cos_own, sin_own)], -1)
    dkvfull = dkvfull.astype(bf16)
    dact = dot_pieces_t(dq_own, wq) + natural(dot_nt(dkvfull, w_down), 1)
    dx_norm, g_attn_gain = normed_back(x_own.astype(f32), gain_attn, dact)
    input_grad = dx1 + dx_norm

    g_down = dot_tn(act_own, dkvfull)
    down = LATENT + ROPE
    gain_count = sum(gain_sizes)

    def rest_grads(r):
        gains = [block_of(g, part + r) for g in (g_attn_gain, g_kv_gain, g_ffn_gain)]
        gains = jnp.concatenate(gains).reshape(groups, 1, gain_count // groups)
        gains = jnp.pad(gains, ((0, 0), (0, 0), (0, down - gain_count // groups)))
        rows_of = block_of(g_down, part + r).reshape(groups, size // groups, down)
        return jnp.concatenate([rows_of, gains], 1)

    rest = exchanged(rest_grads(0), lambda r: rest_grads(r).astype(bf16))
    rest = jnp.sum(swap(rest.astype(bf16)).astype(f32), 0).astype(bf16)
    count = g_attn.shape[1]
    extra = rest[:-1].reshape(-1, count)
    extra_rows = extra.shape[0]
    extra = jnp.concatenate([extra, jnp.pad(rest[-1:], ((0, 15), (0, 0)))[:, :count]], 0)
    g_attn = jnp.concatenate([g_attn.astype(bf16), extra], 0)
    g_attn = stack(row_major(g_attn))
    g_down = g_attn[:, size : size + extra_rows].astype(f32).reshape(size, down)
    gains = g_attn[:, size + extra_rows, : gain_count // groups].astype(f32).reshape(-1)
    gains = jnp.split(gains, cuts)

    mixed = (x1 + out_sum.astype(f32)).astype(bf16)
    g_ein = sum(got_in, expert_in_grad(0))
    g_eout = sum(got_out, expert_out_grad(0))
    out_grad, query_grad = attn_columns(g_attn, size, width // groups, qk)
    kvup_grad = kvup_columns(g_attn, size, width // groups + qk, LATENT // parts)
    shared_in_grad, shared_out_grad = shared_rows(g_shared, 2 * parts, run)
    return (
        mixed.reshape(micro, 1, rows, width),
        input_grad.reshape(micro, 1, rows, width),
        gains[0],
        query_grad,
        g_down,
        gains[1],
        kvup_grad,
        out_grad,
        gains[2],
        shared_in_grad,
        shared_out_grad,
        g_ein[None],
        g_eout[None],
    )


def solution(mesh):
    tok = P(None, "dp", "expert", None)
    row = P("dp", None)
    exp = P("expert", "dp", None)
    in_specs = (
        tok, tok, P(None, "dp", None), tok, tok,
        P("dp"), row, row, P("dp"), row, row, P("dp"), row, row, exp, exp,
    )
    out_specs = (
        tok, tok, P("dp"), row, row, P("dp"), row, row, P("dp"), row, row, exp, exp,
    )

    return jax.shard_map(
        per_device, mesh=mesh, in_specs=in_specs, out_specs=out_specs, check_vma=False
    )
```

```python
import functools

import jax
import jax.numpy as jnp
from jax import lax
from jax.experimental import pallas as pl
from jax.experimental.layout import Layout, with_layout_constraint
from jax.experimental.pallas import tpu as pltpu
from jax.sharding import PartitionSpec as P

HEADS = 16
NOPE = 128
ROPE = 64
VDIM = 128
LATENT = 512
DOC_MAX = 512


theta_base = 50000.0
eps_norm = 1e-06
bf16 = jnp.bfloat16
f32 = jnp.float32


def rope_tables(length, width):
    half = width // 2
    freq = theta_base ** (-2.0 * jnp.arange(half, dtype=f32) / width)
    angle = jnp.arange(length, dtype=f32)[:, None] * freq[None, :]
    cosine = jnp.concatenate([jnp.cos(angle), jnp.cos(angle)], -1)
    sine = jnp.concatenate([jnp.sin(angle), jnp.sin(angle)], -1)
    return (cosine, sine)


def rotate_back(value, cosine, sine):
    half = value.shape[-1] // 2
    scaled = value * sine
    turned = jnp.concatenate([scaled[..., half:], -scaled[..., :half]], -1)
    return value * cosine + turned


def normed(value, gain):
    return (
        value
        * lax.rsqrt(jnp.mean(value * value, -1, keepdims=True) + eps_norm)
        * gain.astype(f32)
    )


def normed_back(value, gain, grad):
    inv = lax.rsqrt(jnp.mean(value * value, -1, keepdims=True) + eps_norm)
    hat = value * inv
    scaled = grad * gain.astype(f32)
    inner = jnp.mean(scaled * hat, -1, keepdims=True)
    return inv * (scaled - hat * inner), jnp.sum(grad * hat, 0)


def swiglu_parts(packed):
    half = packed.shape[-1] // 2
    return packed[..., :half], packed[..., half:]


def swiglu(packed):
    gate, up = swiglu_parts(packed)
    return gate * jax.nn.sigmoid(gate) * up


def swiglu_back(packed, grad):
    gate, up = swiglu_parts(packed)
    sig = jax.nn.sigmoid(gate)
    d_gate = grad * up * sig * (1.0 + gate * (1.0 - sig))
    d_up = grad * gate * sig
    return jnp.concatenate([d_gate, d_up], -1)


def dot(left, right):
    return jnp.dot(left, right, preferred_element_type=f32)


def dot_tn(left, right):
    return lax.dot_general(left, right, (((0,), (0,)), ((), ())), preferred_element_type=f32)


def dot_nt(left, right):
    return lax.dot_general(left, right, (((1,), (1,)), ((), ())), preferred_element_type=f32)


def row_major(x):
    return with_layout_constraint(x, Layout(major_to_minor=tuple(range(x.ndim))))


def after(value, *first):
    return lax.optimization_barrier((value,) + first)[0]


def block_of_keys(refs, start, stop, low):
    qn_ref, rope_ref, kv_ref, seg_col, seg_row = refs
    rows = qn_ref.shape[2]

    def take(ref, first, last):
        return ref[first // rows : last // rows, 0].reshape(last - first, ref.shape[3])

    query = jnp.concatenate([take(qn_ref, start, stop), take(rope_ref, start, stop)[:, :ROPE]], 1)
    kv = take(kv_ref, low, stop)
    key = jnp.concatenate([kv[:, :NOPE], take(rope_ref, low, stop)[:, ROPE:]], 1)
    value = kv[:, NOPE:]
    score = dot_nt(query, key) * ((NOPE + ROPE) ** (-0.5))
    size = (stop - start, stop - low)
    q_at = lax.broadcasted_iota(jnp.int32, size, 0) + (start - low)
    k_at = lax.broadcasted_iota(jnp.int32, size, 1)
    allowed = (seg_col[0, start:stop] == seg_row[0, :, low:stop]) & (k_at <= q_at)
    return query, key, value, jnp.where(allowed, score, -1e30)


def query_blocks(seq, rows, size=256):
    for start in range(0, seq, size):
        low = max(0, start - DOC_MAX + 1) // rows * rows
        yield start, start + size, low


def attend_kernel(qn_ref, rope_ref, kv_ref, seg_col, seg_row, out_ref, lse_ref):
    owners, _, rows, _ = qn_ref.shape
    refs = (qn_ref, rope_ref, kv_ref, seg_col, seg_row)
    for start, stop, low in query_blocks(owners * rows, rows):
        _, _, value, score = block_of_keys(refs, start, stop, low)
        top = jnp.max(score, -1, keepdims=True)
        expo = jnp.exp(score - top)
        total = jnp.sum(expo, -1, keepdims=True)
        out = dot((expo / total).astype(bf16), value).astype(bf16)
        at = slice(start // rows, stop // rows)
        out_ref[at, 0] = out.reshape((stop - start) // rows, rows, VDIM)
        lse_ref[0, start:stop] = top + jnp.log(total)


def attend_back_kernel(
    qn_ref, rope_ref, kv_ref, seg_col, seg_row, lse_ref, dout_ref, cos_ref, sin_ref, back_ref, acc
):
    owners, _, rows, _ = qn_ref.shape
    seq = owners * rows
    refs = (qn_ref, rope_ref, kv_ref, seg_col, seg_row)
    acc[...] = jnp.zeros_like(acc)
    for start, stop, low in query_blocks(seq, rows):
        at = slice(start // rows, stop // rows)
        query, key, value, score = block_of_keys(refs, start, stop, low)
        prob = jnp.exp(score - lse_ref[0, start:stop])
        dout = dout_ref[at, 0].reshape(stop - start, VDIM)
        dprob = dot_nt(dout, value)
        delta = jnp.sum(prob * dprob, -1, keepdims=True)
        dscore = (prob * (dprob - delta) * ((NOPE + ROPE) ** (-0.5))).astype(bf16)
        dquery = dot(dscore, key)
        acc[low:stop, : NOPE + ROPE] += dot_tn(dscore, query)
        acc[low:stop, 256:] += dot_tn(prob.astype(bf16), dout)
        rope = rotate_back(dquery[:, NOPE:], cos_ref[start:stop], sin_ref[start:stop])
        whole = jnp.concatenate([dquery[:, :NOPE], rope, rope, dquery, rope], 1)
        back_ref[at, 0] = whole.astype(bf16).reshape((stop - start) // rows, rows, 512)
    dkey = acc[...]
    tail = jnp.concatenate([dkey[:, NOPE : NOPE + ROPE], dkey[:, :NOPE], dkey[:, 256:]], 1)
    back_ref[:, 0, :, NOPE + ROPE :] = tail.astype(bf16).reshape(owners, rows, 320)


def attend(q_nope, roped, kvup, segs):
    owners, micro, rows, _ = q_nope.shape
    seq = owners * rows
    spec = lambda c: pl.BlockSpec((owners, 1, rows, c), lambda m: (0, m, 0, 0))
    return pl.pallas_call(
        attend_kernel,
        out_shape=(
            jax.ShapeDtypeStruct((owners, micro, rows, VDIM), bf16),
            jax.ShapeDtypeStruct((micro, seq, 1), f32),
        ),
        grid=(micro,),
        in_specs=[
            spec(NOPE),
            spec(2 * ROPE),
            spec(2 * NOPE),
            pl.BlockSpec((1, seq, 1), lambda m: (m, 0, 0)),
            pl.BlockSpec((1, 1, seq), lambda m: (m, 0, 0)),
        ],
        out_specs=(spec(VDIM), pl.BlockSpec((1, seq, 1), lambda m: (m, 0, 0))),
        cost_estimate=pl.CostEstimate(
            flops=2 * micro * seq * 640 * 320,
            transcendentals=micro * seq * 640,
            bytes_accessed=micro * seq * 1400,
        ),
    )(q_nope, roped, kvup, segs[:, :, None], segs[:, None, :])


def attend_back(q_nope, roped, kvup, segs, lse, dout, cosine, sine):
    owners, micro, rows, _ = q_nope.shape
    seq = owners * rows
    spec = lambda c: pl.BlockSpec((owners, 1, rows, c), lambda m: (0, m, 0, 0))
    flat = pl.BlockSpec((seq, ROPE), lambda m: (0, 0))
    return pl.pallas_call(
        attend_back_kernel,
        out_shape=jax.ShapeDtypeStruct((owners, micro, rows, 512), bf16),
        grid=(micro,),
        in_specs=[
            spec(NOPE),
            spec(2 * ROPE),
            spec(2 * NOPE),
            pl.BlockSpec((1, seq, 1), lambda m: (m, 0, 0)),
            pl.BlockSpec((1, 1, seq), lambda m: (m, 0, 0)),
            pl.BlockSpec((1, seq, 1), lambda m: (m, 0, 0)),
            spec(VDIM),
            flat,
            flat,
        ],
        out_specs=spec(512),
        scratch_shapes=[pltpu.VMEM((seq, 384), f32)],
        cost_estimate=pl.CostEstimate(
            flops=2 * micro * seq * 640 * 832,
            transcendentals=micro * seq * 640,
            bytes_accessed=micro * seq * 2600,
        ),
    )(q_nope, roped, kvup, segs[:, :, None], segs[:, None, :], lse, dout, cosine, sine)


def put_back_kernel(place_ref, rows_ref, units_ref, weight_ref, out_ref):
    left = jnp.concatenate([place_ref[0], units_ref[...]], 1)
    right = jnp.concatenate([rows_ref[...], weight_ref[...]], 0)
    out_ref[...] = dot(left, right).astype(bf16)


def put_back(place, rows, units, weight):
    many, size, height = place.shape
    total, count = units.shape
    width = rows.shape[1]
    return pl.pallas_call(
        put_back_kernel,
        out_shape=jax.ShapeDtypeStruct((total, width), bf16),
        grid=(many,),
        in_specs=[
            pl.BlockSpec((1, size, height), lambda i: (i, 0, 0)),
            pl.BlockSpec((height, width), lambda i: (i, 0)),
            pl.BlockSpec((size, count), lambda i: (i, 0)),
            pl.BlockSpec(weight.shape, lambda i: (0, 0)),
        ],
        out_specs=pl.BlockSpec((size, width), lambda i: (i, 0)),
        cost_estimate=pl.CostEstimate(
            flops=2 * total * width * (height + count),
            transcendentals=0,
            bytes_accessed=2 * (total * width + rows.size + units.size + weight.size),
        ),
    )(place, rows, units, weight)


def shared_in_kernel(x_ref, out_ref, *, runs, piece):
    groups = x_ref.shape[0]
    turned = [x_ref[e].astype(f32).T for e in range(groups)]
    length = groups * piece
    parts = []
    for c in range(runs):
        parts += [t[:, c * piece : (c + 1) * piece] for t in turned]
        if length % 128 == 0:
            out_ref[:, c * length : (c + 1) * length] = jnp.concatenate(parts, 1)
            parts = []
    if parts:
        out_ref[...] = jnp.concatenate(parts, 1)


def shared_out_kernel(x_ref, out_ref, *, piece):
    rows = x_ref[0].astype(f32)
    count = rows.shape[0] // piece
    out_ref[0] = jnp.concatenate([rows[c * piece : (c + 1) * piece] for c in range(count)], 1)


def shared_rows(stacked, runs, piece):
    groups, count, size = stacked.shape
    first = runs * piece
    rest = count - first
    step = 128
    in_grad = pl.pallas_call(
        functools.partial(shared_in_kernel, runs=runs, piece=piece),
        out_shape=jax.ShapeDtypeStruct((size, groups * first), f32),
        grid=(size // step,),
        in_specs=[pl.BlockSpec((groups, first, step), lambda i: (0, 0, i))],
        out_specs=pl.BlockSpec((step, groups * first), lambda i: (i, 0)),
        cost_estimate=pl.CostEstimate(
            flops=0, transcendentals=0, bytes_accessed=6 * groups * first * size
        ),
    )(stacked)
    out_grad = pl.pallas_call(
        functools.partial(shared_out_kernel, piece=piece),
        out_shape=jax.ShapeDtypeStruct((groups, piece, rest // piece * size), f32),
        grid=(groups,),
        in_specs=[pl.BlockSpec((1, rest, size), lambda e: (e, first // rest, 0))],
        out_specs=pl.BlockSpec((1, piece, rest // piece * size), lambda e: (e, 0, 0)),
        cost_estimate=pl.CostEstimate(
            flops=0, transcendentals=0, bytes_accessed=6 * groups * rest * size
        ),
    )(stacked)
    return in_grad, out_grad.reshape(groups * piece, -1)


def attn_rows_kernel(x_ref, extra_ref, out_ref, query_ref, kvup_ref, down_ref, *, a, b, height):
    groups, _, count = x_ref.shape
    rest = count - a - b
    runs = x_ref.shape[1] // kvup_ref.shape[0]
    step = kvup_ref.shape[0]
    for e in range(0, groups, 2):
        one, two = x_ref[e].astype(f32), x_ref[e + 1].astype(f32)
        out_ref[:, e * a : (e + 2) * a] = jnp.concatenate([one[:, :a], two[:, :a]], 1)
        query_ref[:, e * b : (e + 2) * b] = jnp.concatenate(
            [one[:, a : a + b], two[:, a : a + b]], 1
        )
        pieces = [
            x[c * step : (c + 1) * step, a + b :] for x in (one, two) for c in range(runs)
        ]
        kvup_ref[:, e * runs * rest : (e + 2) * runs * rest] = jnp.concatenate(pieces, 1)
    for e in range(extra_ref.shape[0]):
        x = extra_ref[e].astype(f32)
        tail = x[height : height + height // 2]
        half = count // 2
        tail = jnp.concatenate([tail[:, :half], tail[:, half:]], 0)
        down_ref[e * height : (e + 1) * height] = jnp.concatenate([x[:height], tail], 1)


def attn_rows(stacked, rows, a, b, kvup_height, down_height):
    groups, _, count = stacked.shape
    size = 128
    steps = rows // size
    kvup_width = (count - a - b) * rows // kvup_height
    return pl.pallas_call(
        functools.partial(attn_rows_kernel, a=a, b=b, height=down_height),
        out_shape=(
            jax.ShapeDtypeStruct((rows, groups * a), f32),
            jax.ShapeDtypeStruct((rows, groups * b), f32),
            jax.ShapeDtypeStruct((kvup_height, groups * kvup_width), f32),
            jax.ShapeDtypeStruct((groups * down_height, count * 3 // 2), f32),
        ),
        grid=(steps,),
        in_specs=[
            pl.BlockSpec((groups, size, count), lambda i: (0, i, 0)),
            pl.BlockSpec((groups // steps, size, count), lambda i: (i, steps, 0)),
        ],
        out_specs=(
            pl.BlockSpec((size, groups * a), lambda i: (i, 0)),
            pl.BlockSpec((size, groups * b), lambda i: (i, 0)),
            pl.BlockSpec((kvup_height // steps, groups * kvup_width), lambda i: (i, 0)),
            pl.BlockSpec((groups // steps * down_height, count * 3 // 2), lambda i: (i, 0)),
        ),
        cost_estimate=pl.CostEstimate(
            flops=0, transcendentals=0, bytes_accessed=6 * stacked.size
        ),
    )(stacked, stacked)


def per_device(
    tokens,
    grad_out,
    segments,
    routes,
    gates,
    attn_gain,
    w_query,
    w_kv_down,
    kv_gain,
    w_kv_up,
    w_out,
    ffn_gain,
    w_shared_in,
    w_shared_out,
    w_expert_in,
    w_expert_out,
):
    micro, _, rows, width = tokens.shape
    groups = lax.axis_size("expert")
    parts = lax.axis_size("dp")
    me = lax.axis_index("expert")
    part = lax.axis_index("dp")
    own = micro * rows
    total = groups * own
    seq = rows * groups
    top = routes.shape[3]
    capacity = max(2, rows * top * 4 // (3 * groups))
    qk = NOPE + ROPE
    assert HEADS == groups

    def shift(x, step):
        return lax.ppermute(x, "dp", [((i + step) % parts, i) for i in range(parts)])

    def send(x, step):
        return lax.ppermute(x, "dp", [(i, (i + step) % parts) for i in range(parts)])

    def others(x):
        return [shift(x, r) for r in range(1, parts)]

    def turn(x, axis, amount):
        size = x.shape[axis]
        return lax.dynamic_slice_in_dim(
            jnp.concatenate([x, x], axis), amount * (size // parts), size, axis
        )

    def own_first(x, axis):
        return turn(x, axis, part)

    def natural(x, axis):
        return turn(x, axis, (parts - part) % parts)

    def lay_out(x, rest):
        size = x.shape[0]
        whole = jnp.zeros((parts * size,) + x.shape[1:], x.dtype)
        for r, piece in enumerate([x] + rest):
            at = ((part + r) % parts) * size
            whole = lax.dynamic_update_slice_in_dim(whole, piece, at, 0)
        return whole

    def block_of(full, index):
        size = full.shape[0] // parts
        return lax.dynamic_slice_in_dim(full, (index % parts) * size, size, 0)

    def exchanged(own_block, block_for):
        result = own_block.astype(f32)
        for r in range(1, parts):
            result = result + send(block_for(r), r).astype(f32)
        return result

    pairs = [(i, i ^ 1) for i in range(groups)]
    odd = me % 2

    def pieces(x, *first):
        size = x.shape[0]
        found = [(x, part * size)]
        if parts == 2:
            half = size // 2
            asked = lax.dynamic_slice_in_dim(x, odd * half, half, 0)
            if first:
                asked = after(asked, *first)
            got = shift(asked, 1)
            swapped = lax.ppermute(got, "expert", pairs)
            base = (1 - part) * size
            found += [(got, base + odd * half), (swapped, base + (1 - odd) * half)]
        else:
            asked = after(x, *first) if first else x
            found += [(y, ((part + r) % parts) * size) for r, y in enumerate(others(asked), 1)]
        return found

    def dot_pieces(x, blocks):
        return sum(
            dot(lax.dynamic_slice_in_dim(x, at, w.shape[0], 1), w) for w, at in blocks
        )

    def dot_pieces_t(x, blocks):
        whole = jnp.zeros((x.shape[0], sum(w.shape[0] for w, _ in blocks)), f32)
        for w, at in blocks:
            whole = lax.dynamic_update_slice_in_dim(whole, dot_nt(x, w), at, 1)
        return whole

    def spread(x):
        return lax.all_gather(x, "expert", axis=0, tiled=True)

    def stack(x):
        return lax.all_gather(x, "expert", axis=0, tiled=False)

    def swap(x):
        return lax.all_to_all(x, "expert", split_axis=0, concat_axis=0, tiled=True)

    def collect(x):
        return lax.psum_scatter(x, "expert", scatter_dimension=0, tiled=True)

    gain_sizes = (width // parts, LATENT // parts, width // parts)
    cuts = (gain_sizes[0], gain_sizes[0] + gain_sizes[1])
    own_gains = jnp.concatenate([attn_gain, kv_gain, ffn_gain])
    gain_rows = jnp.split(lay_out(own_gains[None], [y[None] for y in others(own_gains)]), cuts, 1)
    gain_attn, gain_kv, gain_ffn = (rows_of.reshape(-1) for rows_of in gain_rows)

    wq_own = lax.dynamic_slice_in_dim(w_query, me * qk, qk, 1)
    wq_me = jnp.concatenate([wq_own] + others(wq_own), 0)
    down_pieces = pieces(w_kv_down)
    w_down = jnp.zeros((width, LATENT + ROPE), bf16)
    for w, start in down_pieces:
        start = (start - part * (width // parts)) % width
        w_down = lax.dynamic_update_slice_in_dim(w_down, w, start, 0)
    wkvup_own = lax.dynamic_slice_in_dim(w_kv_up, me * 2 * NOPE, 2 * NOPE, 1)
    wkvup_me = lay_out(wkvup_own, others(wkvup_own))
    wout = pieces(w_out)

    def turned(w):
        return jnp.concatenate([-w[:, ROPE // 2 :], w[:, : ROPE // 2]], 1)

    rope_q, rope_k = wq_me[:, NOPE:], w_down[:, LATENT:]
    w_first = jnp.concatenate(
        [
            wq_me[:, :NOPE],
            w_down[:, :LATENT],
            rope_q,
            rope_k,
            turned(rope_q),
            turned(rope_k),
        ],
        1,
    )

    x_own = tokens[:, 0].reshape(own, width)
    dy_own = grad_out[:, 0].reshape(own, width)
    act_own = normed(x_own.astype(f32), gain_attn).astype(bf16)
    act = spread(own_first(act_own, 1))
    dy_all = spread(after(dy_own, act))

    expert_ids = jnp.arange(groups, dtype=jnp.int32)
    routes_own = routes[:, 0].reshape(own, top)
    gates_own = gates[:, 0].reshape(own, top)
    table = jnp.sum(
        jnp.where(routes_own[None] == expert_ids[:, None, None], gates_own[None], 0.0), -1
    )
    gate_rows = swap(table).reshape(groups * micro, rows)
    hit = gate_rows > 0.0
    slot = jnp.cumsum(hit.astype(jnp.int32), 1) - 1
    pick = (slot[:, None, :] == jnp.arange(capacity, dtype=jnp.int32)[None, :, None]) & hit[
        :, None, :
    ]
    gate_slots = jnp.sum(jnp.where(pick, gate_rows[:, None, :], 0.0), -1).reshape(-1, 1)
    pick = pick.astype(bf16)
    together = 4
    place = pick.swapaxes(1, 2).reshape(-1, together, rows, 1, capacity)
    place = place * jnp.eye(together, dtype=bf16)[None, :, None, :, None]
    place = place.reshape(-1, together * rows, together * capacity)

    def dispatch(x):
        picked = jnp.einsum(
            "bst,btd->bsd",
            pick,
            x.reshape(groups * micro, rows, width),
            preferred_element_type=f32,
        )
        return picked.reshape(groups * micro * capacity, width)

    ff = w_shared_in.shape[1] // 2
    run = ff // (parts * groups)
    wsi_own = jnp.concatenate(
        [
            lax.dynamic_slice_in_dim(w_shared_in, c * (ff // parts) + me * run, run, 1).T
            for c in range(2 * parts)
        ],
        0,
    )
    wso_own = lax.dynamic_slice_in_dim(w_shared_out, me * run, run, 0)
    wsi_me = jnp.concatenate([wsi_own] + others(wsi_own), 1)
    wso_me = lay_out(wso_own, others(wso_own))
    wei_others = others(w_expert_in[0])
    weo_others = others(w_expert_out[0])
    wq = pieces(w_query, wei_others[0], weo_others[0])
    wkvup = pieces(w_kv_up, wei_others[0], weo_others[0])
    wso = pieces(w_shared_out, wei_others[0], weo_others[0])

    cosine, sine = rope_tables(seq, ROPE)

    def table_of(values):
        both = jnp.concatenate([values, values], 1).reshape(groups, 1, rows, 2 * ROPE)
        return jnp.broadcast_to(both, (groups, micro, rows, 2 * ROPE)).reshape(total, 2 * ROPE)

    first = dot(after(act, gate_rows), w_first)
    q_nope = first[:, :NOPE].astype(bf16)
    latent_raw = first[:, NOPE : NOPE + LATENT]
    latent = normed(latent_raw, gain_kv).astype(bf16)
    at = NOPE + LATENT
    roped = (
        first[:, at : at + 2 * ROPE] * table_of(cosine) + first[:, at + 2 * ROPE :] * table_of(sine)
    ).astype(bf16)
    kvup = dot(latent, wkvup_me).astype(bf16)

    def owners(x):
        return x.reshape(groups, micro, rows, x.shape[-1])

    segs = segments[:, 0]
    head = (owners(q_nope), owners(roped), owners(kvup), segs)
    attn, lse = attend(*head)
    attn_own = swap(attn.reshape(groups, own, VDIM))
    attn_own = attn_own.swapaxes(0, 1).reshape(own, groups * VDIM)
    x1 = x_own.astype(f32) + dot_pieces(attn_own, wout)
    hid_own = normed(x1, gain_ffn).astype(bf16)
    hid_all = spread(own_first(hid_own, 1))
    attn_all = spread(after(attn_own, hid_all))

    size = width // parts
    arrived = dispatch(hid_all).astype(bf16)
    dyexp = (gate_slots * dispatch(dy_all)).astype(bf16)
    wei = jnp.concatenate([w_expert_in[0]] + wei_others, 0)
    weo = lay_out(w_expert_out[0], weo_others)
    epre = dot(arrived, wei)
    eact = swiglu(epre).astype(bf16)
    deact = dot_nt(dyexp, weo)
    depre = swiglu_back(epre, deact).astype(bf16)
    dhid_rows = dot_nt(depre, wei).astype(bf16)

    spre = dot_nt(hid_all, wsi_me)
    sact = swiglu(spre).astype(bf16)
    dsact = dot_nt(dy_all, wso_me)
    dspre = swiglu_back(spre, dsact).astype(bf16)
    dhid_part = put_back(place, dhid_rows, dspre, wsi_me)
    dhid_sum = collect(dhid_part)

    arrived, depre, eact, dyexp, dspre, sact = lax.optimization_barrier(
        (arrived, depre, eact, dyexp, dspre, sact, dhid_part)
    )[:6]
    g_si = dot_tn(dspre, hid_all)
    g_so = dot_tn(sact, dy_all)

    def shared_grads(r):
        rows_of = block_of(g_so, part + r)
        return jnp.concatenate(
            [g_si[:, r * size : (r + 1) * size]] + jnp.split(rows_of, parts, 1), 0
        )

    g_shared = exchanged(shared_grads(0), lambda r: shared_grads(r).astype(bf16))
    g_shared = stack(after(g_shared.astype(bf16), dhid_sum))

    def expert_in_grad(r):
        return dot_tn(arrived[:, r * size : (r + 1) * size], depre)

    def expert_out_grad(r):
        short = eact.shape[1] // parts
        some = lax.dynamic_slice_in_dim(eact, ((part + r) % parts) * short, short, 1)
        return dot_tn(some, dyexp)

    sent_in = [expert_in_grad(r).astype(bf16) for r in range(1, parts)]
    sent_out = [expert_out_grad(r).astype(bf16) for r in range(1, parts)]
    gated = (gate_slots * dot(eact, weo)).astype(bf16)
    dhid_sum = after(dhid_sum, gated, *sent_in, *sent_out)
    got_in = [send(x, r).astype(f32) for r, x in enumerate(sent_in, 1)]
    got_out = [send(x, r).astype(f32) for r, x in enumerate(sent_out, 1)]
    dhid = natural(dhid_sum, 1).astype(f32)

    dy = dy_own.astype(f32)
    dx1_norm, g_ffn_gain = normed_back(x1, gain_ffn, dhid)
    dx1 = dy + dx1_norm
    dx1_low = dx1.astype(bf16)
    dattn_own = dot_pieces_t(dx1_low, wout).astype(bf16)
    dattn = swap(dattn_own.reshape(own, groups, VDIM).swapaxes(0, 1))
    dao = after(dx1_low, dattn).reshape(own, groups, width // groups).swapaxes(0, 1)
    dao = swap(dao)
    dattn = dattn.reshape(groups, micro, rows, VDIM)
    back = attend_back(*head, lse, dattn, cosine, sine)
    moved = swap(back.reshape(groups, own, 512))

    def back_of(x, first_column, last_column):
        piece = x[..., first_column:last_column]
        return piece.swapaxes(0, 1).reshape(own, groups * (last_column - first_column))

    flat = back.reshape(total, 512)
    g_query = dot_tn(act, flat[:, :qk])
    g_kvup = dot_tn(latent, flat[:, 256:])
    g_out = dot_tn(attn_all, dao.reshape(total, width // groups))

    def fold(x):
        steps = size // 128
        runs = size // x.shape[0]
        x = x.reshape(steps, x.shape[0] // steps, runs, x.shape[1] // runs)
        return x.swapaxes(1, 2).reshape(size, -1)

    def attn_grads(r):
        return jnp.concatenate(
            [
                block_of(g_out, part + r),
                g_query[r * size : (r + 1) * size],
                fold(block_of(g_kvup, part + r)),
            ],
            1,
        )

    g_attn = exchanged(attn_grads(0), lambda r: attn_grads(r).astype(bf16))

    gated, sact = lax.optimization_barrier((gated, sact, moved))[:2]
    returned = swap(gated.reshape(groups, micro * capacity, width))
    hidden = swap(after(sact, returned).reshape(groups, own, -1))
    hidden = hidden.reshape(groups, own, parts, run).transpose(1, 2, 0, 3).reshape(own, ff)
    hit_own = routes_own.reshape(micro, rows, 1, top) == expert_ids[:, None]
    hit_own = jnp.any(hit_own, -1)
    slot_own = jnp.cumsum(hit_own.astype(jnp.int32), 1) - 1
    slots = jnp.arange(capacity, dtype=jnp.int32)
    find = ((slot_own[..., None] == slots) & hit_own[..., None]).astype(bf16)
    routed = jnp.einsum(
        "mtk,mkd->mtd",
        find.reshape(micro, rows, groups * capacity),
        returned.reshape(groups, micro, capacity, width)
        .swapaxes(0, 1)
        .reshape(micro, groups * capacity, width),
        preferred_element_type=f32,
    ).reshape(own, width)
    out_sum = routed + dot_pieces(hidden, wso)

    dq_own = back_of(moved, 0, qk)
    dkvup_own = back_of(moved, 256, 512)
    dkrope_own = jnp.sum(moved[..., qk:256].astype(f32), 0)
    dlatent = dot_pieces_t(dkvup_own, wkvup)
    latent_own = lax.dynamic_slice_in_dim(latent_raw, me * own, own, 0)
    cos_own = jnp.tile(lax.dynamic_slice_in_dim(cosine, me * rows, rows, 0), (micro, 1))
    sin_own = jnp.tile(lax.dynamic_slice_in_dim(sine, me * rows, rows, 0), (micro, 1))
    dlatent_raw, g_kv_gain = normed_back(latent_own, gain_kv, dlatent)
    dkvfull = jnp.concatenate([dlatent_raw, rotate_back(dkrope_own, cos_own, sin_own)], -1)
    dkvfull = dkvfull.astype(bf16)
    down = LATENT + ROPE
    early = jnp.concatenate([g_kv_gain, g_ffn_gain])
    short = early.shape[0]
    early = jnp.pad(early, (0, 16 * down - short)).reshape(16, down)
    dkv_all = spread(jnp.concatenate([dkvfull, early.astype(bf16)], 0))
    dkv_all = dkv_all.reshape(groups, own + 16, down)
    early = jnp.sum(dkv_all[:, own:].astype(f32), 0).reshape(-1)[:short]
    dkv_all = dkv_all[:, :own].reshape(total, down)
    dact = dot_pieces_t(dq_own, wq) + natural(dot_nt(dkvfull, w_down), 1)
    dx_norm, g_attn_gain = normed_back(x_own.astype(f32), gain_attn, dact)
    input_grad = dx1 + dx_norm

    height = size // groups
    act_rows = jnp.concatenate(
        [
            lax.dynamic_slice_in_dim(act, c * size + me * height, height, 1)
            for c in range(parts)
        ],
        1,
    )
    g_down = dot_tn(act_rows, dkv_all)
    g_down = exchanged(
        g_down[:height], lambda r: g_down[r * height : (r + 1) * height].astype(bf16)
    ).astype(bf16)
    early_kv, early_ffn = early[:LATENT], early[LATENT:]

    def early_gains(r):
        return jnp.concatenate([block_of(early_kv, part + r), block_of(early_ffn, part + r)])

    early = exchanged(early_gains(0), early_gains)
    late = exchanged(block_of(g_attn_gain, part), lambda r: block_of(g_attn_gain, part + r))
    count = g_attn.shape[1]
    tail = g_down[:, count:]
    tail = jnp.concatenate([tail[: height // 2], tail[height // 2 :]], 1)
    extra = jnp.concatenate([g_down[:, :count], tail], 0)
    at_late = size + extra.shape[0]
    late_rows = -(-size // count)
    late = jnp.pad(late, (0, late_rows * count - size)).reshape(late_rows, count)
    extra = jnp.concatenate([extra, late.astype(bf16)], 0)
    extra = jnp.pad(extra, ((0, 128 - extra.shape[0]), (0, 0)))
    g_attn = jnp.concatenate([g_attn.astype(bf16), extra], 0)
    g_attn = stack(row_major(g_attn))
    late = jnp.sum(g_attn[:, at_late : at_late + late_rows].astype(f32), 0).reshape(-1)[:size]
    gains = (late, early[: LATENT // parts], early[LATENT // parts :])

    mixed = (x1 + out_sum).astype(bf16)
    g_ein = sum(got_in, expert_in_grad(0))
    g_eout = sum(got_out, expert_out_grad(0))
    out_grad, query_grad, kvup_grad, g_down = attn_rows(
        g_attn, size, width // groups, qk, LATENT // parts, height
    )
    shared_in_grad, shared_out_grad = shared_rows(g_shared, 2 * parts, run)
    return (
        mixed.reshape(micro, 1, rows, width),
        input_grad.reshape(micro, 1, rows, width),
        gains[0],
        query_grad,
        g_down,
        gains[1],
        kvup_grad,
        out_grad,
        gains[2],
        shared_in_grad,
        shared_out_grad,
        g_ein[None],
        g_eout[None],
    )


def solution(mesh):
    tok = P(None, "dp", "expert", None)
    row = P("dp", None)
    exp = P("expert", "dp", None)
    in_specs = (
        tok, tok, P(None, "dp", None), tok, tok,
        P("dp"), row, row, P("dp"), row, row, P("dp"), row, row, exp, exp,
    )
    out_specs = (
        tok, tok, P("dp"), row, row, P("dp"), row, row, P("dp"), row, row, exp, exp,
    )

    return jax.shard_map(
        per_device, mesh=mesh, in_specs=in_specs, out_specs=out_specs, check_vma=False
    )
```

```python
import functools

import jax
import jax.numpy as jnp
from jax import lax
from jax.experimental import pallas as pl
from jax.experimental.layout import Layout, with_layout_constraint
from jax.experimental.pallas import tpu as pltpu
from jax.sharding import PartitionSpec as P

HEADS = 16
NOPE = 128
ROPE = 64
VDIM = 128
LATENT = 512
DOC_MAX = 512


theta_base = 50000.0
eps_norm = 1e-06
bf16 = jnp.bfloat16
f32 = jnp.float32


def rope_tables(length, width):
    half = width // 2
    freq = theta_base ** (-2.0 * jnp.arange(half, dtype=f32) / width)
    angle = jnp.arange(length, dtype=f32)[:, None] * freq[None, :]
    cosine = jnp.concatenate([jnp.cos(angle), jnp.cos(angle)], -1)
    sine = jnp.concatenate([jnp.sin(angle), jnp.sin(angle)], -1)
    return (cosine, sine)


def rotate_back(value, cosine, sine):
    half = value.shape[-1] // 2
    scaled = value * sine
    turned = jnp.concatenate([scaled[..., half:], -scaled[..., :half]], -1)
    return value * cosine + turned


def normed(value, gain):
    return (
        value
        * lax.rsqrt(jnp.mean(value * value, -1, keepdims=True) + eps_norm)
        * gain.astype(f32)
    )


def normed_back(value, gain, grad):
    inv = lax.rsqrt(jnp.mean(value * value, -1, keepdims=True) + eps_norm)
    hat = value * inv
    scaled = grad * gain.astype(f32)
    inner = jnp.mean(scaled * hat, -1, keepdims=True)
    return inv * (scaled - hat * inner), jnp.sum(grad * hat, 0)


def swiglu_parts(packed):
    half = packed.shape[-1] // 2
    return packed[..., :half], packed[..., half:]


def swiglu(packed):
    gate, up = swiglu_parts(packed)
    return gate * jax.nn.sigmoid(gate) * up


def swiglu_back(packed, grad):
    gate, up = swiglu_parts(packed)
    sig = jax.nn.sigmoid(gate)
    d_gate = grad * up * sig * (1.0 + gate * (1.0 - sig))
    d_up = grad * gate * sig
    return jnp.concatenate([d_gate, d_up], -1)


def dot(left, right):
    return jnp.dot(left, right, preferred_element_type=f32)


def dot_tn(left, right):
    return lax.dot_general(left, right, (((0,), (0,)), ((), ())), preferred_element_type=f32)


def dot_nt(left, right):
    return lax.dot_general(left, right, (((1,), (1,)), ((), ())), preferred_element_type=f32)


def row_major(x):
    return with_layout_constraint(x, Layout(major_to_minor=tuple(range(x.ndim))))


def after(value, *first):
    return lax.optimization_barrier((value,) + first)[0]


def block_of_keys(refs, start, stop, low):
    qn_ref, rope_ref, kv_ref, seg_col, seg_row = refs
    rows = qn_ref.shape[2]

    def take(ref, first, last):
        return ref[first // rows : last // rows, 0].reshape(last - first, ref.shape[3])

    query = jnp.concatenate([take(qn_ref, start, stop), take(rope_ref, start, stop)[:, :ROPE]], 1)
    kv = take(kv_ref, low, stop)
    key = jnp.concatenate([kv[:, :NOPE], take(rope_ref, low, stop)[:, ROPE:]], 1)
    value = kv[:, NOPE:]
    score = dot_nt(query, key) * ((NOPE + ROPE) ** (-0.5))
    size = (stop - start, stop - low)
    q_at = lax.broadcasted_iota(jnp.int32, size, 0) + (start - low)
    k_at = lax.broadcasted_iota(jnp.int32, size, 1)
    allowed = (seg_col[0, start:stop] == seg_row[0, :, low:stop]) & (k_at <= q_at)
    return query, key, value, jnp.where(allowed, score, -1e30)


def query_blocks(seq, rows, size=256):
    for start in range(0, seq, size):
        low = max(0, start - DOC_MAX + 1) // rows * rows
        yield start, start + size, low


def attend_kernel(qn_ref, rope_ref, kv_ref, seg_col, seg_row, out_ref, lse_ref):
    owners, _, rows, _ = qn_ref.shape
    refs = (qn_ref, rope_ref, kv_ref, seg_col, seg_row)
    for start, stop, low in query_blocks(owners * rows, rows):
        _, _, value, score = block_of_keys(refs, start, stop, low)
        top = jnp.max(score, -1, keepdims=True)
        expo = jnp.exp(score - top)
        total = jnp.sum(expo, -1, keepdims=True)
        out = dot((expo / total).astype(bf16), value).astype(bf16)
        at = slice(start // rows, stop // rows)
        out_ref[at, 0] = out.reshape((stop - start) // rows, rows, VDIM)
        lse_ref[0, start:stop] = top + jnp.log(total)


def attend_back_kernel(
    qn_ref, rope_ref, kv_ref, seg_col, seg_row, lse_ref, dout_ref, cos_ref, sin_ref, back_ref, acc
):
    owners, _, rows, _ = qn_ref.shape
    seq = owners * rows
    refs = (qn_ref, rope_ref, kv_ref, seg_col, seg_row)
    acc[...] = jnp.zeros_like(acc)
    for start, stop, low in query_blocks(seq, rows):
        at = slice(start // rows, stop // rows)
        query, key, value, score = block_of_keys(refs, start, stop, low)
        prob = jnp.exp(score - lse_ref[0, start:stop])
        dout = dout_ref[at, 0].reshape(stop - start, VDIM)
        dprob = dot_nt(dout, value)
        delta = jnp.sum(prob * dprob, -1, keepdims=True)
        dscore = (prob * (dprob - delta) * ((NOPE + ROPE) ** (-0.5))).astype(bf16)
        dquery = dot(dscore, key)
        acc[low:stop, : NOPE + ROPE] += dot_tn(dscore, query)
        acc[low:stop, 256:] += dot_tn(prob.astype(bf16), dout)
        rope = rotate_back(dquery[:, NOPE:], cos_ref[start:stop], sin_ref[start:stop])
        whole = jnp.concatenate([dquery[:, :NOPE], rope, rope, dquery, rope], 1)
        back_ref[at, 0] = whole.astype(bf16).reshape((stop - start) // rows, rows, 512)
    dkey = acc[...]
    tail = jnp.concatenate([dkey[:, NOPE : NOPE + ROPE], dkey[:, :NOPE], dkey[:, 256:]], 1)
    back_ref[:, 0, :, NOPE + ROPE :] = tail.astype(bf16).reshape(owners, rows, 320)


def attend(q_nope, roped, kvup, segs):
    owners, micro, rows, _ = q_nope.shape
    seq = owners * rows
    spec = lambda c: pl.BlockSpec((owners, 1, rows, c), lambda m: (0, m, 0, 0))
    return pl.pallas_call(
        attend_kernel,
        out_shape=(
            jax.ShapeDtypeStruct((owners, micro, rows, VDIM), bf16),
            jax.ShapeDtypeStruct((micro, seq, 1), f32),
        ),
        grid=(micro,),
        in_specs=[
            spec(NOPE),
            spec(2 * ROPE),
            spec(2 * NOPE),
            pl.BlockSpec((1, seq, 1), lambda m: (m, 0, 0)),
            pl.BlockSpec((1, 1, seq), lambda m: (m, 0, 0)),
        ],
        out_specs=(spec(VDIM), pl.BlockSpec((1, seq, 1), lambda m: (m, 0, 0))),
        cost_estimate=pl.CostEstimate(
            flops=2 * micro * seq * 640 * 320,
            transcendentals=micro * seq * 640,
            bytes_accessed=micro * seq * 1400,
        ),
    )(q_nope, roped, kvup, segs[:, :, None], segs[:, None, :])


def attend_back(q_nope, roped, kvup, segs, lse, dout, cosine, sine):
    owners, micro, rows, _ = q_nope.shape
    seq = owners * rows
    spec = lambda c: pl.BlockSpec((owners, 1, rows, c), lambda m: (0, m, 0, 0))
    flat = pl.BlockSpec((seq, ROPE), lambda m: (0, 0))
    return pl.pallas_call(
        attend_back_kernel,
        out_shape=jax.ShapeDtypeStruct((owners, micro, rows, 512), bf16),
        grid=(micro,),
        in_specs=[
            spec(NOPE),
            spec(2 * ROPE),
            spec(2 * NOPE),
            pl.BlockSpec((1, seq, 1), lambda m: (m, 0, 0)),
            pl.BlockSpec((1, 1, seq), lambda m: (m, 0, 0)),
            pl.BlockSpec((1, seq, 1), lambda m: (m, 0, 0)),
            spec(VDIM),
            flat,
            flat,
        ],
        out_specs=spec(512),
        scratch_shapes=[pltpu.VMEM((seq, 384), f32)],
        cost_estimate=pl.CostEstimate(
            flops=2 * micro * seq * 640 * 832,
            transcendentals=micro * seq * 640,
            bytes_accessed=micro * seq * 2600,
        ),
    )(q_nope, roped, kvup, segs[:, :, None], segs[:, None, :], lse, dout, cosine, sine)


def put_back_kernel(place_ref, rows_ref, units_ref, *refs):
    *weight_refs, out_ref = refs
    left = jnp.concatenate([place_ref[0], units_ref[...]], 1)
    weight = jnp.concatenate([w[...] for w in weight_refs], 1)
    right = jnp.concatenate([rows_ref[...], weight], 0)
    out_ref[...] = dot(left, right).astype(bf16)


def put_back(place, rows, units, *weights):
    many, size, height = place.shape
    total, count = units.shape
    width = rows.shape[1]
    return pl.pallas_call(
        put_back_kernel,
        out_shape=jax.ShapeDtypeStruct((total, width), bf16),
        grid=(many,),
        in_specs=[
            pl.BlockSpec((1, size, height), lambda i: (i, 0, 0)),
            pl.BlockSpec((height, width), lambda i: (i, 0)),
            pl.BlockSpec((size, count), lambda i: (i, 0)),
            *(pl.BlockSpec(w.shape, lambda i: (0, 0)) for w in weights),
        ],
        out_specs=pl.BlockSpec((size, width), lambda i: (i, 0)),
        cost_estimate=pl.CostEstimate(
            flops=2 * total * width * (height + count),
            transcendentals=0,
            bytes_accessed=2 * (total * width + rows.size + units.size + count * width),
        ),
    )(place, rows, units, *weights)


def shared_in_kernel(x_ref, out_ref, *, runs, piece):
    groups = x_ref.shape[0]
    turned = [x_ref[e].astype(f32).T for e in range(groups)]
    length = groups * piece
    parts = []
    for c in range(runs):
        parts += [t[:, c * piece : (c + 1) * piece] for t in turned]
        if length % 128 == 0:
            out_ref[:, c * length : (c + 1) * length] = jnp.concatenate(parts, 1)
            parts = []
    if parts:
        out_ref[...] = jnp.concatenate(parts, 1)


def shared_out_kernel(x_ref, out_ref, *, piece):
    rows = x_ref[0].astype(f32)
    count = rows.shape[0] // piece
    out_ref[0] = jnp.concatenate([rows[c * piece : (c + 1) * piece] for c in range(count)], 1)


def shared_rows(stacked, runs, piece):
    groups, count, size = stacked.shape
    first = runs * piece
    rest = count - first
    step = 128
    in_grad = pl.pallas_call(
        functools.partial(shared_in_kernel, runs=runs, piece=piece),
        out_shape=jax.ShapeDtypeStruct((size, groups * first), f32),
        grid=(size // step,),
        in_specs=[pl.BlockSpec((groups, first, step), lambda i: (0, 0, i))],
        out_specs=pl.BlockSpec((step, groups * first), lambda i: (i, 0)),
        cost_estimate=pl.CostEstimate(
            flops=0, transcendentals=0, bytes_accessed=6 * groups * first * size
        ),
    )(stacked)
    out_grad = pl.pallas_call(
        functools.partial(shared_out_kernel, piece=piece),
        out_shape=jax.ShapeDtypeStruct((groups, piece, rest // piece * size), f32),
        grid=(groups,),
        in_specs=[pl.BlockSpec((1, rest, size), lambda e: (e, first // rest, 0))],
        out_specs=pl.BlockSpec((1, piece, rest // piece * size), lambda e: (e, 0, 0)),
        cost_estimate=pl.CostEstimate(
            flops=0, transcendentals=0, bytes_accessed=6 * groups * rest * size
        ),
    )(stacked)
    return in_grad, out_grad.reshape(groups * piece, -1)


def attn_rows_kernel(x_ref, extra_ref, out_ref, query_ref, kvup_ref, down_ref, *, a, b, height):
    groups, _, count = x_ref.shape
    rest = count - a - b
    runs = x_ref.shape[1] // kvup_ref.shape[0]
    step = kvup_ref.shape[0]
    for e in range(0, groups, 2):
        one, two = x_ref[e].astype(f32), x_ref[e + 1].astype(f32)
        out_ref[:, e * a : (e + 2) * a] = jnp.concatenate([one[:, :a], two[:, :a]], 1)
        query_ref[:, e * b : (e + 2) * b] = jnp.concatenate(
            [one[:, a : a + b], two[:, a : a + b]], 1
        )
        pieces = [
            x[c * step : (c + 1) * step, a + b :] for x in (one, two) for c in range(runs)
        ]
        kvup_ref[:, e * runs * rest : (e + 2) * runs * rest] = jnp.concatenate(pieces, 1)
    half = count // 2
    rows = []
    for e in range(extra_ref.shape[0]):
        x = extra_ref[e].astype(f32)
        tail = x[height : height + height // 2]
        tail = jnp.concatenate([tail[:, :half], tail[:, half:]], 0)
        rows.append(jnp.concatenate([x[:height], tail], 1))
    down_ref[...] = jnp.concatenate(rows, 0).T


def attn_rows(stacked, rows, a, b, kvup_height, down_height):
    groups, _, count = stacked.shape
    size = 128
    steps = rows // size
    kvup_width = (count - a - b) * rows // kvup_height
    return pl.pallas_call(
        functools.partial(attn_rows_kernel, a=a, b=b, height=down_height),
        out_shape=(
            jax.ShapeDtypeStruct((rows, groups * a), f32),
            jax.ShapeDtypeStruct((rows, groups * b), f32),
            jax.ShapeDtypeStruct((kvup_height, groups * kvup_width), f32),
            jax.ShapeDtypeStruct((count * 3 // 2, groups * down_height), f32),
        ),
        grid=(steps,),
        in_specs=[
            pl.BlockSpec((groups, size, count), lambda i: (0, i, 0)),
            pl.BlockSpec((groups // steps, size, count), lambda i: (i, steps, 0)),
        ],
        out_specs=(
            pl.BlockSpec((size, groups * a), lambda i: (i, 0)),
            pl.BlockSpec((size, groups * b), lambda i: (i, 0)),
            pl.BlockSpec((kvup_height // steps, groups * kvup_width), lambda i: (i, 0)),
            pl.BlockSpec((count * 3 // 2, groups // steps * down_height), lambda i: (0, i)),
        ),
        cost_estimate=pl.CostEstimate(
            flops=0, transcendentals=0, bytes_accessed=6 * stacked.size
        ),
    )(stacked, stacked)


def per_device(
    tokens,
    grad_out,
    segments,
    routes,
    gates,
    attn_gain,
    w_query,
    w_kv_down,
    kv_gain,
    w_kv_up,
    w_out,
    ffn_gain,
    w_shared_in,
    w_shared_out,
    w_expert_in,
    w_expert_out,
):
    micro, _, rows, width = tokens.shape
    groups = lax.axis_size("expert")
    parts = lax.axis_size("dp")
    me = lax.axis_index("expert")
    part = lax.axis_index("dp")
    own = micro * rows
    total = groups * own
    seq = rows * groups
    top = routes.shape[3]
    capacity = max(2, rows * top * 4 // (3 * groups))
    qk = NOPE + ROPE
    assert HEADS == groups

    def shift(x, step):
        return lax.ppermute(x, "dp", [((i + step) % parts, i) for i in range(parts)])

    def send(x, step):
        return lax.ppermute(x, "dp", [(i, (i + step) % parts) for i in range(parts)])

    def others(x):
        return [shift(x, r) for r in range(1, parts)]

    def turn(x, axis, amount):
        size = x.shape[axis]
        return lax.dynamic_slice_in_dim(
            jnp.concatenate([x, x], axis), amount * (size // parts), size, axis
        )

    def own_first(x, axis):
        return turn(x, axis, part)

    def natural(x, axis):
        return turn(x, axis, (parts - part) % parts)

    def lay_out(x, rest):
        size = x.shape[0]
        whole = jnp.zeros((parts * size,) + x.shape[1:], x.dtype)
        for r, piece in enumerate([x] + rest):
            at = ((part + r) % parts) * size
            whole = lax.dynamic_update_slice_in_dim(whole, piece, at, 0)
        return whole

    def block_of(full, index):
        size = full.shape[0] // parts
        return lax.dynamic_slice_in_dim(full, (index % parts) * size, size, 0)

    def exchanged(own_block, block_for):
        result = own_block.astype(f32)
        for r in range(1, parts):
            result = result + send(block_for(r), r).astype(f32)
        return result

    pairs = [(i, i ^ 1) for i in range(groups)]
    odd = me % 2

    def pieces(x, *first):
        size = x.shape[0]
        found = [(x, part * size)]
        if parts == 2:
            half = size // 2
            asked = lax.dynamic_slice_in_dim(x, odd * half, half, 0)
            if first:
                asked = after(asked, *first)
            got = shift(asked, 1)
            swapped = lax.ppermute(got, "expert", pairs)
            base = (1 - part) * size
            found += [(got, base + odd * half), (swapped, base + (1 - odd) * half)]
        else:
            asked = after(x, *first) if first else x
            found += [(y, ((part + r) % parts) * size) for r, y in enumerate(others(asked), 1)]
        return found

    def dot_pieces(x, blocks):
        return sum(
            dot(lax.dynamic_slice_in_dim(x, at, w.shape[0], 1), w) for w, at in blocks
        )

    def dot_pieces_t(x, blocks):
        whole = jnp.zeros((x.shape[0], sum(w.shape[0] for w, _ in blocks)), f32)
        for w, at in blocks:
            whole = lax.dynamic_update_slice_in_dim(whole, dot_nt(x, w), at, 1)
        return whole

    def spread(x):
        return lax.all_gather(x, "expert", axis=0, tiled=True)

    def stack(x):
        return lax.all_gather(x, "expert", axis=0, tiled=False)

    def swap(x):
        return lax.all_to_all(x, "expert", split_axis=0, concat_axis=0, tiled=True)

    def collect(x):
        return lax.psum_scatter(x, "expert", scatter_dimension=0, tiled=True)

    gain_sizes = (width // parts, LATENT // parts, width // parts)
    cuts = (gain_sizes[0], gain_sizes[0] + gain_sizes[1])
    own_gains = jnp.concatenate([attn_gain, kv_gain, ffn_gain])
    gain_rows = jnp.split(lay_out(own_gains[None], [y[None] for y in others(own_gains)]), cuts, 1)
    gain_attn, gain_kv, gain_ffn = (rows_of.reshape(-1) for rows_of in gain_rows)

    wq_own = lax.dynamic_slice_in_dim(w_query, me * qk, qk, 1)
    wq_me = jnp.concatenate([wq_own] + others(wq_own), 0)
    down_pieces = pieces(w_kv_down)
    w_down = jnp.zeros((width, LATENT + ROPE), bf16)
    for w, start in down_pieces:
        start = (start - part * (width // parts)) % width
        w_down = lax.dynamic_update_slice_in_dim(w_down, w, start, 0)
    wkvup_own = lax.dynamic_slice_in_dim(w_kv_up, me * 2 * NOPE, 2 * NOPE, 1)
    wkvup_me = lay_out(wkvup_own, others(wkvup_own))
    wout = pieces(w_out)

    def turned(w):
        return jnp.concatenate([-w[:, ROPE // 2 :], w[:, : ROPE // 2]], 1)

    rope_q, rope_k = wq_me[:, NOPE:], w_down[:, LATENT:]
    w_first = jnp.concatenate(
        [
            wq_me[:, :NOPE],
            w_down[:, :LATENT],
            rope_q,
            rope_k,
            turned(rope_q),
            turned(rope_k),
        ],
        1,
    )

    x_own = tokens[:, 0].reshape(own, width)
    dy_own = grad_out[:, 0].reshape(own, width)
    act_own = normed(x_own.astype(f32), gain_attn).astype(bf16)
    act = spread(own_first(act_own, 1))
    dy_all = spread(after(dy_own, act))

    expert_ids = jnp.arange(groups, dtype=jnp.int32)
    routes_own = routes[:, 0].reshape(own, top)
    gates_own = gates[:, 0].reshape(own, top)
    table = jnp.sum(
        jnp.where(routes_own[None] == expert_ids[:, None, None], gates_own[None], 0.0), -1
    )
    gate_rows = swap(table).reshape(groups * micro, rows)
    hit = gate_rows > 0.0
    slot = jnp.cumsum(hit.astype(jnp.int32), 1) - 1
    pick = (slot[:, None, :] == jnp.arange(capacity, dtype=jnp.int32)[None, :, None]) & hit[
        :, None, :
    ]
    gate_slots = jnp.sum(jnp.where(pick, gate_rows[:, None, :], 0.0), -1).reshape(-1, 1)
    pick = pick.astype(bf16)
    together = 4
    place = pick.swapaxes(1, 2).reshape(-1, together, rows, 1, capacity)
    place = place * jnp.eye(together, dtype=bf16)[None, :, None, :, None]
    place = place.reshape(-1, together * rows, together * capacity)

    def dispatch(x):
        picked = jnp.einsum(
            "bst,btd->bsd",
            pick,
            x.reshape(groups * micro, rows, width),
            preferred_element_type=f32,
        )
        return picked.reshape(groups * micro * capacity, width)

    ff = w_shared_in.shape[1] // 2
    run = ff // (parts * groups)
    wsi_own = jnp.concatenate(
        [
            lax.dynamic_slice_in_dim(w_shared_in, c * (ff // parts) + me * run, run, 1).T
            for c in range(2 * parts)
        ],
        0,
    )
    wso_own = lax.dynamic_slice_in_dim(w_shared_out, me * run, run, 0)
    wsi_blocks = [wsi_own] + others(wsi_own)
    wsi_me = jnp.concatenate(wsi_blocks, 1)
    wso_me = lay_out(wso_own, others(wso_own))
    wei_others = others(w_expert_in[0])
    weo_others = others(w_expert_out[0])
    wq = pieces(w_query, wei_others[0], weo_others[0])
    wkvup = pieces(w_kv_up, wei_others[0], weo_others[0])
    wso = pieces(w_shared_out, wei_others[0], weo_others[0])

    cosine, sine = rope_tables(seq, ROPE)

    def table_of(values):
        both = jnp.concatenate([values, values], 1).reshape(groups, 1, rows, 2 * ROPE)
        return jnp.broadcast_to(both, (groups, micro, rows, 2 * ROPE)).reshape(total, 2 * ROPE)

    first = dot(after(act, gate_rows), w_first)
    q_nope = first[:, :NOPE].astype(bf16)
    latent_raw = first[:, NOPE : NOPE + LATENT]
    latent = normed(latent_raw, gain_kv).astype(bf16)
    at = NOPE + LATENT
    roped = (
        first[:, at : at + 2 * ROPE] * table_of(cosine) + first[:, at + 2 * ROPE :] * table_of(sine)
    ).astype(bf16)
    kvup = dot(latent, wkvup_me).astype(bf16)

    def owners(x):
        return x.reshape(groups, micro, rows, x.shape[-1])

    segs = segments[:, 0]
    head = (owners(q_nope), owners(roped), owners(kvup), segs)
    attn, lse = attend(*head)
    attn_own = swap(attn.reshape(groups, own, VDIM))
    attn_own = attn_own.swapaxes(0, 1).reshape(own, groups * VDIM)
    x1 = x_own.astype(f32) + dot_pieces(attn_own, wout)
    hid_own = normed(x1, gain_ffn).astype(bf16)
    hid_all = spread(own_first(hid_own, 1))
    attn_all = spread(after(attn_own, hid_all))

    size = width // parts
    arrived = dispatch(hid_all).astype(bf16)
    dyexp = (gate_slots * dispatch(dy_all)).astype(bf16)
    wei = jnp.concatenate([w_expert_in[0]] + wei_others, 0)
    weo = lay_out(w_expert_out[0], weo_others)
    epre = dot(arrived, wei)
    eact = swiglu(epre).astype(bf16)
    gated = (gate_slots * dot(eact, weo)).astype(bf16)
    returned = swap(gated.reshape(groups, micro * capacity, width))
    deact = dot_nt(after(dyexp, gated), weo)
    depre = swiglu_back(epre, deact).astype(bf16)
    dhid_rows = dot_nt(depre, wei).astype(bf16)

    spre = dot_nt(hid_all, wsi_me)
    sact = swiglu(spre).astype(bf16)
    dsact = dot_nt(dy_all, wso_me)
    dspre = swiglu_back(spre, dsact).astype(bf16)
    dhid_part = put_back(place, dhid_rows, dspre, *wsi_blocks)
    dhid_sum = collect(dhid_part)

    arrived, depre, eact, dyexp, dspre, sact = lax.optimization_barrier(
        (arrived, depre, eact, dyexp, dspre, sact, dhid_part)
    )[:6]
    g_si = dot_tn(dspre, hid_all)
    g_so = dot_tn(sact, dy_all)

    def shared_grads(r):
        rows_of = block_of(g_so, part + r)
        return jnp.concatenate(
            [g_si[:, r * size : (r + 1) * size]] + jnp.split(rows_of, parts, 1), 0
        )

    g_shared = exchanged(shared_grads(0), lambda r: shared_grads(r).astype(bf16))
    g_shared = stack(after(g_shared.astype(bf16), dhid_sum))

    def expert_in_grad(r):
        return dot_tn(arrived[:, r * size : (r + 1) * size], depre)

    def expert_out_grad(r):
        short = eact.shape[1] // parts
        some = lax.dynamic_slice_in_dim(eact, ((part + r) % parts) * short, short, 1)
        return dot_tn(some, dyexp)

    sent_in = [expert_in_grad(r).astype(bf16) for r in range(1, parts)]
    sent_out = [expert_out_grad(r).astype(bf16) for r in range(1, parts)]
    hidden = swap(after(sact, returned).reshape(groups, own, -1))
    dhid_sum = after(dhid_sum, returned, hidden, *sent_in, *sent_out)
    got_in = [send(x, r).astype(f32) for r, x in enumerate(sent_in, 1)]
    got_out = [send(x, r).astype(f32) for r, x in enumerate(sent_out, 1)]
    dhid = natural(dhid_sum, 1).astype(f32)

    dy = dy_own.astype(f32)
    dx1_norm, g_ffn_gain = normed_back(x1, gain_ffn, dhid)
    dx1 = dy + dx1_norm
    dx1_low = dx1.astype(bf16)
    dattn_own = dot_pieces_t(dx1_low, wout).astype(bf16)
    dattn = swap(dattn_own.reshape(own, groups, VDIM).swapaxes(0, 1))
    dao = after(dx1_low, dattn).reshape(own, groups, width // groups).swapaxes(0, 1)
    dao = swap(dao)
    dattn = dattn.reshape(groups, micro, rows, VDIM)
    back = attend_back(*head, lse, dattn, cosine, sine)
    moved = swap(back.reshape(groups, own, 512))

    def back_of(x, first_column, last_column):
        piece = x[..., first_column:last_column]
        return piece.swapaxes(0, 1).reshape(own, groups * (last_column - first_column))

    flat = back.reshape(total, 512)
    g_query = dot_tn(act, flat[:, :qk])
    g_kvup = dot_tn(latent, flat[:, 256:])
    g_out = dot_tn(attn_all, dao.reshape(total, width // groups))

    def fold(x):
        steps = size // 128
        runs = size // x.shape[0]
        x = x.reshape(steps, x.shape[0] // steps, runs, x.shape[1] // runs)
        return x.swapaxes(1, 2).reshape(size, -1)

    def attn_grads(r):
        return jnp.concatenate(
            [
                block_of(g_out, part + r),
                g_query[r * size : (r + 1) * size],
                fold(block_of(g_kvup, part + r)),
            ],
            1,
        )

    g_attn = exchanged(attn_grads(0), lambda r: attn_grads(r).astype(bf16))

    returned, hidden = lax.optimization_barrier((returned, hidden, moved))[:2]
    hidden = hidden.reshape(groups, own, parts, run).transpose(1, 2, 0, 3).reshape(own, ff)
    hit_own = routes_own.reshape(micro, rows, 1, top) == expert_ids[:, None]
    hit_own = jnp.any(hit_own, -1)
    slot_own = jnp.cumsum(hit_own.astype(jnp.int32), 1) - 1
    slots = jnp.arange(capacity, dtype=jnp.int32)
    find = ((slot_own[..., None] == slots) & hit_own[..., None]).astype(bf16)
    routed = jnp.einsum(
        "mtk,mkd->mtd",
        find.reshape(micro, rows, groups * capacity),
        returned.reshape(groups, micro, capacity, width)
        .swapaxes(0, 1)
        .reshape(micro, groups * capacity, width),
        preferred_element_type=f32,
    ).reshape(own, width)
    out_sum = routed + dot_pieces(hidden, wso)

    dq_own = back_of(moved, 0, qk)
    dkvup_own = back_of(moved, 256, 512)
    dkrope_own = jnp.sum(moved[..., qk:256].astype(f32), 0)
    dlatent = dot_pieces_t(dkvup_own, wkvup)
    latent_own = lax.dynamic_slice_in_dim(latent_raw, me * own, own, 0)
    cos_own = jnp.tile(lax.dynamic_slice_in_dim(cosine, me * rows, rows, 0), (micro, 1))
    sin_own = jnp.tile(lax.dynamic_slice_in_dim(sine, me * rows, rows, 0), (micro, 1))
    dlatent_raw, g_kv_gain = normed_back(latent_own, gain_kv, dlatent)
    dkvfull = jnp.concatenate([dlatent_raw, rotate_back(dkrope_own, cos_own, sin_own)], -1)
    dkvfull = dkvfull.astype(bf16)
    down = LATENT + ROPE
    early = jnp.concatenate([g_kv_gain, g_ffn_gain])
    short = early.shape[0]
    early = jnp.pad(early, (0, 16 * down - short)).reshape(16, down)
    dkv_all = spread(jnp.concatenate([dkvfull, early.astype(bf16)], 0))
    dkv_all = dkv_all.reshape(groups, own + 16, down)
    early = jnp.sum(dkv_all[:, own:].astype(f32), 0).reshape(-1)[:short]
    dkv_all = dkv_all[:, :own].reshape(total, down)
    dact = dot_pieces_t(dq_own, wq) + natural(dot_nt(dkvfull, w_down), 1)
    dx_norm, g_attn_gain = normed_back(x_own.astype(f32), gain_attn, dact)
    input_grad = dx1 + dx_norm

    height = size // groups
    act_rows = jnp.concatenate(
        [
            lax.dynamic_slice_in_dim(act, c * size + me * height, height, 1)
            for c in range(parts)
        ],
        1,
    )
    g_down = dot_tn(act_rows, dkv_all)
    g_down = exchanged(
        g_down[:height], lambda r: g_down[r * height : (r + 1) * height].astype(bf16)
    ).astype(bf16)
    early_kv, early_ffn = early[:LATENT], early[LATENT:]

    def early_gains(r):
        return jnp.concatenate([block_of(early_kv, part + r), block_of(early_ffn, part + r)])

    early = exchanged(early_gains(0), early_gains)
    late = exchanged(block_of(g_attn_gain, part), lambda r: block_of(g_attn_gain, part + r))
    count = g_attn.shape[1]
    tail = g_down[:, count:]
    tail = jnp.concatenate([tail[: height // 2], tail[height // 2 :]], 1)
    extra = jnp.concatenate([g_down[:, :count], tail], 0)
    at_late = size + extra.shape[0]
    late_rows = -(-size // count)
    late = jnp.pad(late, (0, late_rows * count - size)).reshape(late_rows, count)
    extra = jnp.concatenate([extra, late.astype(bf16)], 0)
    extra = jnp.pad(extra, ((0, 128 - extra.shape[0]), (0, 0)))
    g_attn = jnp.concatenate([g_attn.astype(bf16), extra], 0)
    g_attn = stack(row_major(g_attn))
    late = jnp.sum(g_attn[:, at_late : at_late + late_rows].astype(f32), 0).reshape(-1)[:size]
    gains = (late, early[: LATENT // parts], early[LATENT // parts :])

    mixed = (x1 + out_sum).astype(bf16)
    g_ein = sum(got_in, expert_in_grad(0))
    g_eout = sum(got_out, expert_out_grad(0))
    out_grad, query_grad, kvup_grad, g_down = attn_rows(
        g_attn, size, width // groups, qk, LATENT // parts, height
    )
    shared_in_grad, shared_out_grad = shared_rows(g_shared, 2 * parts, run)
    return (
        mixed.reshape(micro, 1, rows, width),
        input_grad.reshape(micro, 1, rows, width),
        gains[0],
        query_grad,
        g_down.T,
        gains[1],
        kvup_grad,
        out_grad,
        gains[2],
        shared_in_grad,
        shared_out_grad,
        g_ein[None],
        g_eout[None],
    )


def solution(mesh):
    tok = P(None, "dp", "expert", None)
    row = P("dp", None)
    exp = P("expert", "dp", None)
    in_specs = (
        tok, tok, P(None, "dp", None), tok, tok,
        P("dp"), row, row, P("dp"), row, row, P("dp"), row, row, exp, exp,
    )
    out_specs = (
        tok, tok, P("dp"), row, row, P("dp"), row, row, P("dp"), row, row, exp, exp,
    )

    return jax.shard_map(
        per_device, mesh=mesh, in_specs=in_specs, out_specs=out_specs, check_vma=False
    )
```

```python
import functools

import jax
import jax.numpy as jnp
from jax import lax
from jax.experimental import pallas as pl
from jax.experimental.layout import Layout, with_layout_constraint
from jax.experimental.pallas import tpu as pltpu
from jax.sharding import PartitionSpec as P

HEADS = 16
NOPE = 128
ROPE = 64
VDIM = 128
LATENT = 512
DOC_MAX = 512


theta_base = 50000.0
eps_norm = 1e-06
bf16 = jnp.bfloat16
f32 = jnp.float32


def rope_tables(length, width):
    half = width // 2
    freq = theta_base ** (-2.0 * jnp.arange(half, dtype=f32) / width)
    angle = jnp.arange(length, dtype=f32)[:, None] * freq[None, :]
    cosine = jnp.concatenate([jnp.cos(angle), jnp.cos(angle)], -1)
    sine = jnp.concatenate([jnp.sin(angle), jnp.sin(angle)], -1)
    return (cosine, sine)


def rotate_back(value, cosine, sine):
    half = value.shape[-1] // 2
    scaled = value * sine
    turned = jnp.concatenate([scaled[..., half:], -scaled[..., :half]], -1)
    return value * cosine + turned


def normed(value, gain):
    return (
        value
        * lax.rsqrt(jnp.mean(value * value, -1, keepdims=True) + eps_norm)
        * gain.astype(f32)
    )


def normed_back(value, gain, grad):
    inv = lax.rsqrt(jnp.mean(value * value, -1, keepdims=True) + eps_norm)
    hat = value * inv
    scaled = grad * gain.astype(f32)
    inner = jnp.mean(scaled * hat, -1, keepdims=True)
    return inv * (scaled - hat * inner), jnp.sum(grad * hat, 0)


def swiglu_parts(packed):
    half = packed.shape[-1] // 2
    return packed[..., :half], packed[..., half:]


def swiglu(packed):
    gate, up = swiglu_parts(packed)
    return gate * jax.nn.sigmoid(gate) * up


def swiglu_back(packed, grad):
    gate, up = swiglu_parts(packed)
    sig = jax.nn.sigmoid(gate)
    d_gate = grad * up * sig * (1.0 + gate * (1.0 - sig))
    d_up = grad * gate * sig
    return jnp.concatenate([d_gate, d_up], -1)


def dot(left, right):
    return jnp.dot(left, right, preferred_element_type=f32)


def dot_tn(left, right):
    return lax.dot_general(left, right, (((0,), (0,)), ((), ())), preferred_element_type=f32)


def dot_nt(left, right):
    return lax.dot_general(left, right, (((1,), (1,)), ((), ())), preferred_element_type=f32)


def row_major(x):
    return with_layout_constraint(x, Layout(major_to_minor=tuple(range(x.ndim))))


def after(value, *first):
    return lax.optimization_barrier((value,) + first)[0]


def block_of_keys(refs, start, stop, low):
    qn_ref, rope_ref, kv_ref, seg_col, seg_row = refs
    rows = qn_ref.shape[2]

    def take(ref, first, last):
        return ref[first // rows : last // rows, 0].reshape(last - first, ref.shape[3])

    query = jnp.concatenate([take(qn_ref, start, stop), take(rope_ref, start, stop)[:, :ROPE]], 1)
    kv = take(kv_ref, low, stop)
    key = jnp.concatenate([kv[:, :NOPE], take(rope_ref, low, stop)[:, ROPE:]], 1)
    value = kv[:, NOPE:]
    score = dot_nt(query, key) * ((NOPE + ROPE) ** (-0.5))
    size = (stop - start, stop - low)
    q_at = lax.broadcasted_iota(jnp.int32, size, 0) + (start - low)
    k_at = lax.broadcasted_iota(jnp.int32, size, 1)
    allowed = (seg_col[0, start:stop] == seg_row[0, :, low:stop]) & (k_at <= q_at)
    return query, key, value, jnp.where(allowed, score, -1e30)


def query_blocks(seq, rows, size=256):
    for start in range(0, seq, size):
        low = max(0, start - DOC_MAX + 1) // rows * rows
        yield start, start + size, low


def attend_kernel(qn_ref, rope_ref, kv_ref, seg_col, seg_row, out_ref, lse_ref):
    owners, _, rows, _ = qn_ref.shape
    refs = (qn_ref, rope_ref, kv_ref, seg_col, seg_row)
    for start, stop, low in query_blocks(owners * rows, rows):
        _, _, value, score = block_of_keys(refs, start, stop, low)
        top = jnp.max(score, -1, keepdims=True)
        expo = jnp.exp(score - top)
        total = jnp.sum(expo, -1, keepdims=True)
        out = dot((expo / total).astype(bf16), value).astype(bf16)
        at = slice(start // rows, stop // rows)
        out_ref[at, 0] = out.reshape((stop - start) // rows, rows, VDIM)
        lse_ref[0, start:stop] = top + jnp.log(total)


def attend_back_kernel(
    qn_ref, rope_ref, kv_ref, seg_col, seg_row, lse_ref, dout_ref, cos_ref, sin_ref, back_ref, acc
):
    owners, _, rows, _ = qn_ref.shape
    seq = owners * rows
    refs = (qn_ref, rope_ref, kv_ref, seg_col, seg_row)
    acc[...] = jnp.zeros_like(acc)
    for start, stop, low in query_blocks(seq, rows):
        at = slice(start // rows, stop // rows)
        query, key, value, score = block_of_keys(refs, start, stop, low)
        prob = jnp.exp(score - lse_ref[0, start:stop])
        dout = dout_ref[at, 0].reshape(stop - start, VDIM)
        dprob = dot_nt(dout, value)
        delta = jnp.sum(prob * dprob, -1, keepdims=True)
        dscore = (prob * (dprob - delta) * ((NOPE + ROPE) ** (-0.5))).astype(bf16)
        dquery = dot(dscore, key)
        acc[low:stop, : NOPE + ROPE] += dot_tn(dscore, query)
        acc[low:stop, 256:] += dot_tn(prob.astype(bf16), dout)
        rope = rotate_back(dquery[:, NOPE:], cos_ref[start:stop], sin_ref[start:stop])
        whole = jnp.concatenate([dquery[:, :NOPE], rope, rope, dquery, rope], 1)
        back_ref[at, 0] = whole.astype(bf16).reshape((stop - start) // rows, rows, 512)
    dkey = acc[...]
    tail = jnp.concatenate([dkey[:, NOPE : NOPE + ROPE], dkey[:, :NOPE], dkey[:, 256:]], 1)
    back_ref[:, 0, :, NOPE + ROPE :] = tail.astype(bf16).reshape(owners, rows, 320)


def attend(q_nope, roped, kvup, segs):
    owners, micro, rows, _ = q_nope.shape
    seq = owners * rows
    spec = lambda c: pl.BlockSpec((owners, 1, rows, c), lambda m: (0, m, 0, 0))
    return pl.pallas_call(
        attend_kernel,
        out_shape=(
            jax.ShapeDtypeStruct((owners, micro, rows, VDIM), bf16),
            jax.ShapeDtypeStruct((micro, seq, 1), f32),
        ),
        grid=(micro,),
        in_specs=[
            spec(NOPE),
            spec(2 * ROPE),
            spec(2 * NOPE),
            pl.BlockSpec((1, seq, 1), lambda m: (m, 0, 0)),
            pl.BlockSpec((1, 1, seq), lambda m: (m, 0, 0)),
        ],
        out_specs=(spec(VDIM), pl.BlockSpec((1, seq, 1), lambda m: (m, 0, 0))),
        cost_estimate=pl.CostEstimate(
            flops=2 * micro * seq * 640 * 320,
            transcendentals=micro * seq * 640,
            bytes_accessed=micro * seq * 1400,
        ),
    )(q_nope, roped, kvup, segs[:, :, None], segs[:, None, :])


def attend_back(q_nope, roped, kvup, segs, lse, dout, cosine, sine):
    owners, micro, rows, _ = q_nope.shape
    seq = owners * rows
    spec = lambda c: pl.BlockSpec((owners, 1, rows, c), lambda m: (0, m, 0, 0))
    flat = pl.BlockSpec((seq, ROPE), lambda m: (0, 0))
    return pl.pallas_call(
        attend_back_kernel,
        out_shape=jax.ShapeDtypeStruct((owners, micro, rows, 512), bf16),
        grid=(micro,),
        in_specs=[
            spec(NOPE),
            spec(2 * ROPE),
            spec(2 * NOPE),
            pl.BlockSpec((1, seq, 1), lambda m: (m, 0, 0)),
            pl.BlockSpec((1, 1, seq), lambda m: (m, 0, 0)),
            pl.BlockSpec((1, seq, 1), lambda m: (m, 0, 0)),
            spec(VDIM),
            flat,
            flat,
        ],
        out_specs=spec(512),
        scratch_shapes=[pltpu.VMEM((seq, 384), f32)],
        cost_estimate=pl.CostEstimate(
            flops=2 * micro * seq * 640 * 832,
            transcendentals=micro * seq * 640,
            bytes_accessed=micro * seq * 2600,
        ),
    )(q_nope, roped, kvup, segs[:, :, None], segs[:, None, :], lse, dout, cosine, sine)


def put_back_kernel(place_ref, rows_ref, units_ref, *refs):
    *weight_refs, out_ref = refs
    left = jnp.concatenate([place_ref[0], units_ref[...]], 1)
    weight = jnp.concatenate([w[...] for w in weight_refs], 1)
    right = jnp.concatenate([rows_ref[...], weight], 0)
    out_ref[...] = dot(left, right).astype(bf16)


def put_back(place, rows, units, *weights):
    many, size, height = place.shape
    total, count = units.shape
    width = rows.shape[1]
    return pl.pallas_call(
        put_back_kernel,
        out_shape=jax.ShapeDtypeStruct((total, width), bf16),
        grid=(many,),
        in_specs=[
            pl.BlockSpec((1, size, height), lambda i: (i, 0, 0)),
            pl.BlockSpec((height, width), lambda i: (i, 0)),
            pl.BlockSpec((size, count), lambda i: (i, 0)),
            *(pl.BlockSpec(w.shape, lambda i: (0, 0)) for w in weights),
        ],
        out_specs=pl.BlockSpec((size, width), lambda i: (i, 0)),
        cost_estimate=pl.CostEstimate(
            flops=2 * total * width * (height + count),
            transcendentals=0,
            bytes_accessed=2 * (total * width + rows.size + units.size + count * width),
        ),
    )(place, rows, units, *weights)


def shared_in_kernel(x_ref, out_ref, *, runs, piece):
    groups = x_ref.shape[0]
    turned = [x_ref[e].astype(f32).T for e in range(groups)]
    length = groups * piece
    parts = []
    for c in range(runs):
        parts += [t[:, c * piece : (c + 1) * piece] for t in turned]
        if length % 128 == 0:
            out_ref[:, c * length : (c + 1) * length] = jnp.concatenate(parts, 1)
            parts = []
    if parts:
        out_ref[...] = jnp.concatenate(parts, 1)


def shared_out_kernel(x_ref, out_ref, *, piece):
    rows = x_ref[0].astype(f32)
    count = rows.shape[0] // piece
    out_ref[0] = jnp.concatenate([rows[c * piece : (c + 1) * piece] for c in range(count)], 1)


def shared_rows(stacked, runs, piece):
    groups, count, size = stacked.shape
    first = runs * piece
    rest = count - first
    step = 128
    in_grad = pl.pallas_call(
        functools.partial(shared_in_kernel, runs=runs, piece=piece),
        out_shape=jax.ShapeDtypeStruct((size, groups * first), f32),
        grid=(size // step,),
        in_specs=[pl.BlockSpec((groups, first, step), lambda i: (0, 0, i))],
        out_specs=pl.BlockSpec((step, groups * first), lambda i: (i, 0)),
        cost_estimate=pl.CostEstimate(
            flops=0, transcendentals=0, bytes_accessed=6 * groups * first * size
        ),
    )(stacked)
    out_grad = pl.pallas_call(
        functools.partial(shared_out_kernel, piece=piece),
        out_shape=jax.ShapeDtypeStruct((groups, piece, rest // piece * size), f32),
        grid=(groups,),
        in_specs=[pl.BlockSpec((1, rest, size), lambda e: (e, first // rest, 0))],
        out_specs=pl.BlockSpec((1, piece, rest // piece * size), lambda e: (e, 0, 0)),
        cost_estimate=pl.CostEstimate(
            flops=0, transcendentals=0, bytes_accessed=6 * groups * rest * size
        ),
    )(stacked)
    return in_grad, out_grad.reshape(groups * piece, -1)


def attn_rows_kernel(x_ref, extra_ref, out_ref, query_ref, kvup_ref, down_ref, *, a, b, height):
    groups, _, count = x_ref.shape
    rest = count - a - b
    runs = x_ref.shape[1] // kvup_ref.shape[0]
    step = kvup_ref.shape[0]
    for e in range(0, groups, 2):
        one, two = x_ref[e].astype(f32), x_ref[e + 1].astype(f32)
        out_ref[:, e * a : (e + 2) * a] = jnp.concatenate([one[:, :a], two[:, :a]], 1)
        query_ref[:, e * b : (e + 2) * b] = jnp.concatenate(
            [one[:, a : a + b], two[:, a : a + b]], 1
        )
        pieces = [
            x[c * step : (c + 1) * step, a + b :] for x in (one, two) for c in range(runs)
        ]
        kvup_ref[:, e * runs * rest : (e + 2) * runs * rest] = jnp.concatenate(pieces, 1)
    half = count // 2
    rows = []
    for e in range(extra_ref.shape[0]):
        x = extra_ref[e].astype(f32)
        tail = x[height : height + height // 2]
        tail = jnp.concatenate([tail[:, :half], tail[:, half:]], 0)
        rows.append(jnp.concatenate([x[:height], tail], 1))
    down_ref[...] = jnp.concatenate(rows, 0).T


def attn_rows(stacked, rows, a, b, kvup_height, down_height):
    groups, _, count = stacked.shape
    size = 128
    steps = rows // size
    kvup_width = (count - a - b) * rows // kvup_height
    return pl.pallas_call(
        functools.partial(attn_rows_kernel, a=a, b=b, height=down_height),
        out_shape=(
            jax.ShapeDtypeStruct((rows, groups * a), f32),
            jax.ShapeDtypeStruct((rows, groups * b), f32),
            jax.ShapeDtypeStruct((kvup_height, groups * kvup_width), f32),
            jax.ShapeDtypeStruct((count * 3 // 2, groups * down_height), f32),
        ),
        grid=(steps,),
        in_specs=[
            pl.BlockSpec((groups, size, count), lambda i: (0, i, 0)),
            pl.BlockSpec((groups // steps, size, count), lambda i: (i, steps, 0)),
        ],
        out_specs=(
            pl.BlockSpec((size, groups * a), lambda i: (i, 0)),
            pl.BlockSpec((size, groups * b), lambda i: (i, 0)),
            pl.BlockSpec((kvup_height // steps, groups * kvup_width), lambda i: (i, 0)),
            pl.BlockSpec((count * 3 // 2, groups // steps * down_height), lambda i: (0, i)),
        ),
        cost_estimate=pl.CostEstimate(
            flops=0, transcendentals=0, bytes_accessed=6 * stacked.size
        ),
    )(stacked, stacked)


def per_device(
    tokens,
    grad_out,
    segments,
    routes,
    gates,
    attn_gain,
    w_query,
    w_kv_down,
    kv_gain,
    w_kv_up,
    w_out,
    ffn_gain,
    w_shared_in,
    w_shared_out,
    w_expert_in,
    w_expert_out,
):
    micro, _, rows, width = tokens.shape
    groups = lax.axis_size("expert")
    parts = lax.axis_size("dp")
    me = lax.axis_index("expert")
    part = lax.axis_index("dp")
    own = micro * rows
    total = groups * own
    seq = rows * groups
    top = routes.shape[3]
    capacity = max(2, rows * top * 4 // (3 * groups))
    qk = NOPE + ROPE
    assert HEADS == groups

    def shift(x, step):
        return lax.ppermute(x, "dp", [((i + step) % parts, i) for i in range(parts)])

    def send(x, step):
        return lax.ppermute(x, "dp", [(i, (i + step) % parts) for i in range(parts)])

    def others(x):
        return [shift(x, r) for r in range(1, parts)]

    def turn(x, axis, amount):
        size = x.shape[axis]
        return lax.dynamic_slice_in_dim(
            jnp.concatenate([x, x], axis), amount * (size // parts), size, axis
        )

    def own_first(x, axis):
        return turn(x, axis, part)

    def natural(x, axis):
        return turn(x, axis, (parts - part) % parts)

    def lay_out(x, rest):
        size = x.shape[0]
        whole = jnp.zeros((parts * size,) + x.shape[1:], x.dtype)
        for r, piece in enumerate([x] + rest):
            at = ((part + r) % parts) * size
            whole = lax.dynamic_update_slice_in_dim(whole, piece, at, 0)
        return whole

    def block_of(full, index):
        size = full.shape[0] // parts
        return lax.dynamic_slice_in_dim(full, (index % parts) * size, size, 0)

    def exchanged(own_block, block_for):
        result = own_block.astype(f32)
        for r in range(1, parts):
            result = result + send(block_for(r), r).astype(f32)
        return result

    pairs = [(i, i ^ 1) for i in range(groups)]
    odd = me % 2

    def pieces(x, *first):
        size = x.shape[0]
        found = [(x, part * size)]
        if parts == 2:
            half = size // 2
            asked = lax.dynamic_slice_in_dim(x, odd * half, half, 0)
            if first:
                asked = after(asked, *first)
            got = shift(asked, 1)
            swapped = lax.ppermute(got, "expert", pairs)
            base = (1 - part) * size
            found += [(got, base + odd * half), (swapped, base + (1 - odd) * half)]
        else:
            asked = after(x, *first) if first else x
            found += [(y, ((part + r) % parts) * size) for r, y in enumerate(others(asked), 1)]
        return found

    def dot_pieces(x, blocks):
        return sum(
            dot(lax.dynamic_slice_in_dim(x, at, w.shape[0], 1), w) for w, at in blocks
        )

    def dot_pieces_t(x, blocks):
        whole = jnp.zeros((x.shape[0], sum(w.shape[0] for w, _ in blocks)), f32)
        for w, at in blocks:
            whole = lax.dynamic_update_slice_in_dim(whole, dot_nt(x, w), at, 1)
        return whole

    def spread(x):
        return lax.all_gather(x, "expert", axis=0, tiled=True)

    def stack(x):
        return lax.all_gather(x, "expert", axis=0, tiled=False)

    def swap(x):
        return lax.all_to_all(x, "expert", split_axis=0, concat_axis=0, tiled=True)

    def collect(x):
        return lax.psum_scatter(x, "expert", scatter_dimension=0, tiled=True)

    gain_sizes = (width // parts, LATENT // parts, width // parts)
    cuts = (gain_sizes[0], gain_sizes[0] + gain_sizes[1])
    own_gains = jnp.concatenate([attn_gain, kv_gain, ffn_gain])
    gain_rows = jnp.split(lay_out(own_gains[None], [y[None] for y in others(own_gains)]), cuts, 1)
    gain_attn, gain_kv, gain_ffn = (rows_of.reshape(-1) for rows_of in gain_rows)

    wq_own = lax.dynamic_slice_in_dim(w_query, me * qk, qk, 1)
    wq_me = jnp.concatenate([wq_own] + others(wq_own), 0)
    down_pieces = pieces(w_kv_down)
    w_down = jnp.zeros((width, LATENT + ROPE), bf16)
    for w, start in down_pieces:
        start = (start - part * (width // parts)) % width
        w_down = lax.dynamic_update_slice_in_dim(w_down, w, start, 0)
    wkvup_own = lax.dynamic_slice_in_dim(w_kv_up, me * 2 * NOPE, 2 * NOPE, 1)
    wkvup_me = lay_out(wkvup_own, others(wkvup_own))
    wout = pieces(w_out)

    def turned(w):
        return jnp.concatenate([-w[:, ROPE // 2 :], w[:, : ROPE // 2]], 1)

    rope_q, rope_k = wq_me[:, NOPE:], w_down[:, LATENT:]
    w_first = jnp.concatenate(
        [
            wq_me[:, :NOPE],
            w_down[:, :LATENT],
            rope_q,
            rope_k,
            turned(rope_q),
            turned(rope_k),
        ],
        1,
    )

    x_own = tokens[:, 0].reshape(own, width)
    dy_own = grad_out[:, 0].reshape(own, width)
    act_own = normed(x_own.astype(f32), gain_attn).astype(bf16)
    act = spread(own_first(act_own, 1))
    dy_all = spread(after(dy_own, act))

    expert_ids = jnp.arange(groups, dtype=jnp.int32)
    routes_own = routes[:, 0].reshape(own, top)
    gates_own = gates[:, 0].reshape(own, top)
    table = jnp.sum(
        jnp.where(routes_own[None] == expert_ids[:, None, None], gates_own[None], 0.0), -1
    )
    gate_rows = swap(table).reshape(groups * micro, rows)
    hit = gate_rows > 0.0
    slot = jnp.cumsum(hit.astype(jnp.int32), 1) - 1
    pick = (slot[:, None, :] == jnp.arange(capacity, dtype=jnp.int32)[None, :, None]) & hit[
        :, None, :
    ]
    gate_slots = jnp.sum(jnp.where(pick, gate_rows[:, None, :], 0.0), -1).reshape(-1, 1)
    pick = pick.astype(bf16)
    together = 4
    place = pick.swapaxes(1, 2).reshape(-1, together, rows, 1, capacity)
    place = place * jnp.eye(together, dtype=bf16)[None, :, None, :, None]
    place = place.reshape(-1, together * rows, together * capacity)

    def dispatch(x):
        picked = jnp.einsum(
            "bst,btd->bsd",
            pick,
            x.reshape(groups * micro, rows, width),
            preferred_element_type=f32,
        )
        return picked.reshape(groups * micro * capacity, width)

    ff = w_shared_in.shape[1] // 2
    run = ff // (parts * groups)
    wsi_own = jnp.concatenate(
        [
            lax.dynamic_slice_in_dim(w_shared_in, c * (ff // parts) + me * run, run, 1).T
            for c in range(2 * parts)
        ],
        0,
    )
    wso_own = lax.dynamic_slice_in_dim(w_shared_out, me * run, run, 0)
    wsi_blocks = [wsi_own] + others(wsi_own)
    wsi_me = jnp.concatenate(wsi_blocks, 1)
    wso_me = lay_out(wso_own, others(wso_own))
    wei_others = others(w_expert_in[0])
    weo_others = others(w_expert_out[0])
    wq = pieces(w_query, wei_others[0], weo_others[0])
    wkvup = pieces(w_kv_up, wei_others[0], weo_others[0])
    wso = pieces(w_shared_out, wei_others[0], weo_others[0])

    cosine, sine = rope_tables(seq, ROPE)

    def table_of(values):
        both = jnp.concatenate([values, values], 1).reshape(groups, 1, rows, 2 * ROPE)
        return jnp.broadcast_to(both, (groups, micro, rows, 2 * ROPE)).reshape(total, 2 * ROPE)

    first = dot(after(act, gate_rows), w_first)
    q_nope = first[:, :NOPE].astype(bf16)
    latent_raw = first[:, NOPE : NOPE + LATENT]
    latent = normed(latent_raw, gain_kv).astype(bf16)
    at = NOPE + LATENT
    roped = (
        first[:, at : at + 2 * ROPE] * table_of(cosine) + first[:, at + 2 * ROPE :] * table_of(sine)
    ).astype(bf16)
    kvup = dot(latent, wkvup_me).astype(bf16)

    def owners(x):
        return x.reshape(groups, micro, rows, x.shape[-1])

    segs = segments[:, 0]
    head = (owners(q_nope), owners(roped), owners(kvup), segs)
    attn, lse = attend(*head)
    attn_own = swap(attn.reshape(groups, own, VDIM))
    attn_own = attn_own.swapaxes(0, 1).reshape(own, groups * VDIM)
    x1 = x_own.astype(f32) + dot_pieces(attn_own, wout)
    hid_own = normed(x1, gain_ffn).astype(bf16)
    hid_all = spread(own_first(hid_own, 1))
    attn_all = spread(after(attn_own, hid_all))

    size = width // parts
    arrived = dispatch(hid_all).astype(bf16)
    dyexp = (gate_slots * dispatch(dy_all)).astype(bf16)
    wei = jnp.concatenate([w_expert_in[0]] + wei_others, 0)
    weo = lay_out(w_expert_out[0], weo_others)
    epre = dot(arrived, wei)
    eact = swiglu(epre).astype(bf16)
    deact = dot_nt(dyexp, weo)
    depre = swiglu_back(epre, deact).astype(bf16)
    dhid_rows = dot_nt(depre, wei).astype(bf16)

    spre = dot_nt(hid_all, wsi_me)
    sact = swiglu(spre).astype(bf16)
    dsact = dot_nt(dy_all, wso_me)
    dspre = swiglu_back(spre, dsact).astype(bf16)
    dhid_part = put_back(place, dhid_rows, dspre, *wsi_blocks)
    dhid_sum = collect(dhid_part)

    arrived, depre, eact, dyexp, dspre, sact = lax.optimization_barrier(
        (arrived, depre, eact, dyexp, dspre, sact, dhid_part)
    )[:6]
    hidden = swap(sact.reshape(groups, own, -1))
    gated = (gate_slots * dot(eact, weo)).astype(bf16)
    returned = swap(after(gated, hidden).reshape(groups, micro * capacity, width))
    dspre, sact = lax.optimization_barrier((dspre, sact, gated))[:2]
    g_si = dot_tn(dspre, hid_all)
    g_so = dot_tn(sact, dy_all)

    def shared_grads(r):
        rows_of = block_of(g_so, part + r)
        return jnp.concatenate(
            [g_si[:, r * size : (r + 1) * size]] + jnp.split(rows_of, parts, 1), 0
        )

    g_shared = exchanged(shared_grads(0), lambda r: shared_grads(r).astype(bf16))
    g_shared = stack(after(g_shared.astype(bf16), dhid_sum))

    def expert_in_grad(r):
        return dot_tn(arrived[:, r * size : (r + 1) * size], depre)

    def expert_out_grad(r):
        short = eact.shape[1] // parts
        some = lax.dynamic_slice_in_dim(eact, ((part + r) % parts) * short, short, 1)
        return dot_tn(some, dyexp)

    sent_in = [expert_in_grad(r).astype(bf16) for r in range(1, parts)]
    sent_out = [expert_out_grad(r).astype(bf16) for r in range(1, parts)]
    dhid_sum = after(dhid_sum, returned, hidden, *sent_in, *sent_out)
    got_in = [send(x, r).astype(f32) for r, x in enumerate(sent_in, 1)]
    got_out = [send(x, r).astype(f32) for r, x in enumerate(sent_out, 1)]
    dhid = natural(dhid_sum, 1).astype(f32)

    dy = dy_own.astype(f32)
    dx1_norm, g_ffn_gain = normed_back(x1, gain_ffn, dhid)
    dx1 = dy + dx1_norm
    dx1_low = dx1.astype(bf16)
    dattn_own = dot_pieces_t(dx1_low, wout).astype(bf16)
    dattn = swap(dattn_own.reshape(own, groups, VDIM).swapaxes(0, 1))
    dao = after(dx1_low, dattn).reshape(own, groups, width // groups).swapaxes(0, 1)
    dao = swap(dao)
    dattn = dattn.reshape(groups, micro, rows, VDIM)
    back = attend_back(*head, lse, dattn, cosine, sine)
    moved = swap(back.reshape(groups, own, 512))

    def back_of(x, first_column, last_column):
        piece = x[..., first_column:last_column]
        return piece.swapaxes(0, 1).reshape(own, groups * (last_column - first_column))

    flat = back.reshape(total, 512)
    g_query = dot_tn(act, flat[:, :qk])
    g_kvup = dot_tn(latent, flat[:, 256:])
    g_out = dot_tn(attn_all, dao.reshape(total, width // groups))

    def fold(x):
        steps = size // 128
        runs = size // x.shape[0]
        x = x.reshape(steps, x.shape[0] // steps, runs, x.shape[1] // runs)
        return x.swapaxes(1, 2).reshape(size, -1)

    def attn_grads(r):
        return jnp.concatenate(
            [
                block_of(g_out, part + r),
                g_query[r * size : (r + 1) * size],
                fold(block_of(g_kvup, part + r)),
            ],
            1,
        )

    g_attn = exchanged(attn_grads(0), lambda r: attn_grads(r).astype(bf16))

    returned, hidden = lax.optimization_barrier((returned, hidden, moved))[:2]
    hidden = hidden.reshape(groups, own, parts, run).transpose(1, 2, 0, 3).reshape(own, ff)
    hit_own = routes_own.reshape(micro, rows, 1, top) == expert_ids[:, None]
    hit_own = jnp.any(hit_own, -1)
    slot_own = jnp.cumsum(hit_own.astype(jnp.int32), 1) - 1
    slots = jnp.arange(capacity, dtype=jnp.int32)
    find = ((slot_own[..., None] == slots) & hit_own[..., None]).astype(bf16)
    routed = jnp.einsum(
        "mtk,mkd->mtd",
        find.reshape(micro, rows, groups * capacity),
        returned.reshape(groups, micro, capacity, width)
        .swapaxes(0, 1)
        .reshape(micro, groups * capacity, width),
        preferred_element_type=f32,
    ).reshape(own, width)
    out_sum = routed + dot_pieces(hidden, wso)

    dq_own = back_of(moved, 0, qk)
    dkvup_own = back_of(moved, 256, 512)
    dkrope_own = jnp.sum(moved[..., qk:256].astype(f32), 0)
    dlatent = dot_pieces_t(dkvup_own, wkvup)
    latent_own = lax.dynamic_slice_in_dim(latent_raw, me * own, own, 0)
    cos_own = jnp.tile(lax.dynamic_slice_in_dim(cosine, me * rows, rows, 0), (micro, 1))
    sin_own = jnp.tile(lax.dynamic_slice_in_dim(sine, me * rows, rows, 0), (micro, 1))
    dlatent_raw, g_kv_gain = normed_back(latent_own, gain_kv, dlatent)
    dkvfull = jnp.concatenate([dlatent_raw, rotate_back(dkrope_own, cos_own, sin_own)], -1)
    dkvfull = dkvfull.astype(bf16)
    down = LATENT + ROPE
    early = jnp.concatenate([g_kv_gain, g_ffn_gain])
    short = early.shape[0]
    early = jnp.pad(early, (0, 16 * down - short)).reshape(16, down)
    dkv_all = spread(jnp.concatenate([dkvfull, early.astype(bf16)], 0))
    dkv_all = dkv_all.reshape(groups, own + 16, down)
    early = jnp.sum(dkv_all[:, own:].astype(f32), 0).reshape(-1)[:short]
    dkv_all = dkv_all[:, :own].reshape(total, down)
    dact = dot_pieces_t(dq_own, wq) + natural(dot_nt(dkvfull, w_down), 1)
    dx_norm, g_attn_gain = normed_back(x_own.astype(f32), gain_attn, dact)
    input_grad = dx1 + dx_norm

    height = size // groups
    act_rows = jnp.concatenate(
        [
            lax.dynamic_slice_in_dim(act, c * size + me * height, height, 1)
            for c in range(parts)
        ],
        1,
    )
    g_down = dot_tn(act_rows, dkv_all)
    g_down = exchanged(
        g_down[:height], lambda r: g_down[r * height : (r + 1) * height].astype(bf16)
    ).astype(bf16)
    early_kv, early_ffn = early[:LATENT], early[LATENT:]

    def early_gains(r):
        return jnp.concatenate([block_of(early_kv, part + r), block_of(early_ffn, part + r)])

    early = exchanged(early_gains(0), early_gains)
    late = exchanged(block_of(g_attn_gain, part), lambda r: block_of(g_attn_gain, part + r))
    count = g_attn.shape[1]
    tail = g_down[:, count:]
    tail = jnp.concatenate([tail[: height // 2], tail[height // 2 :]], 1)
    extra = jnp.concatenate([g_down[:, :count], tail], 0)
    at_late = size + extra.shape[0]
    late_rows = -(-size // count)
    late = jnp.pad(late, (0, late_rows * count - size)).reshape(late_rows, count)
    extra = jnp.concatenate([extra, late.astype(bf16)], 0)
    extra = jnp.pad(extra, ((0, 128 - extra.shape[0]), (0, 0)))
    g_attn = jnp.concatenate([g_attn.astype(bf16), extra], 0)
    g_attn = stack(row_major(g_attn))
    late = jnp.sum(g_attn[:, at_late : at_late + late_rows].astype(f32), 0).reshape(-1)[:size]
    gains = (late, early[: LATENT // parts], early[LATENT // parts :])

    mixed = (x1 + out_sum).astype(bf16)
    g_ein = sum(got_in, expert_in_grad(0))
    g_eout = sum(got_out, expert_out_grad(0))
    out_grad, query_grad, kvup_grad, g_down = attn_rows(
        g_attn, size, width // groups, qk, LATENT // parts, height
    )
    shared_in_grad, shared_out_grad = shared_rows(g_shared, 2 * parts, run)
    return (
        mixed.reshape(micro, 1, rows, width),
        input_grad.reshape(micro, 1, rows, width),
        gains[0],
        query_grad,
        g_down.T,
        gains[1],
        kvup_grad,
        out_grad,
        gains[2],
        shared_in_grad,
        shared_out_grad,
        g_ein[None],
        g_eout[None],
    )


def solution(mesh):
    tok = P(None, "dp", "expert", None)
    row = P("dp", None)
    exp = P("expert", "dp", None)
    in_specs = (
        tok, tok, P(None, "dp", None), tok, tok,
        P("dp"), row, row, P("dp"), row, row, P("dp"), row, row, exp, exp,
    )
    out_specs = (
        tok, tok, P("dp"), row, row, P("dp"), row, row, P("dp"), row, row, exp, exp,
    )

    return jax.shard_map(
        per_device, mesh=mesh, in_specs=in_specs, out_specs=out_specs, check_vma=False
    )
```

```python
import functools

import jax
import jax.numpy as jnp
from jax import lax
from jax.experimental import pallas as pl
from jax.experimental.layout import Layout, with_layout_constraint
from jax.experimental.pallas import tpu as pltpu
from jax.sharding import PartitionSpec as P

HEADS = 16
NOPE = 128
ROPE = 64
VDIM = 128
LATENT = 512
DOC_MAX = 512


theta_base = 50000.0
eps_norm = 1e-06
bf16 = jnp.bfloat16
f32 = jnp.float32


def rope_tables(length, width):
    half = width // 2
    freq = theta_base ** (-2.0 * jnp.arange(half, dtype=f32) / width)
    angle = jnp.arange(length, dtype=f32)[:, None] * freq[None, :]
    cosine = jnp.concatenate([jnp.cos(angle), jnp.cos(angle)], -1)
    sine = jnp.concatenate([jnp.sin(angle), jnp.sin(angle)], -1)
    return (cosine, sine)


def rotate_back(value, cosine, sine):
    half = value.shape[-1] // 2
    scaled = value * sine
    turned = jnp.concatenate([scaled[..., half:], -scaled[..., :half]], -1)
    return value * cosine + turned


def normed(value, gain):
    return (
        value
        * lax.rsqrt(jnp.mean(value * value, -1, keepdims=True) + eps_norm)
        * gain.astype(f32)
    )


def normed_back(value, gain, grad):
    inv = lax.rsqrt(jnp.mean(value * value, -1, keepdims=True) + eps_norm)
    hat = value * inv
    scaled = grad * gain.astype(f32)
    inner = jnp.mean(scaled * hat, -1, keepdims=True)
    return inv * (scaled - hat * inner), jnp.sum(grad * hat, 0)


def swiglu_parts(packed):
    half = packed.shape[-1] // 2
    return packed[..., :half], packed[..., half:]


def swiglu(packed):
    gate, up = swiglu_parts(packed)
    return gate * jax.nn.sigmoid(gate) * up


def swiglu_back(packed, grad):
    gate, up = swiglu_parts(packed)
    sig = jax.nn.sigmoid(gate)
    d_gate = grad * up * sig * (1.0 + gate * (1.0 - sig))
    d_up = grad * gate * sig
    return jnp.concatenate([d_gate, d_up], -1)


def dot(left, right):
    return jnp.dot(left, right, preferred_element_type=f32)


def dot_tn(left, right):
    return lax.dot_general(left, right, (((0,), (0,)), ((), ())), preferred_element_type=f32)


def dot_nt(left, right):
    return lax.dot_general(left, right, (((1,), (1,)), ((), ())), preferred_element_type=f32)


def row_major(x):
    return with_layout_constraint(x, Layout(major_to_minor=tuple(range(x.ndim))))


def after(value, *first):
    return lax.optimization_barrier((value,) + first)[0]


def block_of_keys(refs, start, stop, low):
    qn_ref, rope_ref, kv_ref, seg_col, seg_row = refs
    rows = qn_ref.shape[2]

    def take(ref, first, last):
        return ref[first // rows : last // rows, 0].reshape(last - first, ref.shape[3])

    query = jnp.concatenate([take(qn_ref, start, stop), take(rope_ref, start, stop)[:, :ROPE]], 1)
    kv = take(kv_ref, low, stop)
    key = jnp.concatenate([kv[:, :NOPE], take(rope_ref, low, stop)[:, ROPE:]], 1)
    value = kv[:, NOPE:]
    score = dot_nt(query, key) * ((NOPE + ROPE) ** (-0.5))
    size = (stop - start, stop - low)
    q_at = lax.broadcasted_iota(jnp.int32, size, 0) + (start - low)
    k_at = lax.broadcasted_iota(jnp.int32, size, 1)
    allowed = (seg_col[0, start:stop] == seg_row[0, :, low:stop]) & (k_at <= q_at)
    return query, key, value, jnp.where(allowed, score, -1e30)


def query_blocks(seq, rows, size=256):
    for start in range(0, seq, size):
        low = max(0, start - DOC_MAX + 1) // rows * rows
        yield start, start + size, low


def attend_kernel(qn_ref, rope_ref, kv_ref, seg_col, seg_row, out_ref, lse_ref):
    owners, _, rows, _ = qn_ref.shape
    refs = (qn_ref, rope_ref, kv_ref, seg_col, seg_row)
    for start, stop, low in query_blocks(owners * rows, rows):
        _, _, value, score = block_of_keys(refs, start, stop, low)
        top = jnp.max(score, -1, keepdims=True)
        expo = jnp.exp(score - top)
        total = jnp.sum(expo, -1, keepdims=True)
        out = dot((expo / total).astype(bf16), value).astype(bf16)
        at = slice(start // rows, stop // rows)
        out_ref[at, 0] = out.reshape((stop - start) // rows, rows, VDIM)
        lse_ref[0, start:stop] = top + jnp.log(total)


def attend_back_kernel(
    qn_ref, rope_ref, kv_ref, seg_col, seg_row, lse_ref, dout_ref, cos_ref, sin_ref, back_ref, acc
):
    owners, _, rows, _ = qn_ref.shape
    seq = owners * rows
    refs = (qn_ref, rope_ref, kv_ref, seg_col, seg_row)
    acc[...] = jnp.zeros_like(acc)
    for start, stop, low in query_blocks(seq, rows):
        at = slice(start // rows, stop // rows)
        query, key, value, score = block_of_keys(refs, start, stop, low)
        prob = jnp.exp(score - lse_ref[0, start:stop])
        dout = dout_ref[at, 0].reshape(stop - start, VDIM)
        dprob = dot_nt(dout, value)
        delta = jnp.sum(prob * dprob, -1, keepdims=True)
        dscore = (prob * (dprob - delta) * ((NOPE + ROPE) ** (-0.5))).astype(bf16)
        dquery = dot(dscore, key)
        acc[low:stop, : NOPE + ROPE] += dot_tn(dscore, query)
        acc[low:stop, 256:] += dot_tn(prob.astype(bf16), dout)
        rope = rotate_back(dquery[:, NOPE:], cos_ref[start:stop], sin_ref[start:stop])
        whole = jnp.concatenate([dquery[:, :NOPE], rope, rope, dquery, rope], 1)
        back_ref[at, 0] = whole.astype(bf16).reshape((stop - start) // rows, rows, 512)
    dkey = acc[...]
    tail = jnp.concatenate([dkey[:, NOPE : NOPE + ROPE], dkey[:, :NOPE], dkey[:, 256:]], 1)
    back_ref[:, 0, :, NOPE + ROPE :] = tail.astype(bf16).reshape(owners, rows, 320)


def attend(q_nope, roped, kvup, segs):
    owners, micro, rows, _ = q_nope.shape
    seq = owners * rows
    spec = lambda c: pl.BlockSpec((owners, 1, rows, c), lambda m: (0, m, 0, 0))
    return pl.pallas_call(
        attend_kernel,
        out_shape=(
            jax.ShapeDtypeStruct((owners, micro, rows, VDIM), bf16),
            jax.ShapeDtypeStruct((micro, seq, 1), f32),
        ),
        grid=(micro,),
        in_specs=[
            spec(NOPE),
            spec(2 * ROPE),
            spec(2 * NOPE),
            pl.BlockSpec((1, seq, 1), lambda m: (m, 0, 0)),
            pl.BlockSpec((1, 1, seq), lambda m: (m, 0, 0)),
        ],
        out_specs=(spec(VDIM), pl.BlockSpec((1, seq, 1), lambda m: (m, 0, 0))),
        cost_estimate=pl.CostEstimate(
            flops=2 * micro * seq * 640 * 320,
            transcendentals=micro * seq * 640,
            bytes_accessed=micro * seq * 1400,
        ),
    )(q_nope, roped, kvup, segs[:, :, None], segs[:, None, :])


def attend_back(q_nope, roped, kvup, segs, lse, dout, cosine, sine):
    owners, micro, rows, _ = q_nope.shape
    seq = owners * rows
    spec = lambda c: pl.BlockSpec((owners, 1, rows, c), lambda m: (0, m, 0, 0))
    flat = pl.BlockSpec((seq, ROPE), lambda m: (0, 0))
    return pl.pallas_call(
        attend_back_kernel,
        out_shape=jax.ShapeDtypeStruct((owners, micro, rows, 512), bf16),
        grid=(micro,),
        in_specs=[
            spec(NOPE),
            spec(2 * ROPE),
            spec(2 * NOPE),
            pl.BlockSpec((1, seq, 1), lambda m: (m, 0, 0)),
            pl.BlockSpec((1, 1, seq), lambda m: (m, 0, 0)),
            pl.BlockSpec((1, seq, 1), lambda m: (m, 0, 0)),
            spec(VDIM),
            flat,
            flat,
        ],
        out_specs=spec(512),
        scratch_shapes=[pltpu.VMEM((seq, 384), f32)],
        cost_estimate=pl.CostEstimate(
            flops=2 * micro * seq * 640 * 832,
            transcendentals=micro * seq * 640,
            bytes_accessed=micro * seq * 2600,
        ),
    )(q_nope, roped, kvup, segs[:, :, None], segs[:, None, :], lse, dout, cosine, sine)


def put_back_kernel(place_ref, rows_ref, units_ref, *refs):
    *weight_refs, out_ref = refs
    left = jnp.concatenate([place_ref[0], units_ref[...]], 1)
    weight = jnp.concatenate([w[...] for w in weight_refs], 1)
    right = jnp.concatenate([rows_ref[...], weight], 0)
    out_ref[...] = dot(left, right).astype(bf16)


def put_back(place, rows, units, *weights):
    many, size, height = place.shape
    total, count = units.shape
    width = rows.shape[1]
    return pl.pallas_call(
        put_back_kernel,
        out_shape=jax.ShapeDtypeStruct((total, width), bf16),
        grid=(many,),
        in_specs=[
            pl.BlockSpec((1, size, height), lambda i: (i, 0, 0)),
            pl.BlockSpec((height, width), lambda i: (i, 0)),
            pl.BlockSpec((size, count), lambda i: (i, 0)),
            *(pl.BlockSpec(w.shape, lambda i: (0, 0)) for w in weights),
        ],
        out_specs=pl.BlockSpec((size, width), lambda i: (i, 0)),
        cost_estimate=pl.CostEstimate(
            flops=2 * total * width * (height + count),
            transcendentals=0,
            bytes_accessed=2 * (total * width + rows.size + units.size + count * width),
        ),
    )(place, rows, units, *weights)


def shared_in_kernel(x_ref, out_ref, *, runs, piece):
    groups = x_ref.shape[0]
    turned = [x_ref[e].astype(f32).T for e in range(groups)]
    length = groups * piece
    parts = []
    for c in range(runs):
        parts += [t[:, c * piece : (c + 1) * piece] for t in turned]
        if length % 128 == 0:
            out_ref[:, c * length : (c + 1) * length] = jnp.concatenate(parts, 1)
            parts = []
    if parts:
        out_ref[...] = jnp.concatenate(parts, 1)


def shared_out_kernel(x_ref, out_ref, *, piece):
    rows = x_ref[0].astype(f32)
    count = rows.shape[0] // piece
    out_ref[0] = jnp.concatenate([rows[c * piece : (c + 1) * piece] for c in range(count)], 1)


def shared_rows(stacked, runs, piece):
    groups, count, size = stacked.shape
    first = runs * piece
    rest = count - first
    step = 128
    in_grad = pl.pallas_call(
        functools.partial(shared_in_kernel, runs=runs, piece=piece),
        out_shape=jax.ShapeDtypeStruct((size, groups * first), f32),
        grid=(size // step,),
        in_specs=[pl.BlockSpec((groups, first, step), lambda i: (0, 0, i))],
        out_specs=pl.BlockSpec((step, groups * first), lambda i: (i, 0)),
        cost_estimate=pl.CostEstimate(
            flops=0, transcendentals=0, bytes_accessed=6 * groups * first * size
        ),
    )(stacked)
    out_grad = pl.pallas_call(
        functools.partial(shared_out_kernel, piece=piece),
        out_shape=jax.ShapeDtypeStruct((groups, piece, rest // piece * size), f32),
        grid=(groups,),
        in_specs=[pl.BlockSpec((1, rest, size), lambda e: (e, first // rest, 0))],
        out_specs=pl.BlockSpec((1, piece, rest // piece * size), lambda e: (e, 0, 0)),
        cost_estimate=pl.CostEstimate(
            flops=0, transcendentals=0, bytes_accessed=6 * groups * rest * size
        ),
    )(stacked)
    return in_grad, out_grad.reshape(groups * piece, -1)


def attn_rows_kernel(x_ref, extra_ref, out_ref, query_ref, kvup_ref, down_ref, *, a, b, height):
    groups, _, count = x_ref.shape
    rest = count - a - b
    runs = x_ref.shape[1] // kvup_ref.shape[0]
    step = kvup_ref.shape[0]
    for e in range(0, groups, 2):
        one, two = x_ref[e].astype(f32), x_ref[e + 1].astype(f32)
        out_ref[:, e * a : (e + 2) * a] = jnp.concatenate([one[:, :a], two[:, :a]], 1)
        query_ref[:, e * b : (e + 2) * b] = jnp.concatenate(
            [one[:, a : a + b], two[:, a : a + b]], 1
        )
        pieces = [
            x[c * step : (c + 1) * step, a + b :] for x in (one, two) for c in range(runs)
        ]
        kvup_ref[:, e * runs * rest : (e + 2) * runs * rest] = jnp.concatenate(pieces, 1)
    half = count // 2
    rows = []
    for e in range(extra_ref.shape[0]):
        x = extra_ref[e].astype(f32)
        tail = x[height : height + height // 2]
        tail = jnp.concatenate([tail[:, :half], tail[:, half:]], 0)
        rows.append(jnp.concatenate([x[:height], tail], 1))
    down_ref[...] = jnp.concatenate(rows, 0).T


def attn_rows(stacked, rows, a, b, kvup_height, down_height):
    groups, _, count = stacked.shape
    size = 128
    steps = rows // size
    kvup_width = (count - a - b) * rows // kvup_height
    return pl.pallas_call(
        functools.partial(attn_rows_kernel, a=a, b=b, height=down_height),
        out_shape=(
            jax.ShapeDtypeStruct((rows, groups * a), f32),
            jax.ShapeDtypeStruct((rows, groups * b), f32),
            jax.ShapeDtypeStruct((kvup_height, groups * kvup_width), f32),
            jax.ShapeDtypeStruct((count * 3 // 2, groups * down_height), f32),
        ),
        grid=(steps,),
        in_specs=[
            pl.BlockSpec((groups, size, count), lambda i: (0, i, 0)),
            pl.BlockSpec((groups // steps, size, count), lambda i: (i, steps, 0)),
        ],
        out_specs=(
            pl.BlockSpec((size, groups * a), lambda i: (i, 0)),
            pl.BlockSpec((size, groups * b), lambda i: (i, 0)),
            pl.BlockSpec((kvup_height // steps, groups * kvup_width), lambda i: (i, 0)),
            pl.BlockSpec((count * 3 // 2, groups // steps * down_height), lambda i: (0, i)),
        ),
        cost_estimate=pl.CostEstimate(
            flops=0, transcendentals=0, bytes_accessed=6 * stacked.size
        ),
    )(stacked, stacked)


def per_device(
    tokens,
    grad_out,
    segments,
    routes,
    gates,
    attn_gain,
    w_query,
    w_kv_down,
    kv_gain,
    w_kv_up,
    w_out,
    ffn_gain,
    w_shared_in,
    w_shared_out,
    w_expert_in,
    w_expert_out,
):
    micro, _, rows, width = tokens.shape
    groups = lax.axis_size("expert")
    parts = lax.axis_size("dp")
    me = lax.axis_index("expert")
    part = lax.axis_index("dp")
    own = micro * rows
    total = groups * own
    seq = rows * groups
    top = routes.shape[3]
    capacity = max(2, rows * top * 4 // (3 * groups))
    qk = NOPE + ROPE
    assert HEADS == groups

    def shift(x, step):
        return lax.ppermute(x, "dp", [((i + step) % parts, i) for i in range(parts)])

    def send(x, step):
        return lax.ppermute(x, "dp", [(i, (i + step) % parts) for i in range(parts)])

    def others(x):
        return [shift(x, r) for r in range(1, parts)]

    def turn(x, axis, amount):
        size = x.shape[axis]
        return lax.dynamic_slice_in_dim(
            jnp.concatenate([x, x], axis), amount * (size // parts), size, axis
        )

    def own_first(x, axis):
        return turn(x, axis, part)

    def natural(x, axis):
        return turn(x, axis, (parts - part) % parts)

    def lay_out(x, rest):
        size = x.shape[0]
        whole = jnp.zeros((parts * size,) + x.shape[1:], x.dtype)
        for r, piece in enumerate([x] + rest):
            at = ((part + r) % parts) * size
            whole = lax.dynamic_update_slice_in_dim(whole, piece, at, 0)
        return whole

    def block_of(full, index):
        size = full.shape[0] // parts
        return lax.dynamic_slice_in_dim(full, (index % parts) * size, size, 0)

    def exchanged(own_block, block_for):
        result = own_block.astype(f32)
        for r in range(1, parts):
            result = result + send(block_for(r), r).astype(f32)
        return result

    pairs = [(i, i ^ 1) for i in range(groups)]
    odd = me % 2

    def pieces(x, *first):
        size = x.shape[0]
        found = [(x, part * size)]
        if parts == 2:
            half = size // 2
            asked = lax.dynamic_slice_in_dim(x, odd * half, half, 0)
            if first:
                asked = after(asked, *first)
            got = shift(asked, 1)
            swapped = lax.ppermute(got, "expert", pairs)
            base = (1 - part) * size
            found += [(got, base + odd * half), (swapped, base + (1 - odd) * half)]
        else:
            asked = after(x, *first) if first else x
            found += [(y, ((part + r) % parts) * size) for r, y in enumerate(others(asked), 1)]
        return found

    def dot_pieces(x, blocks):
        return sum(
            dot(lax.dynamic_slice_in_dim(x, at, w.shape[0], 1), w) for w, at in blocks
        )

    def dot_pieces_t(x, blocks):
        whole = jnp.zeros((x.shape[0], sum(w.shape[0] for w, _ in blocks)), f32)
        for w, at in blocks:
            whole = lax.dynamic_update_slice_in_dim(whole, dot_nt(x, w), at, 1)
        return whole

    def spread(x):
        return lax.all_gather(x, "expert", axis=0, tiled=True)

    def stack(x):
        return lax.all_gather(x, "expert", axis=0, tiled=False)

    def swap(x):
        return lax.all_to_all(x, "expert", split_axis=0, concat_axis=0, tiled=True)

    def collect(x):
        return lax.psum_scatter(x, "expert", scatter_dimension=0, tiled=True)

    gain_sizes = (width // parts, LATENT // parts, width // parts)
    cuts = (gain_sizes[0], gain_sizes[0] + gain_sizes[1])
    own_gains = jnp.concatenate([attn_gain, kv_gain, ffn_gain])
    gain_rows = jnp.split(lay_out(own_gains[None], [y[None] for y in others(own_gains)]), cuts, 1)
    gain_attn, gain_kv, gain_ffn = (rows_of.reshape(-1) for rows_of in gain_rows)

    wq_own = lax.dynamic_slice_in_dim(w_query, me * qk, qk, 1)
    wq_me = jnp.concatenate([wq_own] + others(wq_own), 0)
    down_pieces = pieces(w_kv_down)
    w_down = jnp.zeros((width, LATENT + ROPE), bf16)
    for w, start in down_pieces:
        start = (start - part * (width // parts)) % width
        w_down = lax.dynamic_update_slice_in_dim(w_down, w, start, 0)
    wkvup_own = lax.dynamic_slice_in_dim(w_kv_up, me * 2 * NOPE, 2 * NOPE, 1)
    wkvup_me = lay_out(wkvup_own, others(wkvup_own))
    wout = pieces(w_out)

    def turned(w):
        return jnp.concatenate([-w[:, ROPE // 2 :], w[:, : ROPE // 2]], 1)

    rope_q, rope_k = wq_me[:, NOPE:], w_down[:, LATENT:]
    w_first = jnp.concatenate(
        [
            wq_me[:, :NOPE],
            w_down[:, :LATENT],
            rope_q,
            rope_k,
            turned(rope_q),
            turned(rope_k),
        ],
        1,
    )

    x_own = tokens[:, 0].reshape(own, width)
    dy_own = grad_out[:, 0].reshape(own, width)
    act_own = normed(x_own.astype(f32), gain_attn).astype(bf16)
    act = spread(own_first(act_own, 1))
    dy_all = spread(after(dy_own, act))

    expert_ids = jnp.arange(groups, dtype=jnp.int32)
    routes_own = routes[:, 0].reshape(own, top)
    gates_own = gates[:, 0].reshape(own, top)
    table = jnp.sum(
        jnp.where(routes_own[None] == expert_ids[:, None, None], gates_own[None], 0.0), -1
    )
    gate_rows = swap(table).reshape(groups * micro, rows)
    hit = gate_rows > 0.0
    slot = jnp.cumsum(hit.astype(jnp.int32), 1) - 1
    pick = (slot[:, None, :] == jnp.arange(capacity, dtype=jnp.int32)[None, :, None]) & hit[
        :, None, :
    ]
    gate_slots = jnp.sum(jnp.where(pick, gate_rows[:, None, :], 0.0), -1).reshape(-1, 1)
    pick = pick.astype(bf16)
    together = 4
    place = pick.swapaxes(1, 2).reshape(-1, together, rows, 1, capacity)
    place = place * jnp.eye(together, dtype=bf16)[None, :, None, :, None]
    place = place.reshape(-1, together * rows, together * capacity)

    def dispatch(x):
        picked = jnp.einsum(
            "bst,btd->bsd",
            pick,
            x.reshape(groups * micro, rows, width),
            preferred_element_type=f32,
        )
        return picked.reshape(groups * micro * capacity, width)

    ff = w_shared_in.shape[1] // 2
    run = ff // (parts * groups)
    wsi_own = jnp.concatenate(
        [
            lax.dynamic_slice_in_dim(w_shared_in, c * (ff // parts) + me * run, run, 1).T
            for c in range(2 * parts)
        ],
        0,
    )
    wso_own = lax.dynamic_slice_in_dim(w_shared_out, me * run, run, 0)
    wsi_blocks = [wsi_own] + others(wsi_own)
    wsi_me = jnp.concatenate(wsi_blocks, 1)
    wso_me = lay_out(wso_own, others(wso_own))
    wei_others = others(w_expert_in[0])
    weo_others = others(w_expert_out[0])
    wq = pieces(w_query, wei_others[0], weo_others[0])
    wkvup = pieces(w_kv_up, wei_others[0], weo_others[0])
    wso = pieces(w_shared_out, wei_others[0], weo_others[0])

    cosine, sine = rope_tables(seq, ROPE)

    def table_of(values):
        both = jnp.concatenate([values, values], 1).reshape(groups, 1, rows, 2 * ROPE)
        return jnp.broadcast_to(both, (groups, micro, rows, 2 * ROPE)).reshape(total, 2 * ROPE)

    first = dot(after(act, gate_rows), w_first)
    q_nope = first[:, :NOPE].astype(bf16)
    latent_raw = first[:, NOPE : NOPE + LATENT]
    latent = normed(latent_raw, gain_kv).astype(bf16)
    at = NOPE + LATENT
    roped = (
        first[:, at : at + 2 * ROPE] * table_of(cosine) + first[:, at + 2 * ROPE :] * table_of(sine)
    ).astype(bf16)
    kvup = dot(latent, wkvup_me).astype(bf16)

    def owners(x):
        return x.reshape(groups, micro, rows, x.shape[-1])

    segs = segments[:, 0]
    head = (owners(q_nope), owners(roped), owners(kvup), segs)
    attn, lse = attend(*head)
    attn_own = swap(attn.reshape(groups, own, VDIM))
    attn_own = attn_own.swapaxes(0, 1).reshape(own, groups * VDIM)
    x1 = x_own.astype(f32) + dot_pieces(attn_own, wout)
    hid_own = normed(x1, gain_ffn).astype(bf16)
    hid_all = spread(own_first(hid_own, 1))
    attn_all = spread(after(attn_own, hid_all))

    size = width // parts
    arrived = dispatch(hid_all).astype(bf16)
    dyexp = (gate_slots * dispatch(dy_all)).astype(bf16)
    wei = jnp.concatenate([w_expert_in[0]] + wei_others, 0)
    weo = lay_out(w_expert_out[0], weo_others)
    epre = dot(arrived, wei)
    eact = swiglu(epre).astype(bf16)
    deact = dot_nt(dyexp, weo)
    depre = swiglu_back(epre, deact).astype(bf16)
    dhid_rows = dot_nt(depre, wei).astype(bf16)

    spre = dot_nt(hid_all, wsi_me)
    sact = swiglu(spre).astype(bf16)
    dsact = dot_nt(dy_all, wso_me)
    dspre = swiglu_back(spre, dsact).astype(bf16)
    dhid_part = put_back(place, dhid_rows, dspre, *wsi_blocks)
    dhid_sum = collect(dhid_part)

    arrived, depre, eact, dyexp, dspre, sact = lax.optimization_barrier(
        (arrived, depre, eact, dyexp, dspre, sact, dhid_part)
    )[:6]
    hidden = swap(sact.reshape(groups, own, -1))
    gated = (gate_slots * dot(eact, weo)).astype(bf16)
    dspre, sact = lax.optimization_barrier((dspre, sact, gated))[:2]
    g_si = dot_tn(dspre, hid_all)
    g_so = dot_tn(sact, dy_all)

    def shared_grads(r):
        rows_of = block_of(g_so, part + r)
        return jnp.concatenate(
            [g_si[:, r * size : (r + 1) * size]] + jnp.split(rows_of, parts, 1), 0
        )

    g_shared = exchanged(shared_grads(0), lambda r: shared_grads(r).astype(bf16))
    g_shared = stack(after(g_shared.astype(bf16), dhid_sum))

    def expert_in_grad(r):
        return dot_tn(arrived[:, r * size : (r + 1) * size], depre)

    def expert_out_grad(r):
        short = eact.shape[1] // parts
        some = lax.dynamic_slice_in_dim(eact, ((part + r) % parts) * short, short, 1)
        return dot_tn(some, dyexp)

    sent_in = [expert_in_grad(r).astype(bf16) for r in range(1, parts)]
    sent_out = [expert_out_grad(r).astype(bf16) for r in range(1, parts)]
    dhid_sum = after(dhid_sum, gated, hidden, *sent_in, *sent_out)
    got_in = [send(x, r).astype(f32) for r, x in enumerate(sent_in, 1)]
    got_out = [send(x, r).astype(f32) for r, x in enumerate(sent_out, 1)]
    dhid = natural(dhid_sum, 1).astype(f32)

    dy = dy_own.astype(f32)
    dx1_norm, g_ffn_gain = normed_back(x1, gain_ffn, dhid)
    dx1 = dy + dx1_norm
    dx1_low = dx1.astype(bf16)
    dattn_own = dot_pieces_t(dx1_low, wout).astype(bf16)
    dattn = swap(dattn_own.reshape(own, groups, VDIM).swapaxes(0, 1))
    dao = after(dx1_low, dattn).reshape(own, groups, width // groups).swapaxes(0, 1)
    dao = swap(dao)
    dattn = dattn.reshape(groups, micro, rows, VDIM)
    back = attend_back(*head, lse, dattn, cosine, sine)
    moved = swap(back.reshape(groups, own, 512))

    def back_of(x, first_column, last_column):
        piece = x[..., first_column:last_column]
        return piece.swapaxes(0, 1).reshape(own, groups * (last_column - first_column))

    flat = back.reshape(total, 512)
    g_query = dot_tn(act, flat[:, :qk])
    g_kvup = dot_tn(latent, flat[:, 256:])
    g_out = dot_tn(attn_all, dao.reshape(total, width // groups))

    def fold(x):
        steps = size // 128
        runs = size // x.shape[0]
        x = x.reshape(steps, x.shape[0] // steps, runs, x.shape[1] // runs)
        return x.swapaxes(1, 2).reshape(size, -1)

    def attn_grads(r):
        return jnp.concatenate(
            [
                block_of(g_out, part + r),
                g_query[r * size : (r + 1) * size],
                fold(block_of(g_kvup, part + r)),
            ],
            1,
        )

    g_attn = exchanged(attn_grads(0), lambda r: attn_grads(r).astype(bf16))

    returned = after(gated, moved).reshape(groups, micro * capacity, width)
    returned = swap(returned)
    hidden = hidden.reshape(groups, own, parts, run).transpose(1, 2, 0, 3).reshape(own, ff)
    hit_own = routes_own.reshape(micro, rows, 1, top) == expert_ids[:, None]
    hit_own = jnp.any(hit_own, -1)
    slot_own = jnp.cumsum(hit_own.astype(jnp.int32), 1) - 1
    slots = jnp.arange(capacity, dtype=jnp.int32)
    find = ((slot_own[..., None] == slots) & hit_own[..., None]).astype(bf16)
    routed = jnp.einsum(
        "mtk,mkd->mtd",
        find.reshape(micro, rows, groups * capacity),
        returned.reshape(groups, micro, capacity, width)
        .swapaxes(0, 1)
        .reshape(micro, groups * capacity, width),
        preferred_element_type=f32,
    ).reshape(own, width)
    out_sum = routed + dot_pieces(hidden, wso)

    dq_own = back_of(moved, 0, qk)
    dkvup_own = back_of(moved, 256, 512)
    dkrope_own = jnp.sum(moved[..., qk:256].astype(f32), 0)
    dlatent = dot_pieces_t(dkvup_own, wkvup)
    latent_own = lax.dynamic_slice_in_dim(latent_raw, me * own, own, 0)
    cos_own = jnp.tile(lax.dynamic_slice_in_dim(cosine, me * rows, rows, 0), (micro, 1))
    sin_own = jnp.tile(lax.dynamic_slice_in_dim(sine, me * rows, rows, 0), (micro, 1))
    dlatent_raw, g_kv_gain = normed_back(latent_own, gain_kv, dlatent)
    dkvfull = jnp.concatenate([dlatent_raw, rotate_back(dkrope_own, cos_own, sin_own)], -1)
    dkvfull = dkvfull.astype(bf16)
    down = LATENT + ROPE
    early = jnp.concatenate([g_kv_gain, g_ffn_gain])
    short = early.shape[0]
    early = jnp.pad(early, (0, 16 * down - short)).reshape(16, down)
    dkv_all = spread(jnp.concatenate([dkvfull, early.astype(bf16)], 0))
    dkv_all = dkv_all.reshape(groups, own + 16, down)
    early = jnp.sum(dkv_all[:, own:].astype(f32), 0).reshape(-1)[:short]
    dkv_all = dkv_all[:, :own].reshape(total, down)
    dact = dot_pieces_t(dq_own, wq) + natural(dot_nt(dkvfull, w_down), 1)
    dx_norm, g_attn_gain = normed_back(x_own.astype(f32), gain_attn, dact)
    input_grad = dx1 + dx_norm

    height = size // groups
    act_rows = jnp.concatenate(
        [
            lax.dynamic_slice_in_dim(act, c * size + me * height, height, 1)
            for c in range(parts)
        ],
        1,
    )
    g_down = dot_tn(act_rows, dkv_all)
    g_down = exchanged(
        g_down[:height], lambda r: g_down[r * height : (r + 1) * height].astype(bf16)
    ).astype(bf16)
    early_kv, early_ffn = early[:LATENT], early[LATENT:]

    def early_gains(r):
        return jnp.concatenate([block_of(early_kv, part + r), block_of(early_ffn, part + r)])

    early = exchanged(early_gains(0), early_gains)
    late = exchanged(block_of(g_attn_gain, part), lambda r: block_of(g_attn_gain, part + r))
    count = g_attn.shape[1]
    tail = g_down[:, count:]
    tail = jnp.concatenate([tail[: height // 2], tail[height // 2 :]], 1)
    extra = jnp.concatenate([g_down[:, :count], tail], 0)
    at_late = size + extra.shape[0]
    late_rows = -(-size // count)
    late = jnp.pad(late, (0, late_rows * count - size)).reshape(late_rows, count)
    extra = jnp.concatenate([extra, late.astype(bf16)], 0)
    extra = jnp.pad(extra, ((0, 128 - extra.shape[0]), (0, 0)))
    g_attn = jnp.concatenate([g_attn.astype(bf16), extra], 0)
    g_attn = stack(row_major(g_attn))
    late = jnp.sum(g_attn[:, at_late : at_late + late_rows].astype(f32), 0).reshape(-1)[:size]
    gains = (late, early[: LATENT // parts], early[LATENT // parts :])

    mixed = (x1 + out_sum).astype(bf16)
    g_ein = sum(got_in, expert_in_grad(0))
    g_eout = sum(got_out, expert_out_grad(0))
    out_grad, query_grad, kvup_grad, g_down = attn_rows(
        g_attn, size, width // groups, qk, LATENT // parts, height
    )
    shared_in_grad, shared_out_grad = shared_rows(g_shared, 2 * parts, run)
    return (
        mixed.reshape(micro, 1, rows, width),
        input_grad.reshape(micro, 1, rows, width),
        gains[0],
        query_grad,
        g_down.T,
        gains[1],
        kvup_grad,
        out_grad,
        gains[2],
        shared_in_grad,
        shared_out_grad,
        g_ein[None],
        g_eout[None],
    )


def solution(mesh):
    tok = P(None, "dp", "expert", None)
    row = P("dp", None)
    exp = P("expert", "dp", None)
    in_specs = (
        tok, tok, P(None, "dp", None), tok, tok,
        P("dp"), row, row, P("dp"), row, row, P("dp"), row, row, exp, exp,
    )
    out_specs = (
        tok, tok, P("dp"), row, row, P("dp"), row, row, P("dp"), row, row, exp, exp,
    )

    return jax.shard_map(
        per_device, mesh=mesh, in_specs=in_specs, out_specs=out_specs, check_vma=False
    )
```

```python
import functools

import jax
import jax.numpy as jnp
from jax import lax
from jax.experimental import pallas as pl
from jax.experimental.layout import Layout, with_layout_constraint
from jax.experimental.pallas import tpu as pltpu
from jax.sharding import PartitionSpec as P

HEADS = 16
NOPE = 128
ROPE = 64
VDIM = 128
LATENT = 512
DOC_MAX = 512


theta_base = 50000.0
eps_norm = 1e-06
bf16 = jnp.bfloat16
f32 = jnp.float32


def rope_tables(length, width):
    half = width // 2
    freq = theta_base ** (-2.0 * jnp.arange(half, dtype=f32) / width)
    angle = jnp.arange(length, dtype=f32)[:, None] * freq[None, :]
    cosine = jnp.concatenate([jnp.cos(angle), jnp.cos(angle)], -1)
    sine = jnp.concatenate([jnp.sin(angle), jnp.sin(angle)], -1)
    return (cosine, sine)


def rotate_back(value, cosine, sine):
    half = value.shape[-1] // 2
    scaled = value * sine
    turned = jnp.concatenate([scaled[..., half:], -scaled[..., :half]], -1)
    return value * cosine + turned


def normed(value, gain):
    return (
        value
        * lax.rsqrt(jnp.mean(value * value, -1, keepdims=True) + eps_norm)
        * gain.astype(f32)
    )


def normed_back(value, gain, grad):
    inv = lax.rsqrt(jnp.mean(value * value, -1, keepdims=True) + eps_norm)
    hat = value * inv
    scaled = grad * gain.astype(f32)
    inner = jnp.mean(scaled * hat, -1, keepdims=True)
    return inv * (scaled - hat * inner), jnp.sum(grad * hat, 0)


def swiglu_parts(packed):
    half = packed.shape[-1] // 2
    return packed[..., :half], packed[..., half:]


def swiglu(packed):
    gate, up = swiglu_parts(packed)
    return gate * jax.nn.sigmoid(gate) * up


def swiglu_back(packed, grad):
    gate, up = swiglu_parts(packed)
    sig = jax.nn.sigmoid(gate)
    d_gate = grad * up * sig * (1.0 + gate * (1.0 - sig))
    d_up = grad * gate * sig
    return jnp.concatenate([d_gate, d_up], -1)


def dot(left, right):
    return jnp.dot(left, right, preferred_element_type=f32)


def dot_tn(left, right):
    return lax.dot_general(left, right, (((0,), (0,)), ((), ())), preferred_element_type=f32)


def dot_nt(left, right):
    return lax.dot_general(left, right, (((1,), (1,)), ((), ())), preferred_element_type=f32)


def row_major(x):
    return with_layout_constraint(x, Layout(major_to_minor=tuple(range(x.ndim))))


def after(value, *first):
    return lax.optimization_barrier((value,) + first)[0]


def block_of_keys(refs, start, stop, low):
    qn_ref, rope_ref, kv_ref, seg_col, seg_row = refs
    rows = qn_ref.shape[2]

    def take(ref, first, last):
        return ref[first // rows : last // rows, 0].reshape(last - first, ref.shape[3])

    query = jnp.concatenate([take(qn_ref, start, stop), take(rope_ref, start, stop)[:, :ROPE]], 1)
    kv = take(kv_ref, low, stop)
    key = jnp.concatenate([kv[:, :NOPE], take(rope_ref, low, stop)[:, ROPE:]], 1)
    value = kv[:, NOPE:]
    score = dot_nt(query, key) * ((NOPE + ROPE) ** (-0.5))
    size = (stop - start, stop - low)
    q_at = lax.broadcasted_iota(jnp.int32, size, 0) + (start - low)
    k_at = lax.broadcasted_iota(jnp.int32, size, 1)
    allowed = (seg_col[0, start:stop] == seg_row[0, :, low:stop]) & (k_at <= q_at)
    return query, key, value, jnp.where(allowed, score, -1e30)


def query_blocks(seq, rows, size=256):
    for start in range(0, seq, size):
        low = max(0, start - DOC_MAX + 1) // rows * rows
        yield start, start + size, low


def attend_kernel(qn_ref, rope_ref, kv_ref, seg_col, seg_row, out_ref, lse_ref):
    owners, _, rows, _ = qn_ref.shape
    refs = (qn_ref, rope_ref, kv_ref, seg_col, seg_row)
    for start, stop, low in query_blocks(owners * rows, rows):
        _, _, value, score = block_of_keys(refs, start, stop, low)
        top = jnp.max(score, -1, keepdims=True)
        expo = jnp.exp(score - top)
        total = jnp.sum(expo, -1, keepdims=True)
        out = dot((expo / total).astype(bf16), value).astype(bf16)
        at = slice(start // rows, stop // rows)
        out_ref[at, 0] = out.reshape((stop - start) // rows, rows, VDIM)
        lse_ref[0, start:stop] = top + jnp.log(total)


def attend_back_kernel(
    qn_ref, rope_ref, kv_ref, seg_col, seg_row, lse_ref, dout_ref, cos_ref, sin_ref, back_ref, acc
):
    owners, _, rows, _ = qn_ref.shape
    seq = owners * rows
    refs = (qn_ref, rope_ref, kv_ref, seg_col, seg_row)
    acc[...] = jnp.zeros_like(acc)
    for start, stop, low in query_blocks(seq, rows):
        at = slice(start // rows, stop // rows)
        query, key, value, score = block_of_keys(refs, start, stop, low)
        prob = jnp.exp(score - lse_ref[0, start:stop])
        dout = dout_ref[at, 0].reshape(stop - start, VDIM)
        dprob = dot_nt(dout, value)
        delta = jnp.sum(prob * dprob, -1, keepdims=True)
        dscore = (prob * (dprob - delta) * ((NOPE + ROPE) ** (-0.5))).astype(bf16)
        dquery = dot(dscore, key)
        acc[low:stop, : NOPE + ROPE] += dot_tn(dscore, query)
        acc[low:stop, 256:] += dot_tn(prob.astype(bf16), dout)
        rope = rotate_back(dquery[:, NOPE:], cos_ref[start:stop], sin_ref[start:stop])
        whole = jnp.concatenate([dquery[:, :NOPE], rope, rope, dquery, rope], 1)
        back_ref[at, 0] = whole.astype(bf16).reshape((stop - start) // rows, rows, 512)
    dkey = acc[...]
    tail = jnp.concatenate([dkey[:, NOPE : NOPE + ROPE], dkey[:, :NOPE], dkey[:, 256:]], 1)
    back_ref[:, 0, :, NOPE + ROPE :] = tail.astype(bf16).reshape(owners, rows, 320)


def attend(q_nope, roped, kvup, segs):
    owners, micro, rows, _ = q_nope.shape
    seq = owners * rows
    spec = lambda c: pl.BlockSpec((owners, 1, rows, c), lambda m: (0, m, 0, 0))
    return pl.pallas_call(
        attend_kernel,
        out_shape=(
            jax.ShapeDtypeStruct((owners, micro, rows, VDIM), bf16),
            jax.ShapeDtypeStruct((micro, seq, 1), f32),
        ),
        grid=(micro,),
        in_specs=[
            spec(NOPE),
            spec(2 * ROPE),
            spec(2 * NOPE),
            pl.BlockSpec((1, seq, 1), lambda m: (m, 0, 0)),
            pl.BlockSpec((1, 1, seq), lambda m: (m, 0, 0)),
        ],
        out_specs=(spec(VDIM), pl.BlockSpec((1, seq, 1), lambda m: (m, 0, 0))),
        cost_estimate=pl.CostEstimate(
            flops=2 * micro * seq * 640 * 320,
            transcendentals=micro * seq * 640,
            bytes_accessed=micro * seq * 1400,
        ),
    )(q_nope, roped, kvup, segs[:, :, None], segs[:, None, :])


def attend_back(q_nope, roped, kvup, segs, lse, dout, cosine, sine):
    owners, micro, rows, _ = q_nope.shape
    seq = owners * rows
    spec = lambda c: pl.BlockSpec((owners, 1, rows, c), lambda m: (0, m, 0, 0))
    flat = pl.BlockSpec((seq, ROPE), lambda m: (0, 0))
    return pl.pallas_call(
        attend_back_kernel,
        out_shape=jax.ShapeDtypeStruct((owners, micro, rows, 512), bf16),
        grid=(micro,),
        in_specs=[
            spec(NOPE),
            spec(2 * ROPE),
            spec(2 * NOPE),
            pl.BlockSpec((1, seq, 1), lambda m: (m, 0, 0)),
            pl.BlockSpec((1, 1, seq), lambda m: (m, 0, 0)),
            pl.BlockSpec((1, seq, 1), lambda m: (m, 0, 0)),
            spec(VDIM),
            flat,
            flat,
        ],
        out_specs=spec(512),
        scratch_shapes=[pltpu.VMEM((seq, 384), f32)],
        cost_estimate=pl.CostEstimate(
            flops=2 * micro * seq * 640 * 832,
            transcendentals=micro * seq * 640,
            bytes_accessed=micro * seq * 2600,
        ),
    )(q_nope, roped, kvup, segs[:, :, None], segs[:, None, :], lse, dout, cosine, sine)


def put_back_kernel(place_ref, rows_ref, units_ref, *refs):
    *weight_refs, out_ref = refs
    left = jnp.concatenate([place_ref[0], units_ref[...]], 1)
    weight = jnp.concatenate([w[...] for w in weight_refs], 1)
    right = jnp.concatenate([rows_ref[...], weight], 0)
    out_ref[...] = dot(left, right).astype(bf16)


def put_back(place, rows, units, *weights):
    many, size, height = place.shape
    total, count = units.shape
    width = rows.shape[1]
    return pl.pallas_call(
        put_back_kernel,
        out_shape=jax.ShapeDtypeStruct((total, width), bf16),
        grid=(many,),
        in_specs=[
            pl.BlockSpec((1, size, height), lambda i: (i, 0, 0)),
            pl.BlockSpec((height, width), lambda i: (i, 0)),
            pl.BlockSpec((size, count), lambda i: (i, 0)),
            *(pl.BlockSpec(w.shape, lambda i: (0, 0)) for w in weights),
        ],
        out_specs=pl.BlockSpec((size, width), lambda i: (i, 0)),
        cost_estimate=pl.CostEstimate(
            flops=2 * total * width * (height + count),
            transcendentals=0,
            bytes_accessed=2 * (total * width + rows.size + units.size + count * width),
        ),
    )(place, rows, units, *weights)


def shared_in_kernel(x_ref, out_ref, *, runs, piece):
    groups = x_ref.shape[0]
    turned = [x_ref[e].astype(f32).T for e in range(groups)]
    length = groups * piece
    parts = []
    for c in range(runs):
        parts += [t[:, c * piece : (c + 1) * piece] for t in turned]
        if length % 128 == 0:
            out_ref[:, c * length : (c + 1) * length] = jnp.concatenate(parts, 1)
            parts = []
    if parts:
        out_ref[...] = jnp.concatenate(parts, 1)


def shared_out_kernel(x_ref, out_ref, *, piece):
    rows = x_ref[0].astype(f32)
    count = rows.shape[0] // piece
    out_ref[0] = jnp.concatenate([rows[c * piece : (c + 1) * piece] for c in range(count)], 1)


def shared_rows(stacked, runs, piece):
    groups, count, size = stacked.shape
    first = runs * piece
    rest = count - first
    step = 128
    in_grad = pl.pallas_call(
        functools.partial(shared_in_kernel, runs=runs, piece=piece),
        out_shape=jax.ShapeDtypeStruct((size, groups * first), f32),
        grid=(size // step,),
        in_specs=[pl.BlockSpec((groups, first, step), lambda i: (0, 0, i))],
        out_specs=pl.BlockSpec((step, groups * first), lambda i: (i, 0)),
        cost_estimate=pl.CostEstimate(
            flops=0, transcendentals=0, bytes_accessed=6 * groups * first * size
        ),
    )(stacked)
    out_grad = pl.pallas_call(
        functools.partial(shared_out_kernel, piece=piece),
        out_shape=jax.ShapeDtypeStruct((groups, piece, rest // piece * size), f32),
        grid=(groups,),
        in_specs=[pl.BlockSpec((1, rest, size), lambda e: (e, first // rest, 0))],
        out_specs=pl.BlockSpec((1, piece, rest // piece * size), lambda e: (e, 0, 0)),
        cost_estimate=pl.CostEstimate(
            flops=0, transcendentals=0, bytes_accessed=6 * groups * rest * size
        ),
    )(stacked)
    return in_grad, out_grad.reshape(groups * piece, -1)


def attn_rows_kernel(x_ref, out_ref, query_ref, kvup_ref, *, a, b):
    groups, _, count = x_ref.shape
    rest = count - a - b
    runs = x_ref.shape[1] // kvup_ref.shape[0]
    step = kvup_ref.shape[0]
    for e in range(0, groups, 2):
        one, two = x_ref[e].astype(f32), x_ref[e + 1].astype(f32)
        out_ref[:, e * a : (e + 2) * a] = jnp.concatenate([one[:, :a], two[:, :a]], 1)
        query_ref[:, e * b : (e + 2) * b] = jnp.concatenate(
            [one[:, a : a + b], two[:, a : a + b]], 1
        )
        pieces = [
            x[c * step : (c + 1) * step, a + b :] for x in (one, two) for c in range(runs)
        ]
        kvup_ref[:, e * runs * rest : (e + 2) * runs * rest] = jnp.concatenate(pieces, 1)


def attn_rows(stacked, a, b, kvup_height):
    groups, rows, count = stacked.shape
    size = 128
    steps = rows // size
    kvup_width = (count - a - b) * rows // kvup_height
    return pl.pallas_call(
        functools.partial(attn_rows_kernel, a=a, b=b),
        out_shape=(
            jax.ShapeDtypeStruct((rows, groups * a), f32),
            jax.ShapeDtypeStruct((rows, groups * b), f32),
            jax.ShapeDtypeStruct((kvup_height, groups * kvup_width), f32),
        ),
        grid=(steps,),
        in_specs=[
            pl.BlockSpec((groups, size, count), lambda i: (0, i, 0)),
        ],
        out_specs=(
            pl.BlockSpec((size, groups * a), lambda i: (i, 0)),
            pl.BlockSpec((size, groups * b), lambda i: (i, 0)),
            pl.BlockSpec((kvup_height // steps, groups * kvup_width), lambda i: (i, 0)),
        ),
        cost_estimate=pl.CostEstimate(
            flops=0, transcendentals=0, bytes_accessed=6 * stacked.size
        ),
    )(stacked)


def per_device(
    tokens,
    grad_out,
    segments,
    routes,
    gates,
    attn_gain,
    w_query,
    w_kv_down,
    kv_gain,
    w_kv_up,
    w_out,
    ffn_gain,
    w_shared_in,
    w_shared_out,
    w_expert_in,
    w_expert_out,
):
    micro, _, rows, width = tokens.shape
    groups = lax.axis_size("expert")
    parts = lax.axis_size("dp")
    me = lax.axis_index("expert")
    part = lax.axis_index("dp")
    own = micro * rows
    total = groups * own
    seq = rows * groups
    top = routes.shape[3]
    capacity = max(2, rows * top * 4 // (3 * groups))
    qk = NOPE + ROPE
    assert HEADS == groups

    def shift(x, step):
        return lax.ppermute(x, "dp", [((i + step) % parts, i) for i in range(parts)])

    def send(x, step):
        return lax.ppermute(x, "dp", [(i, (i + step) % parts) for i in range(parts)])

    def others(x):
        return [shift(x, r) for r in range(1, parts)]

    def turn(x, axis, amount):
        size = x.shape[axis]
        return lax.dynamic_slice_in_dim(
            jnp.concatenate([x, x], axis), amount * (size // parts), size, axis
        )

    def own_first(x, axis):
        return turn(x, axis, part)

    def natural(x, axis):
        return turn(x, axis, (parts - part) % parts)

    def lay_out(x, rest):
        size = x.shape[0]
        whole = jnp.zeros((parts * size,) + x.shape[1:], x.dtype)
        for r, piece in enumerate([x] + rest):
            at = ((part + r) % parts) * size
            whole = lax.dynamic_update_slice_in_dim(whole, piece, at, 0)
        return whole

    def block_of(full, index):
        size = full.shape[0] // parts
        return lax.dynamic_slice_in_dim(full, (index % parts) * size, size, 0)

    def exchanged(own_block, block_for):
        result = own_block.astype(f32)
        for r in range(1, parts):
            result = result + send(block_for(r), r).astype(f32)
        return result

    pairs = [(i, i ^ 1) for i in range(groups)]
    odd = me % 2

    def pieces(x, *first):
        size = x.shape[0]
        found = [(x, part * size)]
        if parts == 2:
            half = size // 2
            asked = lax.dynamic_slice_in_dim(x, odd * half, half, 0)
            if first:
                asked = after(asked, *first)
            got = shift(asked, 1)
            swapped = lax.ppermute(got, "expert", pairs)
            base = (1 - part) * size
            found += [(got, base + odd * half), (swapped, base + (1 - odd) * half)]
        else:
            asked = after(x, *first) if first else x
            found += [(y, ((part + r) % parts) * size) for r, y in enumerate(others(asked), 1)]
        return found

    def dot_pieces(x, blocks):
        return sum(
            dot(lax.dynamic_slice_in_dim(x, at, w.shape[0], 1), w) for w, at in blocks
        )

    def dot_pieces_t(x, blocks):
        whole = jnp.zeros((x.shape[0], sum(w.shape[0] for w, _ in blocks)), f32)
        for w, at in blocks:
            whole = lax.dynamic_update_slice_in_dim(whole, dot_nt(x, w), at, 1)
        return whole

    def spread(x):
        return lax.all_gather(x, "expert", axis=0, tiled=True)

    def stack(x):
        return lax.all_gather(x, "expert", axis=0, tiled=False)

    def swap(x):
        return lax.all_to_all(x, "expert", split_axis=0, concat_axis=0, tiled=True)

    def spread_pairs(x):
        assert groups & (groups - 1) == 0
        whole, mask = x[None], groups // 2
        while mask:
            partners = [(i, i ^ mask) for i in range(groups)]
            other = lax.ppermute(whole, "expert", partners)
            upper = (me // mask) % 2 == 1
            pair = [jnp.where(upper, other, whole), jnp.where(upper, whole, other)]
            whole = jnp.stack(pair, 1).reshape((2 * whole.shape[0],) + x.shape)
            mask //= 2
        return whole

    def collect(x):
        return lax.psum_scatter(x, "expert", scatter_dimension=0, tiled=True)

    gain_sizes = (width // parts, LATENT // parts, width // parts)
    cuts = (gain_sizes[0], gain_sizes[0] + gain_sizes[1])
    own_gains = jnp.concatenate([attn_gain, kv_gain, ffn_gain])
    gain_rows = jnp.split(lay_out(own_gains[None], [y[None] for y in others(own_gains)]), cuts, 1)
    gain_attn, gain_kv, gain_ffn = (rows_of.reshape(-1) for rows_of in gain_rows)

    wq_own = lax.dynamic_slice_in_dim(w_query, me * qk, qk, 1)
    wq_me = jnp.concatenate([wq_own] + others(wq_own), 0)
    down_pieces = pieces(w_kv_down)
    w_down = jnp.zeros((width, LATENT + ROPE), bf16)
    for w, start in down_pieces:
        start = (start - part * (width // parts)) % width
        w_down = lax.dynamic_update_slice_in_dim(w_down, w, start, 0)
    wkvup_own = lax.dynamic_slice_in_dim(w_kv_up, me * 2 * NOPE, 2 * NOPE, 1)
    wkvup_me = lay_out(wkvup_own, others(wkvup_own))
    wout = pieces(w_out)

    def turned(w):
        return jnp.concatenate([-w[:, ROPE // 2 :], w[:, : ROPE // 2]], 1)

    rope_q, rope_k = wq_me[:, NOPE:], w_down[:, LATENT:]
    w_first = jnp.concatenate(
        [
            wq_me[:, :NOPE],
            w_down[:, :LATENT],
            rope_q,
            rope_k,
            turned(rope_q),
            turned(rope_k),
        ],
        1,
    )

    x_own = tokens[:, 0].reshape(own, width)
    dy_own = grad_out[:, 0].reshape(own, width)
    act_own = normed(x_own.astype(f32), gain_attn).astype(bf16)
    act = spread(own_first(act_own, 1))
    dy_all = spread(after(dy_own, act))

    expert_ids = jnp.arange(groups, dtype=jnp.int32)
    routes_own = routes[:, 0].reshape(own, top)
    gates_own = gates[:, 0].reshape(own, top)
    table = jnp.sum(
        jnp.where(routes_own[None] == expert_ids[:, None, None], gates_own[None], 0.0), -1
    )
    gate_rows = swap(table).reshape(groups * micro, rows)
    hit = gate_rows > 0.0
    slot = jnp.cumsum(hit.astype(jnp.int32), 1) - 1
    pick = (slot[:, None, :] == jnp.arange(capacity, dtype=jnp.int32)[None, :, None]) & hit[
        :, None, :
    ]
    gate_slots = jnp.sum(jnp.where(pick, gate_rows[:, None, :], 0.0), -1).reshape(-1, 1)
    pick = pick.astype(bf16)
    together = 4
    place = pick.swapaxes(1, 2).reshape(-1, together, rows, 1, capacity)
    place = place * jnp.eye(together, dtype=bf16)[None, :, None, :, None]
    place = place.reshape(-1, together * rows, together * capacity)

    def dispatch(x):
        picked = jnp.einsum(
            "bst,btd->bsd",
            pick,
            x.reshape(groups * micro, rows, width),
            preferred_element_type=f32,
        )
        return picked.reshape(groups * micro * capacity, width)

    ff = w_shared_in.shape[1] // 2
    run = ff // (parts * groups)
    wsi_own = jnp.concatenate(
        [
            lax.dynamic_slice_in_dim(w_shared_in, c * (ff // parts) + me * run, run, 1).T
            for c in range(2 * parts)
        ],
        0,
    )
    wso_own = lax.dynamic_slice_in_dim(w_shared_out, me * run, run, 0)
    wsi_blocks = [wsi_own] + others(wsi_own)
    wsi_me = jnp.concatenate(wsi_blocks, 1)
    wso_me = lay_out(wso_own, others(wso_own))
    wei_others = others(w_expert_in[0])
    weo_others = others(w_expert_out[0])
    wq = pieces(w_query, wei_others[0], weo_others[0])
    wkvup = pieces(w_kv_up, wei_others[0], weo_others[0])
    wso = pieces(w_shared_out, wei_others[0], weo_others[0])

    cosine, sine = rope_tables(seq, ROPE)

    def table_of(values):
        both = jnp.concatenate([values, values], 1).reshape(groups, 1, rows, 2 * ROPE)
        return jnp.broadcast_to(both, (groups, micro, rows, 2 * ROPE)).reshape(total, 2 * ROPE)

    first = dot(after(act, gate_rows), w_first)
    q_nope = first[:, :NOPE].astype(bf16)
    latent_raw = first[:, NOPE : NOPE + LATENT]
    latent = normed(latent_raw, gain_kv).astype(bf16)
    at = NOPE + LATENT
    roped = (
        first[:, at : at + 2 * ROPE] * table_of(cosine) + first[:, at + 2 * ROPE :] * table_of(sine)
    ).astype(bf16)
    kvup = dot(latent, wkvup_me).astype(bf16)

    def owners(x):
        return x.reshape(groups, micro, rows, x.shape[-1])

    segs = segments[:, 0]
    head = (owners(q_nope), owners(roped), owners(kvup), segs)
    attn, lse = attend(*head)
    attn_own = swap(attn.reshape(groups, own, VDIM))
    attn_own = attn_own.swapaxes(0, 1).reshape(own, groups * VDIM)
    x1 = x_own.astype(f32) + dot_pieces(attn_own, wout)
    hid_own = normed(x1, gain_ffn).astype(bf16)
    hid_all = spread(own_first(hid_own, 1))
    attn_all = spread(after(attn_own, hid_all))

    size = width // parts
    arrived = dispatch(hid_all).astype(bf16)
    dyexp = (gate_slots * dispatch(dy_all)).astype(bf16)
    wei = jnp.concatenate([w_expert_in[0]] + wei_others, 0)
    weo = lay_out(w_expert_out[0], weo_others)
    epre = dot(arrived, wei)
    eact = swiglu(epre).astype(bf16)
    deact = dot_nt(dyexp, weo)
    depre = swiglu_back(epre, deact).astype(bf16)
    dhid_rows = dot_nt(depre, wei).astype(bf16)

    spre = dot_nt(hid_all, wsi_me)
    sact = swiglu(spre).astype(bf16)
    dsact = dot_nt(dy_all, wso_me)
    dspre = swiglu_back(spre, dsact).astype(bf16)
    dhid_part = put_back(place, dhid_rows, dspre, *wsi_blocks)
    dhid_sum = collect(dhid_part)

    arrived, depre, eact, dyexp, dspre, sact = lax.optimization_barrier(
        (arrived, depre, eact, dyexp, dspre, sact, dhid_part)
    )[:6]
    hidden = swap(sact.reshape(groups, own, -1))
    gated = (gate_slots * dot(eact, weo)).astype(bf16)
    dspre, sact = lax.optimization_barrier((dspre, sact, gated))[:2]
    g_si = dot_tn(dspre, hid_all)
    g_so = dot_tn(sact, dy_all)

    def shared_grads(r):
        rows_of = block_of(g_so, part + r)
        return jnp.concatenate(
            [g_si[:, r * size : (r + 1) * size]] + jnp.split(rows_of, parts, 1), 0
        )

    g_shared = exchanged(shared_grads(0), lambda r: shared_grads(r).astype(bf16))
    g_shared = stack(after(g_shared.astype(bf16), dhid_sum))

    def expert_in_grad(r):
        return dot_tn(arrived[:, r * size : (r + 1) * size], depre)

    def expert_out_grad(r):
        short = eact.shape[1] // parts
        some = lax.dynamic_slice_in_dim(eact, ((part + r) % parts) * short, short, 1)
        return dot_tn(some, dyexp)

    sent_in = [expert_in_grad(r).astype(bf16) for r in range(1, parts)]
    sent_out = [expert_out_grad(r).astype(bf16) for r in range(1, parts)]
    dhid_sum = after(dhid_sum, gated, hidden, *sent_in, *sent_out)
    got_in = [send(x, r).astype(f32) for r, x in enumerate(sent_in, 1)]
    got_out = [send(x, r).astype(f32) for r, x in enumerate(sent_out, 1)]
    dhid = natural(dhid_sum, 1).astype(f32)

    dy = dy_own.astype(f32)
    dx1_norm, g_ffn_gain = normed_back(x1, gain_ffn, dhid)
    dx1 = dy + dx1_norm
    dx1_low = dx1.astype(bf16)
    dattn_own = dot_pieces_t(dx1_low, wout).astype(bf16)
    dattn = swap(dattn_own.reshape(own, groups, VDIM).swapaxes(0, 1))
    dao = after(dx1_low, dattn).reshape(own, groups, width // groups).swapaxes(0, 1)
    dao = swap(dao)
    dattn = dattn.reshape(groups, micro, rows, VDIM)
    back = attend_back(*head, lse, dattn, cosine, sine)
    moved = swap(back.reshape(groups, own, 512))

    def back_of(x, first_column, last_column):
        piece = x[..., first_column:last_column]
        return piece.swapaxes(0, 1).reshape(own, groups * (last_column - first_column))

    flat = back.reshape(total, 512)
    g_query = dot_tn(act, flat[:, :qk])
    g_kvup = dot_tn(latent, flat[:, 256:])
    g_out = dot_tn(attn_all, dao.reshape(total, width // groups))

    def fold(x):
        steps = size // 128
        runs = size // x.shape[0]
        x = x.reshape(steps, x.shape[0] // steps, runs, x.shape[1] // runs)
        return x.swapaxes(1, 2).reshape(size, -1)

    def attn_grads(r):
        return jnp.concatenate(
            [
                block_of(g_out, part + r),
                g_query[r * size : (r + 1) * size],
                fold(block_of(g_kvup, part + r)),
            ],
            1,
        )

    g_attn = exchanged(attn_grads(0), lambda r: attn_grads(r).astype(bf16))
    g_attn = stack(row_major(g_attn.astype(bf16)))

    dq_own = back_of(moved, 0, qk)
    dkvup_own = back_of(moved, 256, 512)
    dkrope_own = jnp.sum(moved[..., qk:256].astype(f32), 0)
    dlatent = dot_pieces_t(dkvup_own, wkvup)
    latent_own = lax.dynamic_slice_in_dim(latent_raw, me * own, own, 0)
    cos_own = jnp.tile(lax.dynamic_slice_in_dim(cosine, me * rows, rows, 0), (micro, 1))
    sin_own = jnp.tile(lax.dynamic_slice_in_dim(sine, me * rows, rows, 0), (micro, 1))
    dlatent_raw, g_kv_gain = normed_back(latent_own, gain_kv, dlatent)
    dkvfull = jnp.concatenate([dlatent_raw, rotate_back(dkrope_own, cos_own, sin_own)], -1)
    dkvfull = dkvfull.astype(bf16)
    down = LATENT + ROPE
    early = jnp.concatenate([g_kv_gain, g_ffn_gain])
    short = early.shape[0]
    early = jnp.pad(early, (0, 16 * down - short)).reshape(16, down)
    dkv_all = spread_pairs(jnp.concatenate([dkvfull, early.astype(bf16)], 0))
    early = jnp.sum(dkv_all[:, own:].astype(f32), 0).reshape(-1)[:short]
    dkv_all = dkv_all[:, :own].reshape(total, down)
    dact = dot_pieces_t(dq_own, wq) + natural(dot_nt(dkvfull, w_down), 1)
    dx_norm, g_attn_gain = normed_back(x_own.astype(f32), gain_attn, dact)
    input_grad = dx1 + dx_norm

    height = size // groups
    act_rows = jnp.concatenate(
        [
            lax.dynamic_slice_in_dim(act, c * size + me * height, height, 1)
            for c in range(parts)
        ],
        1,
    )
    g_down = dot_tn(act_rows, dkv_all)
    g_down = exchanged(
        g_down[:height], lambda r: g_down[r * height : (r + 1) * height].astype(bf16)
    ).astype(bf16)
    early_kv, early_ffn = early[:LATENT], early[LATENT:]

    def early_gains(r):
        return jnp.concatenate([block_of(early_kv, part + r), block_of(early_ffn, part + r)])

    early = exchanged(early_gains(0), early_gains)
    late = exchanged(block_of(g_attn_gain, part), lambda r: block_of(g_attn_gain, part + r))
    late_rows = -(-size // down)
    late = jnp.pad(late, (0, 16 * down - size)).reshape(16, down)
    last = spread_pairs(jnp.concatenate([g_down, late.astype(bf16)], 0))
    returned = after(gated, last).reshape(groups, micro * capacity, width)
    returned = swap(returned)
    g_down = last[:, :height].astype(f32).reshape(size, down)
    late = jnp.sum(last[:, height : height + late_rows].astype(f32), 0).reshape(-1)[:size]
    gains = (late, early[: LATENT // parts], early[LATENT // parts :])

    hidden = hidden.reshape(groups, own, parts, run).transpose(1, 2, 0, 3).reshape(own, ff)
    hit_own = routes_own.reshape(micro, rows, 1, top) == expert_ids[:, None]
    hit_own = jnp.any(hit_own, -1)
    slot_own = jnp.cumsum(hit_own.astype(jnp.int32), 1) - 1
    slots = jnp.arange(capacity, dtype=jnp.int32)
    find = ((slot_own[..., None] == slots) & hit_own[..., None]).astype(bf16)
    routed = jnp.einsum(
        "mtk,mkd->mtd",
        find.reshape(micro, rows, groups * capacity),
        returned.reshape(groups, micro, capacity, width)
        .swapaxes(0, 1)
        .reshape(micro, groups * capacity, width),
        preferred_element_type=f32,
    ).reshape(own, width)
    out_sum = routed + dot_pieces(hidden, wso)

    mixed = (x1 + out_sum).astype(bf16)
    g_ein = sum(got_in, expert_in_grad(0))
    g_eout = sum(got_out, expert_out_grad(0))
    out_grad, query_grad, kvup_grad = attn_rows(g_attn, width // groups, qk, LATENT // parts)
    shared_in_grad, shared_out_grad = shared_rows(g_shared, 2 * parts, run)
    return (
        mixed.reshape(micro, 1, rows, width),
        input_grad.reshape(micro, 1, rows, width),
        gains[0],
        query_grad,
        g_down,
        gains[1],
        kvup_grad,
        out_grad,
        gains[2],
        shared_in_grad,
        shared_out_grad,
        g_ein[None],
        g_eout[None],
    )


def solution(mesh):
    tok = P(None, "dp", "expert", None)
    row = P("dp", None)
    exp = P("expert", "dp", None)
    in_specs = (
        tok, tok, P(None, "dp", None), tok, tok,
        P("dp"), row, row, P("dp"), row, row, P("dp"), row, row, exp, exp,
    )
    out_specs = (
        tok, tok, P("dp"), row, row, P("dp"), row, row, P("dp"), row, row, exp, exp,
    )

    return jax.shard_map(
        per_device, mesh=mesh, in_specs=in_specs, out_specs=out_specs, check_vma=False
    )
```
